128 devices in a mesh: dp: 16 (over z, y), expert: 8 (over x, core).
Axes of the slice: x: 4, y: 4, z: 4, core: 2. Of those that a mesh axis runs over, the one named last changes fastest.
Arguments:
- records: bfloat16 [32, 128, 8192], P('dp', None, 'expert'), may hold values from -110 to 110
- pair_blocks: int32 [16, 2], replicated, may hold values from 0 to 31
- lengths: int32 [16], replicated, may hold values from 64 to 256
- norm_gain: float32 [6144], replicated, may hold values from 0.25 to 1.75
- gate_logits: float32 [4096, 2], P('dp'), may hold values from -6 to 6
- expert_ids: int32 [4096, 2], P('dp'), may hold values from 0 to 7, all different within a row; in each aligned block of 256 rows (0 to 255, 256 to 511, ...) at most 80 rows name the same one
- gate_weight: bfloat16 [8, 6144, 8192], P('expert', None, 'dp'), may hold values from -0.078125 to 0.078125
- up_weight: bfloat16 [8, 6144, 8192], P('expert', None, 'dp'), may hold values from -0.078125 to 0.078125
- down_weight: bfloat16 [8, 8192, 6144], P('expert', 'dp'), may hold values from -0.0625 to 0.0625
Outputs:
- layer_out: bfloat16 [4096, 6144], P('dp', 'expert')
The draws below stay inside these ranges and needn't reach their ends.
Inputs may be any that keep to these rules, and one draw needn't show every extreme that they name: `expert_ids`: A token's 2 experts differ. Among the tokens of one prompt no expert is chosen more than 80 times.
All inputs are finite; a program needn't handle non-finite values.
Results may differ from the reference program's by a relative error of at most 0.018.
Values may be sent and summed in bfloat16 or wider, within the bound.
No kernel may reach another device: no remote copies, remote signals or barrier semaphores. Data moves between devices by JAX's collectives and lax.ppermute only.
A program may use at most 128 MiB of HBM per device.

```python
import math
import jax
import jax.numpy as jnp
import numpy as np
from jax import lax

D = 6144
KEY_HEADS = 8
HEAD_SIZE = 128
FF = 8192
TOP = 2
BLOCK_TOKENS = 128
PROMPT_TOKENS = 256
EXPERTS = 8
QUERY_GROUP = 6
QKV = 8192
PB = 2
RECORD_BLOCKS = 32
PROMPTS = 16
TOKENS = 4096
CAP = 80
FF_DEV = 512
N_DP = 16


def draw_records(key, part):
    array_shape = (RECORD_BLOCKS, BLOCK_TOKENS, KEY_HEADS, QUERY_GROUP + 2, HEAD_SIZE)
    base = jnp.clip(jax.random.normal(key, array_shape, jnp.float32), -4.0, 4.0)
    return base.reshape(RECORD_BLOCKS, BLOCK_TOKENS, QKV).astype(jnp.bfloat16)


def draw_lengths(key, part):
    drawn = jax.random.randint(key, (PROMPTS,), BLOCK_TOKENS // 2, PROMPT_TOKENS + 1, jnp.int32)
    longest = jax.random.randint(jax.random.fold_in(key, 3), (), 0, PROMPTS, jnp.int32)
    return jnp.where(jnp.arange(PROMPTS, dtype=jnp.int32) == longest, PROMPT_TOKENS, drawn).astype(jnp.int32)


def plant(values, own_key, low, largest):
    longest = values.shape.index(max(values.shape))
    spots = []
    for shift in (0, 1):
        where = [jax.random.randint(jax.random.fold_in(own_key, axis), (), 0, length) for axis, length in enumerate(values.shape)]
        where[longest] = (where[longest] + shift) % values.shape[longest]
        spots.append(tuple(where))
    return values.at[spots[0]].set(low).at[spots[1]].set(largest)


def steps_of(rng, shape, split, smallest, high):
    factor_of = 1.0
    for axis_at, parts in split:
        draws = jax.random.uniform(jax.random.fold_in(jax.random.fold_in(rng, 6), axis_at), (parts,), jnp.float32, smallest / len(split), high / len(split))
        factor_of = factor_of * jnp.repeat(jnp.exp(draws), shape[axis_at] // parts).reshape((-1,) + (1,) * (len(shape) - 1 - axis_at))
    return factor_of


def routed_block(rng, own, number, rows, count, top, limit, lean):
    ranking = jax.random.permutation(rng, count)
    crowded, ordinary = portions_of(count, rows * top, limit, lean, True), portions_of(count, rows * top, limit, lean, False)
    places = jnp.arange(count)

    def named(tallies, turn):
        used = int((tallies > 0).sum())
        fixed = max(1, used // 4)
        passed = fixed + (places - fixed + turn * (used - fixed)) % max(1, count - fixed)
        return jnp.zeros((count,), jnp.int32).at[ranking[jnp.where(places < fixed, places, passed)]].set(jnp.asarray(tallies, jnp.int32))

    tallies = jnp.where(number % 4 == 0, named(crowded, number // 4), named(ordinary, number - number // 4 - 1))
    mixed = jax.random.permutation(jax.random.fold_in(own, 3), count)
    source_of, receiver = mixed[0:count // 2 * 2:2], mixed[1:count // 2 * 2:2]
    room = jnp.minimum(tallies[source_of] - 1, limit - tallies[receiver]) // 2
    room = jnp.where((source_of == ranking[0]) | (receiver == ranking[0]) | (tallies[receiver] == 0), 0, jnp.maximum(room, 0))
    passed = jax.random.randint(jax.random.fold_in(own, 4), (count // 2,), 0, 1 << 20) % (room + 1)
    tallies = tallies.at[source_of].add(-passed).at[receiver].add(passed)
    labels = jnp.searchsorted(jnp.cumsum(tallies), jnp.arange(rows * top), side="right").astype(jnp.int32)
    table = labels.reshape(top, rows).T
    table = table[jax.random.permutation(jax.random.fold_in(own, 1), rows)]
    turn = jax.random.randint(jax.random.fold_in(own, 2), (rows, 1), 0, top)
    return jnp.take_along_axis(table, (jnp.arange(top)[None, :] + turn) % top, axis=1)


def portions_of(amount, total, bound, slope, full):
    loads = [(1 << 20) // math.isqrt(grade ** slope) + 1 for grade in range(1, amount + 1)]
    largest = bound if full else min(bound, max(-(-total // amount), total * loads[0] // sum(loads)))
    least = 1 if total - largest >= amount - 1 else 0
    counts, surplus = [largest] + [least] * (amount - 1), total - largest - least * (amount - 1)
    while surplus > 0:
        free = [i for i in range(1, amount) if counts[i] < largest] or [i for i in range(1, amount) if counts[i] < bound]
        whole, remaining = sum([loads[i] for i in free]), surplus
        for i in free:
            addition = min(bound - counts[i], max(1, remaining * loads[i] // whole), surplus)
            counts[i] = counts[i] + addition
            surplus = surplus - addition
    return np.array(counts)


def scatter_about(stream_key, dims, scale, limit, pieces=(), held_as=jnp.bfloat16):
    loudness = steps_of(stream_key, dims, pieces, -0.22, 0.18) if pieces else 1.0
    entries = jax.random.normal(stream_key, dims, jnp.float32) * scale * loudness
    return jnp.minimum(jnp.maximum(entries, -limit), limit).astype(held_as)


def setup_inputs(seed: int = 0) -> dict:
    arg_keys = jax.random.split(jax.random.key(seed), 10)
    records = draw_records(jax.random.fold_in(arg_keys[9], 71), 0)
    pair_blocks = plant(jax.random.randint(arg_keys[1], (PROMPTS, PB), 0, RECORD_BLOCKS), jax.random.fold_in(arg_keys[1], 1), 0, RECORD_BLOCKS - 1).astype(jnp.int32)
    lengths = draw_lengths(jax.random.fold_in(arg_keys[9], 71), 0)
    norm_gain = jnp.clip(1.0 + 0.15 * jax.random.normal(arg_keys[3], (D,), jnp.float32), 0.25, 1.75)
    gate_logits = scatter_about(arg_keys[4], (TOKENS, TOP), 1.5, 6.0, ((0, 16),), jnp.float32)
    expert_ids_keys = jax.random.split(jax.random.fold_in(arg_keys[5], 1), TOKENS // PROMPT_TOKENS)
    expert_ids_turns = jax.random.permutation(jax.random.fold_in(arg_keys[5], 3), TOKENS // PROMPT_TOKENS)
    expert_ids = jax.vmap(lambda own, number: routed_block(jax.random.fold_in(arg_keys[5], 2), own, number, PROMPT_TOKENS, EXPERTS, TOP, CAP, 2))(expert_ids_keys, expert_ids_turns).reshape((TOKENS, TOP))
    gate_weight = scatter_about(arg_keys[6], (EXPERTS, D, FF), D ** -0.5, 0.078125, ((0, 8), (2, 16)))
    up_weight = scatter_about(arg_keys[7], (EXPERTS, D, FF), D ** -0.5, 0.078125, ((0, 8), (2, 16)))
    down_weight = scatter_about(arg_keys[8], (EXPERTS, FF, D), FF ** -0.5, 0.0625, ((0, 8), (1, 16)))
    return dict(records=records, pair_blocks=pair_blocks, lengths=lengths, norm_gain=norm_gain, gate_logits=gate_logits, expert_ids=expert_ids, gate_weight=gate_weight, up_weight=up_weight, down_weight=down_weight)


def route_table(expert_block, expert_count, capacity):
    flattened = expert_block.reshape(-1)
    total = flattened.shape[0]
    one_hot = (flattened[:, None] == jnp.arange(expert_count, dtype=jnp.int32)[None, :]).astype(jnp.int32)
    earlier = jnp.cumsum(one_hot, axis=0) - one_hot
    slot_index = lax.optimization_barrier(jnp.sum(earlier * one_hot, axis=1)).astype(jnp.int32)
    token_index = (jnp.arange(total, dtype=jnp.int32) // expert_block.shape[1]).astype(jnp.int32)
    table = jnp.full((expert_count, capacity), -1, jnp.int32).at[flattened, slot_index].set(token_index)
    return (table, slot_index)

def reference(records, pair_blocks, lengths, norm_gain, gate_logits, expert_ids, gate_weight, up_weight, down_weight):
    scale = 1.0 / math.sqrt(HEAD_SIZE)

    def attend(operands):
        block_numbers, key_limit = operands
        rows_of_tokens = records[block_numbers].reshape(PROMPT_TOKENS, KEY_HEADS, QUERY_GROUP + 2, HEAD_SIZE)
        queries = rows_of_tokens[:, :, :QUERY_GROUP, :].astype(jnp.float32)
        key_vecs = rows_of_tokens[:, :, QUERY_GROUP, :].astype(jnp.float32)
        value_vecs = rows_of_tokens[:, :, QUERY_GROUP + 1, :].astype(jnp.float32)
        scores = jnp.einsum('ihgd,khd->hgik', queries, key_vecs, precision=lax.Precision.HIGHEST) * scale
        position = jnp.arange(PROMPT_TOKENS, dtype=jnp.int32)
        allowed = (position[None, :] <= position[:, None]) & (position[None, :] < key_limit)
        scores = jnp.where(allowed, scores, -jnp.inf)
        row_max = lax.optimization_barrier(jnp.max(scores, axis=-1, keepdims=True))
        exponent = jnp.exp(scores - row_max)
        weights_bf = (exponent / lax.optimization_barrier(jnp.sum(exponent, axis=-1, keepdims=True))).astype(jnp.bfloat16)
        mixed = jnp.einsum('hgik,khd->ihgd', weights_bf.astype(jnp.float32), value_vecs, precision=lax.Precision.HIGHEST)
        return mixed.astype(jnp.bfloat16).reshape(PROMPT_TOKENS, D)
    attended = lax.map(attend, (pair_blocks, lengths)).reshape(TOKENS, D)
    attended_f = attended.astype(jnp.float32)
    mean_square = lax.optimization_barrier(jnp.mean(attended_f * attended_f, axis=1, keepdims=True))
    normed = (attended_f * lax.rsqrt(mean_square + 1e-05) * norm_gain).astype(jnp.bfloat16)
    gate_weights = jax.nn.softmax(gate_logits, axis=-1)
    expert_blocks = expert_ids.reshape(N_DP, PROMPT_TOKENS, TOP)
    tables, slots = jax.vmap(lambda blk: route_table(blk, EXPERTS, CAP))(expert_blocks)
    offsets = (jnp.arange(N_DP, dtype=jnp.int32) * PROMPT_TOKENS)[:, None, None]
    global_tables = jnp.where(tables >= 0, tables + offsets, -1)
    per_expert = jnp.transpose(global_tables, (1, 0, 2)).reshape(EXPERTS, N_DP * CAP)

    def run_expert(operands):
        token_list, gate_mat, up_mat, down_mat = operands
        chosen = jnp.where((token_list >= 0)[:, None], normed[jnp.maximum(token_list, 0)], jnp.zeros((), jnp.bfloat16))
        gate_part = jnp.dot(chosen, gate_mat, preferred_element_type=jnp.float32)
        up_part = jnp.dot(chosen, up_mat, preferred_element_type=jnp.float32)
        hidden = (jax.nn.silu(gate_part) * up_part).astype(jnp.bfloat16)
        summed = jnp.zeros((N_DP * CAP, D), jnp.float32)
        for group in range(N_DP):
            lower = group * FF_DEV
            partial_value = jnp.dot(hidden[:, lower:lower + FF_DEV], down_mat[lower:lower + FF_DEV], preferred_element_type=jnp.float32)
            partial_value = lax.optimization_barrier(partial_value.astype(jnp.bfloat16))
            summed = summed + partial_value.astype(jnp.float32)
        return summed.astype(jnp.bfloat16)
    expert_out = lax.map(run_expert, (per_expert, gate_weight, up_weight, down_weight))
    expert_index = expert_blocks.reshape(N_DP, PROMPT_TOKENS * TOP)
    row_index = (jnp.arange(N_DP, dtype=jnp.int32) * CAP)[:, None] + slots
    picked = expert_out[expert_index.reshape(-1), row_index.reshape(-1)].reshape(TOKENS, TOP, D)
    combined = attended_f + lax.optimization_barrier(jnp.sum(gate_weights[:, :, None] * picked.astype(jnp.float32), axis=1))
    return combined.astype(jnp.bfloat16)
```

```python
import math

import jax
import jax.numpy as jnp
from jax import lax
from jax.experimental import pallas as pl
from jax.experimental.pallas import tpu as pltpu
from jax.sharding import Mesh
from jax.sharding import PartitionSpec as P

HEAD = 128
GROUP = 6
BLOCK = 128
PROMPT = 256
EXPERTS = 8
CAP = 80
WIDTH = 768
D = 6144
FF_DEV = 512
N_DP = 16
SIDE = 4
QKV = 1024


def pick_kernel(idx_ref, mine_ref, blocks_ref, out_ref):
    i = pl.program_id(0)

    @pl.when(mine_ref[i] == 1)
    def _():
        out_ref[...] = blocks_ref[...]

    @pl.when(mine_ref[i] == 0)
    def _():
        out_ref[...] = jnp.zeros_like(out_ref)


def pick_blocks(idx, mine, blocks):
    n, (_, rows, cols) = idx.shape[0], blocks.shape
    return pl.pallas_call(
        pick_kernel,
        grid_spec=pltpu.PrefetchScalarGridSpec(
            num_scalar_prefetch=2,
            grid=(n,),
            in_specs=[pl.BlockSpec((1, rows, cols), lambda i, idx, mine: (idx[i], 0, 0))],
            out_specs=pl.BlockSpec((1, rows, cols), lambda i, idx, mine: (i, 0, 0)),
        ),
        out_shape=jax.ShapeDtypeStruct((n, rows, cols), blocks.dtype),
        name="pick_blocks",
    )(idx, mine, blocks)


def attend_kernel(len_ref, rows_ref, ids_ref, att_ref, out_ref):
    limit = len_ref[0]
    scale = 1.0 / math.sqrt(HEAD)
    for top in (0, BLOCK):
        span = top + BLOCK
        keys = rows_ref[0:span, GROUP * HEAD : (GROUP + 1) * HEAD]
        values = rows_ref[0:span, (GROUP + 1) * HEAD : (GROUP + 2) * HEAD]
        row = lax.broadcasted_iota(jnp.int32, (BLOCK, span), 0) + top
        col = lax.broadcasted_iota(jnp.int32, (BLOCK, span), 1)
        allowed = (col <= row) & (col < limit)
        for g in range(GROUP):
            query = rows_ref[top:span, g * HEAD : (g + 1) * HEAD]
            scores = lax.dot_general(
                query, keys, (((1,), (1,)), ((), ())), preferred_element_type=jnp.float32
            )
            scores = jnp.where(allowed, scores * scale, -jnp.inf)
            exponent = jnp.exp(scores - jnp.max(scores, axis=1, keepdims=True))
            probs = (exponent / jnp.sum(exponent, axis=1, keepdims=True)).astype(jnp.bfloat16)
            mixed = jnp.dot(probs, values, preferred_element_type=jnp.float32)
            att_ref[top:span, g * HEAD : (g + 1) * HEAD] = mixed.astype(jnp.bfloat16)
    names = lax.broadcasted_iota(jnp.int32, (EXPERTS, PROMPT), 0)
    named = (ids_ref[0:1, :] == names) | (ids_ref[1:2, :] == names)
    first = lax.broadcasted_iota(jnp.int32, (PROMPT, PROMPT), 0)
    second = lax.broadcasted_iota(jnp.int32, (PROMPT, PROMPT), 1)
    before = jnp.where(first < second, 1.0, 0.0).astype(jnp.bfloat16)
    taken = jnp.where(named, 1.0, 0.0)
    slot = jnp.dot(taken.astype(jnp.bfloat16), before, preferred_element_type=jnp.float32)
    slot = jnp.where(named, slot, -1.0).astype(jnp.int32)
    att = att_ref[...]
    place = lax.broadcasted_iota(jnp.int32, (CAP, PROMPT), 0)
    for e in range(EXPERTS):
        chosen = jnp.where(place == slot[e : e + 1, :], 1.0, 0.0).astype(jnp.bfloat16)
        sent = jnp.dot(chosen, att, preferred_element_type=jnp.float32)
        out_ref[e * CAP : (e + 1) * CAP, :] = sent.astype(jnp.bfloat16)


def attend(limit, rows, ids_t):
    return pl.pallas_call(
        attend_kernel,
        in_specs=[
            pl.BlockSpec(memory_space=pltpu.SMEM),
            pl.BlockSpec(memory_space=pltpu.VMEM),
            pl.BlockSpec(memory_space=pltpu.VMEM),
        ],
        out_specs=[pl.BlockSpec(memory_space=pltpu.VMEM), pl.BlockSpec(memory_space=pltpu.VMEM)],
        out_shape=[
            jax.ShapeDtypeStruct((PROMPT, WIDTH), jnp.bfloat16),
            jax.ShapeDtypeStruct((EXPERTS * CAP, WIDTH), jnp.bfloat16),
        ],
        compiler_params=pltpu.CompilerParams(vmem_limit_bytes=32 << 20),
        name="attend",
    )(limit, rows, ids_t)


def norm_kernel(x_ref, gain_ref, out_ref):
    total = jnp.zeros((CAP, 1), jnp.float32)
    for i in range(EXPERTS):
        part = x_ref[i].astype(jnp.float32)
        total = total + jnp.sum(part * part, axis=1, keepdims=True)
    factor = lax.rsqrt(total * (1.0 / D) + 1e-05)
    for i in range(EXPERTS):
        cols = slice(i * WIDTH, (i + 1) * WIDTH)
        out_ref[:, cols] = (x_ref[i].astype(jnp.float32) * factor * gain_ref[:, cols]).astype(
            jnp.bfloat16
        )


def normalise(arrived, gain):
    return pl.pallas_call(
        norm_kernel,
        out_shape=jax.ShapeDtypeStruct((CAP, D), jnp.bfloat16),
        compiler_params=pltpu.CompilerParams(vmem_limit_bytes=32 << 20),
        name="normalise",
    )(arrived, gain)


def ffn_kernel(x_ref, gate_ref, up_ref, down_ref, out_ref):
    x = x_ref[...]
    gate = jnp.dot(x, gate_ref[0], preferred_element_type=jnp.float32)
    up = jnp.dot(x, up_ref[0], preferred_element_type=jnp.float32)
    hidden = (gate / (1.0 + jnp.exp(-gate)) * up).astype(jnp.bfloat16)
    n = x.shape[0] // CAP
    for i in range(EXPERTS):
        part = jnp.dot(
            hidden, down_ref[0, :, i * WIDTH : (i + 1) * WIDTH], preferred_element_type=jnp.float32
        ).astype(jnp.bfloat16)
        for j in range(n):
            out_ref[j, i] = part[j * CAP : (j + 1) * CAP]


def ffn(slot_rows, gate, up, down, tile):
    n = slot_rows.shape[0]
    whole = lambda i: (0, 0, 0)
    return pl.pallas_call(
        ffn_kernel,
        grid=(n // tile,),
        in_specs=[
            pl.BlockSpec((tile, D), lambda i: (i, 0)),
            pl.BlockSpec((1, D, FF_DEV), whole, pipeline_mode=pl.Buffered(1)),
            pl.BlockSpec((1, D, FF_DEV), whole, pipeline_mode=pl.Buffered(1)),
            pl.BlockSpec((1, FF_DEV, D), whole, pipeline_mode=pl.Buffered(1)),
        ],
        out_specs=pl.BlockSpec((tile // CAP, EXPERTS, CAP, WIDTH), lambda i: (i, 0, 0, 0)),
        out_shape=jax.ShapeDtypeStruct((n // CAP, EXPERTS, CAP, WIDTH), jnp.bfloat16),
        compiler_params=pltpu.CompilerParams(vmem_limit_bytes=56 << 20),
        name="ffn",
    )(slot_rows, gate, up, down)


def combine_kernel(att_ref, ret_ref, ids_ref, logits_ref, out_ref):
    names = lax.broadcasted_iota(jnp.int32, (PROMPT, HEAD), 1)
    ids = [ids_ref[:, c : c + 1] for c in range(2)]
    named = (ids[0] == names) | (ids[1] == names)
    first = lax.broadcasted_iota(jnp.int32, (PROMPT, PROMPT), 0)
    second = lax.broadcasted_iota(jnp.int32, (PROMPT, PROMPT), 1)
    before = jnp.where(second < first, 1.0, 0.0).astype(jnp.bfloat16)
    taken = jnp.where(named, 1.0, 0.0).astype(jnp.bfloat16)
    count = jnp.dot(before, taken, preferred_element_type=jnp.float32)
    logits = [logits_ref[:, c : c + 1] for c in range(2)]
    top = jnp.maximum(logits[0], logits[1])
    exps = [jnp.exp(v - top) for v in logits]
    total = exps[0] + exps[1]
    ret = ret_ref[...]
    column = lax.broadcasted_iota(jnp.int32, (PROMPT, EXPERTS * CAP), 1)
    mixed = None
    for c in range(2):
        slot = jnp.sum(jnp.where(ids[c] == names, count, 0.0), axis=1, keepdims=True)
        at = ids[c] * CAP + slot.astype(jnp.int32)
        chosen = jnp.where(column == at, 1.0, 0.0).astype(jnp.bfloat16)
        picked = jnp.dot(chosen, ret, preferred_element_type=jnp.float32)
        term = exps[c] / total * picked
        mixed = term if mixed is None else mixed + term
    out_ref[...] = (att_ref[...].astype(jnp.float32) + mixed).astype(jnp.bfloat16)


def combine(att, returned, ids, logits):
    return pl.pallas_call(
        combine_kernel,
        out_shape=jax.ShapeDtypeStruct((PROMPT, WIDTH), jnp.bfloat16),
        compiler_params=pltpu.CompilerParams(vmem_limit_bytes=32 << 20),
        name="combine",
    )(att, returned, ids, logits)


def fetch_rows(records, pair_blocks):
    z, y = lax.axis_index("z"), lax.axis_index("y")
    column = lax.all_gather(records, "z", axis=0, tiled=True)
    wanted = lax.dynamic_slice_in_dim(pair_blocks, z * SIDE, SIDE, 0).reshape(-1)
    owner = wanted // 2
    mine = (owner % SIDE == y).astype(jnp.int32)
    idx = (owner // SIDE) * 2 + wanted % 2
    picked = pick_blocks(idx, mine, column)
    return lax.psum_scatter(picked, "y", scatter_dimension=0, tiled=True)


def body(
    records,
    pair_blocks,
    lengths,
    norm_gain,
    gate_logits,
    expert_ids,
    gate_weight,
    up_weight,
    down_weight,
):
    dp_index = lax.axis_index("z") * SIDE + lax.axis_index("y")
    limit = lax.dynamic_slice_in_dim(lengths, dp_index, 1, 0)
    rows = fetch_rows(records, pair_blocks).reshape(PROMPT, QKV)
    att, outgoing = attend(limit, rows, expert_ids.T)
    arrived = lax.all_to_all(
        outgoing.reshape(EXPERTS, CAP, WIDTH), "expert", split_axis=0, concat_axis=0, tiled=True
    )
    normed = normalise(arrived, norm_gain.reshape(1, D))
    slot_rows = lax.all_gather(normed, ("z", "y"), axis=0, tiled=True)
    partial = ffn(slot_rows, gate_weight, up_weight, down_weight, 320)
    summed = lax.psum_scatter(partial, ("z", "y"), scatter_dimension=0, tiled=True)
    returned = lax.all_to_all(summed[0], "expert", split_axis=0, concat_axis=0, tiled=True)
    return combine(att, returned.reshape(EXPERTS * CAP, WIDTH), expert_ids, gate_logits)


def solution(mesh):
    fine = Mesh(mesh.devices.reshape(SIDE, SIDE, EXPERTS), ("z", "y", "expert"))
    dp = ("z", "y")
    placed = (
        P(dp, None, "expert"),
        P(),
        P(),
        P(),
        P(dp, None),
        P(dp, None),
        P("expert", None, dp),
        P("expert", None, dp),
        P("expert", dp, None),
    )
    return jax.shard_map(
        body, mesh=fine, in_specs=placed, out_specs=P(dp, "expert"), check_vma=False
    )
```

```python
import math

import jax
import jax.numpy as jnp
from jax import lax
from jax.experimental import pallas as pl
from jax.experimental.pallas import tpu as pltpu
from jax.sharding import Mesh
from jax.sharding import PartitionSpec as P

HEAD = 128
GROUP = 6
BLOCK = 128
PROMPT = 256
EXPERTS = 8
CAP = 80
WIDTH = 768
D = 6144
FF_DEV = 512
N_DP = 16
SIDE = 4
QKV = 1024


def pick_kernel(idx_ref, mine_ref, blocks_ref, out_ref):
    i = pl.program_id(0)

    @pl.when(mine_ref[i] == 1)
    def _():
        out_ref[...] = blocks_ref[...]

    @pl.when(mine_ref[i] == 0)
    def _():
        out_ref[...] = jnp.zeros_like(out_ref)


def pick_blocks(idx, mine, blocks):
    n, (_, rows, cols) = idx.shape[0], blocks.shape
    return pl.pallas_call(
        pick_kernel,
        grid_spec=pltpu.PrefetchScalarGridSpec(
            num_scalar_prefetch=2,
            grid=(n,),
            in_specs=[pl.BlockSpec((1, rows, cols), lambda i, idx, mine: (idx[i], 0, 0))],
            out_specs=pl.BlockSpec((1, rows, cols), lambda i, idx, mine: (i, 0, 0)),
        ),
        out_shape=jax.ShapeDtypeStruct((n, rows, cols), blocks.dtype),
        name="pick_blocks",
    )(idx, mine, blocks)


def attend_kernel(len_ref, rows_ref, ids_ref, att_ref, out_ref):
    limit = len_ref[0]
    scale = 1.0 / math.sqrt(HEAD)
    for top in (0, BLOCK):
        span = top + BLOCK
        keys = rows_ref[0:span, GROUP * HEAD : (GROUP + 1) * HEAD]
        values = rows_ref[0:span, (GROUP + 1) * HEAD : (GROUP + 2) * HEAD]
        row = lax.broadcasted_iota(jnp.int32, (BLOCK, span), 0) + top
        col = lax.broadcasted_iota(jnp.int32, (BLOCK, span), 1)
        allowed = (col <= row) & (col < limit)
        for g in range(GROUP):
            query = rows_ref[top:span, g * HEAD : (g + 1) * HEAD]
            scores = lax.dot_general(
                query, keys, (((1,), (1,)), ((), ())), preferred_element_type=jnp.float32
            )
            scores = jnp.where(allowed, scores * scale, -jnp.inf)
            exponent = jnp.exp(scores - jnp.max(scores, axis=1, keepdims=True))
            probs = (exponent / jnp.sum(exponent, axis=1, keepdims=True)).astype(jnp.bfloat16)
            mixed = jnp.dot(probs, values, preferred_element_type=jnp.float32)
            att_ref[top:span, g * HEAD : (g + 1) * HEAD] = mixed.astype(jnp.bfloat16)
    names = lax.broadcasted_iota(jnp.int32, (EXPERTS, PROMPT), 0)
    named = (ids_ref[0:1, :] == names) | (ids_ref[1:2, :] == names)
    first = lax.broadcasted_iota(jnp.int32, (PROMPT, PROMPT), 0)
    second = lax.broadcasted_iota(jnp.int32, (PROMPT, PROMPT), 1)
    before = jnp.where(first < second, 1.0, 0.0).astype(jnp.bfloat16)
    taken = jnp.where(named, 1.0, 0.0)
    slot = jnp.dot(taken.astype(jnp.bfloat16), before, preferred_element_type=jnp.float32)
    slot = jnp.where(named, slot, -1.0).astype(jnp.int32)
    att = att_ref[...]
    place = lax.broadcasted_iota(jnp.int32, (CAP, PROMPT), 0)
    for e in range(EXPERTS):
        chosen = jnp.where(place == slot[e : e + 1, :], 1.0, 0.0).astype(jnp.bfloat16)
        sent = jnp.dot(chosen, att, preferred_element_type=jnp.float32)
        out_ref[e * CAP : (e + 1) * CAP, :] = sent.astype(jnp.bfloat16)


def attend(limit, rows, ids_t):
    return pl.pallas_call(
        attend_kernel,
        in_specs=[
            pl.BlockSpec(memory_space=pltpu.SMEM),
            pl.BlockSpec(memory_space=pltpu.VMEM),
            pl.BlockSpec(memory_space=pltpu.VMEM),
        ],
        out_specs=[pl.BlockSpec(memory_space=pltpu.VMEM), pl.BlockSpec(memory_space=pltpu.VMEM)],
        out_shape=[
            jax.ShapeDtypeStruct((PROMPT, WIDTH), jnp.bfloat16),
            jax.ShapeDtypeStruct((EXPERTS * CAP, WIDTH), jnp.bfloat16),
        ],
        compiler_params=pltpu.CompilerParams(vmem_limit_bytes=32 << 20),
        name="attend",
    )(limit, rows, ids_t)


def norm_kernel(x_ref, gain_ref, out_ref):
    total = jnp.zeros((CAP, 1), jnp.float32)
    for i in range(EXPERTS):
        part = x_ref[i].astype(jnp.float32)
        total = total + jnp.sum(part * part, axis=1, keepdims=True)
    factor = lax.rsqrt(total * (1.0 / D) + 1e-05)
    for i in range(EXPERTS):
        cols = slice(i * WIDTH, (i + 1) * WIDTH)
        out_ref[:, cols] = (x_ref[i].astype(jnp.float32) * factor * gain_ref[:, cols]).astype(
            jnp.bfloat16
        )


def normalise(arrived, gain):
    return pl.pallas_call(
        norm_kernel,
        out_shape=jax.ShapeDtypeStruct((CAP, D), jnp.bfloat16),
        compiler_params=pltpu.CompilerParams(vmem_limit_bytes=32 << 20),
        name="normalise",
    )(arrived, gain)


K_PARTS = 4
K_PART = D // K_PARTS
HALF = EXPERTS // 2


def ffn_kernel(
    x0, x1, x2, x3, gate_hbm, up_hbm, down_hbm, o0, o1, o2, o3,
    xs, gate, up, down, outs, x_sem, gate_sem, up_sem, down_sem, out_sem,
):
    x_copies = [
        pltpu.make_async_copy(x, xs.at[pl.ds(j * CAP, CAP)], x_sem.at[j])
        for j, x in enumerate((x0, x1, x2, x3))
    ]
    in_copies = []
    for k in range(K_PARTS):
        rows = pl.ds(k * K_PART, K_PART)
        in_copies.append(
            (
                pltpu.make_async_copy(gate_hbm.at[0, rows], gate.at[rows], gate_sem.at[k]),
                pltpu.make_async_copy(up_hbm.at[0, rows], up.at[rows], up_sem.at[k]),
            )
        )
    down_copies = [
        pltpu.make_async_copy(
            down_hbm.at[0, :, pl.ds(h * HALF * WIDTH, HALF * WIDTH)],
            down.at[:, pl.ds(h * HALF * WIDTH, HALF * WIDTH)],
            down_sem.at[h],
        )
        for h in range(2)
    ]
    for copy in x_copies:
        copy.start()
    for pair in in_copies:
        for copy in pair:
            copy.start()
    for copy in down_copies:
        copy.start()
    for copy in x_copies:
        copy.wait()
    gate_part = up_part = None
    for k, pair in enumerate(in_copies):
        for copy in pair:
            copy.wait()
        rows = slice(k * K_PART, (k + 1) * K_PART)
        x = xs[:, rows]
        g = jnp.dot(x, gate[rows, :], preferred_element_type=jnp.float32)
        u = jnp.dot(x, up[rows, :], preferred_element_type=jnp.float32)
        gate_part = g if gate_part is None else gate_part + g
        up_part = u if up_part is None else up_part + u
    hidden = (gate_part / (1.0 + jnp.exp(-gate_part)) * up_part).astype(jnp.bfloat16)
    out_copies = []
    for h in range(2):
        down_copies[h].wait()
        for i in range(h * HALF, (h + 1) * HALF):
            part = jnp.dot(
                hidden, down[:, i * WIDTH : (i + 1) * WIDTH], preferred_element_type=jnp.float32
            ).astype(jnp.bfloat16)
            for j in range(SIDE):
                outs[j, i] = part[j * CAP : (j + 1) * CAP]
        for j, o in enumerate((o0, o1, o2, o3)):
            some = pl.ds(h * HALF, HALF)
            copy = pltpu.make_async_copy(outs.at[j, some], o.at[some], out_sem.at[h, j])
            copy.start()
            out_copies.append(copy)
    for copy in out_copies:
        copy.wait()


def ffn(shards, gate, up, down):
    anywhere = pl.BlockSpec(memory_space=pl.ANY)
    return pl.pallas_call(
        ffn_kernel,
        in_specs=[anywhere] * 7,
        out_specs=[anywhere] * SIDE,
        out_shape=[jax.ShapeDtypeStruct((EXPERTS, CAP, WIDTH), jnp.bfloat16)] * SIDE,
        scratch_shapes=[
            pltpu.VMEM((SIDE * CAP, D), jnp.bfloat16),
            pltpu.VMEM((D, FF_DEV), jnp.bfloat16),
            pltpu.VMEM((D, FF_DEV), jnp.bfloat16),
            pltpu.VMEM((FF_DEV, D), jnp.bfloat16),
            pltpu.VMEM((SIDE, EXPERTS, CAP, WIDTH), jnp.bfloat16),
            pltpu.SemaphoreType.DMA((SIDE,)),
            pltpu.SemaphoreType.DMA((K_PARTS,)),
            pltpu.SemaphoreType.DMA((K_PARTS,)),
            pltpu.SemaphoreType.DMA((2,)),
            pltpu.SemaphoreType.DMA((2, SIDE)),
        ],
        compiler_params=pltpu.CompilerParams(vmem_limit_bytes=48 << 20),
        cost_estimate=pl.CostEstimate(
            flops=6 * SIDE * CAP * D * FF_DEV,
            transcendentals=SIDE * CAP * FF_DEV,
            bytes_accessed=6 * D * FF_DEV + 4 * SIDE * CAP * D,
        ),
        name="ffn",
    )(*shards, gate, up, down)


def shift(value, first, step):
    pairs = []
    for z in range(SIDE):
        for y in range(SIDE):
            for e in range(EXPERTS):
                along_y = (e % 2 == 0) == first
                to_z, to_y = (z, (y + step) % SIDE) if along_y else ((z + step) % SIDE, y)
                pairs.append(((z * SIDE + y) * EXPERTS + e, (to_z * SIDE + to_y) * EXPERTS + e))
    return lax.ppermute(value, ("z", "y", "expert"), pairs)


def add(*parts):
    total = parts[0].astype(jnp.float32)
    for part in parts[1:]:
        total = total + part.astype(jnp.float32)
    return total.astype(jnp.bfloat16)


def experts(own, gate, up, down):
    low, high = shift(own, True, 1), shift(own, True, -1)
    firsts = {0: own, -1: low, 1: high, 2: shift(low, True, 1)}
    sums = {}
    for a, way in ((0, 1), (-1, -1), (1, 1), (2, -1)):
        near = {step: shift(firsts[a], False, step) for step in (1, -1)}
        far = shift(near[way], False, way)
        here, to_low, to_high, to_far = ffn((firsts[a], near[1], near[-1], far), gate, up, down)
        ahead, behind = (to_high, to_low) if way == 1 else (to_low, to_high)
        passed = shift(to_far, False, way)
        sums[a] = add(here, shift(add(ahead, passed), False, way), shift(behind, False, -way))
    passed = shift(sums[2], True, 1)
    return add(sums[0], shift(add(sums[1], passed), True, 1), shift(sums[-1], True, -1))


def combine_kernel(att_ref, ret_ref, ids_ref, logits_ref, out_ref):
    names = lax.broadcasted_iota(jnp.int32, (PROMPT, HEAD), 1)
    ids = [ids_ref[:, c : c + 1] for c in range(2)]
    named = (ids[0] == names) | (ids[1] == names)
    first = lax.broadcasted_iota(jnp.int32, (PROMPT, PROMPT), 0)
    second = lax.broadcasted_iota(jnp.int32, (PROMPT, PROMPT), 1)
    before = jnp.where(second < first, 1.0, 0.0).astype(jnp.bfloat16)
    taken = jnp.where(named, 1.0, 0.0).astype(jnp.bfloat16)
    count = jnp.dot(before, taken, preferred_element_type=jnp.float32)
    logits = [logits_ref[:, c : c + 1] for c in range(2)]
    top = jnp.maximum(logits[0], logits[1])
    exps = [jnp.exp(v - top) for v in logits]
    total = exps[0] + exps[1]
    ret = ret_ref[...]
    column = lax.broadcasted_iota(jnp.int32, (PROMPT, EXPERTS * CAP), 1)
    mixed = None
    for c in range(2):
        slot = jnp.sum(jnp.where(ids[c] == names, count, 0.0), axis=1, keepdims=True)
        at = ids[c] * CAP + slot.astype(jnp.int32)
        chosen = jnp.where(column == at, 1.0, 0.0).astype(jnp.bfloat16)
        picked = jnp.dot(chosen, ret, preferred_element_type=jnp.float32)
        term = exps[c] / total * picked
        mixed = term if mixed is None else mixed + term
    out_ref[...] = (att_ref[...].astype(jnp.float32) + mixed).astype(jnp.bfloat16)


def combine(att, returned, ids, logits):
    return pl.pallas_call(
        combine_kernel,
        out_shape=jax.ShapeDtypeStruct((PROMPT, WIDTH), jnp.bfloat16),
        compiler_params=pltpu.CompilerParams(vmem_limit_bytes=32 << 20),
        name="combine",
    )(att, returned, ids, logits)


def fetch_rows(records, pair_blocks):
    z, y = lax.axis_index("z"), lax.axis_index("y")
    column = lax.all_gather(records, "z", axis=0, tiled=True)
    wanted = lax.dynamic_slice_in_dim(pair_blocks, z * SIDE, SIDE, 0).reshape(-1)
    owner = wanted // 2
    mine = (owner % SIDE == y).astype(jnp.int32)
    idx = (owner // SIDE) * 2 + wanted % 2
    picked = pick_blocks(idx, mine, column)
    return lax.psum_scatter(picked, "y", scatter_dimension=0, tiled=True)


def body(
    records,
    pair_blocks,
    lengths,
    norm_gain,
    gate_logits,
    expert_ids,
    gate_weight,
    up_weight,
    down_weight,
):
    dp_index = lax.axis_index("z") * SIDE + lax.axis_index("y")
    limit = lax.dynamic_slice_in_dim(lengths, dp_index, 1, 0)
    rows = fetch_rows(records, pair_blocks).reshape(PROMPT, QKV)
    att, outgoing = attend(limit, rows, expert_ids.T)
    arrived = lax.all_to_all(
        outgoing.reshape(EXPERTS, CAP, WIDTH), "expert", split_axis=0, concat_axis=0, tiled=True
    )
    normed = normalise(arrived, norm_gain.reshape(1, D))
    summed = experts(normed, gate_weight, up_weight, down_weight)
    returned = lax.all_to_all(summed, "expert", split_axis=0, concat_axis=0, tiled=True)
    return combine(att, returned.reshape(EXPERTS * CAP, WIDTH), expert_ids, gate_logits)


def solution(mesh):
    fine = Mesh(mesh.devices.reshape(SIDE, SIDE, EXPERTS), ("z", "y", "expert"))
    dp = ("z", "y")
    placed = (
        P(dp, None, "expert"),
        P(),
        P(),
        P(),
        P(dp, None),
        P(dp, None),
        P("expert", None, dp),
        P("expert", None, dp),
        P("expert", dp, None),
    )
    return jax.shard_map(
        body, mesh=fine, in_specs=placed, out_specs=P(dp, "expert"), check_vma=False
    )
```

```python
import math

import jax
import jax.numpy as jnp
from jax import lax
from jax.experimental import pallas as pl
from jax.experimental.pallas import tpu as pltpu
from jax.sharding import Mesh
from jax.sharding import PartitionSpec as P

HEAD = 128
GROUP = 6
BLOCK = 128
PROMPT = 256
EXPERTS = 8
CAP = 80
WIDTH = 768
D = 6144
FF_DEV = 512
N_DP = 16
SIDE = 4
QKV = 1024


def pick_kernel(idx_ref, mine_ref, blocks_ref, out_ref):
    i = pl.program_id(0)

    @pl.when(mine_ref[i] == 1)
    def _():
        out_ref[...] = blocks_ref[...]

    @pl.when(mine_ref[i] == 0)
    def _():
        out_ref[...] = jnp.zeros_like(out_ref)


def pick_blocks(idx, mine, blocks):
    n, (_, rows, cols) = idx.shape[0], blocks.shape
    return pl.pallas_call(
        pick_kernel,
        grid_spec=pltpu.PrefetchScalarGridSpec(
            num_scalar_prefetch=2,
            grid=(n,),
            in_specs=[pl.BlockSpec((1, rows, cols), lambda i, idx, mine: (idx[i], 0, 0))],
            out_specs=pl.BlockSpec((1, rows, cols), lambda i, idx, mine: (i, 0, 0)),
        ),
        out_shape=jax.ShapeDtypeStruct((n, rows, cols), blocks.dtype),
        name="pick_blocks",
    )(idx, mine, blocks)


def attend_kernel(len_ref, rows_ref, ids_ref, att_ref, out_ref):
    limit = len_ref[0]
    scale = 1.0 / math.sqrt(HEAD)
    for top in (0, BLOCK):
        span = top + BLOCK
        keys = rows_ref[0:span, GROUP * HEAD : (GROUP + 1) * HEAD]
        values = rows_ref[0:span, (GROUP + 1) * HEAD : (GROUP + 2) * HEAD]
        row = lax.broadcasted_iota(jnp.int32, (BLOCK, span), 0) + top
        col = lax.broadcasted_iota(jnp.int32, (BLOCK, span), 1)
        allowed = (col <= row) & (col < limit)
        for g in range(GROUP):
            query = rows_ref[top:span, g * HEAD : (g + 1) * HEAD]
            scores = lax.dot_general(
                query, keys, (((1,), (1,)), ((), ())), preferred_element_type=jnp.float32
            )
            scores = jnp.where(allowed, scores * scale, -jnp.inf)
            exponent = jnp.exp(scores - jnp.max(scores, axis=1, keepdims=True))
            probs = (exponent / jnp.sum(exponent, axis=1, keepdims=True)).astype(jnp.bfloat16)
            mixed = jnp.dot(probs, values, preferred_element_type=jnp.float32)
            att_ref[top:span, g * HEAD : (g + 1) * HEAD] = mixed.astype(jnp.bfloat16)
    names = lax.broadcasted_iota(jnp.int32, (EXPERTS, PROMPT), 0)
    named = (ids_ref[0:1, :] == names) | (ids_ref[1:2, :] == names)
    first = lax.broadcasted_iota(jnp.int32, (PROMPT, PROMPT), 0)
    second = lax.broadcasted_iota(jnp.int32, (PROMPT, PROMPT), 1)
    before = jnp.where(first < second, 1.0, 0.0).astype(jnp.bfloat16)
    taken = jnp.where(named, 1.0, 0.0)
    slot = jnp.dot(taken.astype(jnp.bfloat16), before, preferred_element_type=jnp.float32)
    slot = jnp.where(named, slot, -1.0).astype(jnp.int32)
    att = att_ref[...]
    place = lax.broadcasted_iota(jnp.int32, (CAP, PROMPT), 0)
    for e in range(EXPERTS):
        chosen = jnp.where(place == slot[e : e + 1, :], 1.0, 0.0).astype(jnp.bfloat16)
        sent = jnp.dot(chosen, att, preferred_element_type=jnp.float32)
        out_ref[e * CAP : (e + 1) * CAP, :] = sent.astype(jnp.bfloat16)


def attend(limit, rows, ids_t):
    return pl.pallas_call(
        attend_kernel,
        in_specs=[
            pl.BlockSpec(memory_space=pltpu.SMEM),
            pl.BlockSpec(memory_space=pltpu.VMEM),
            pl.BlockSpec(memory_space=pltpu.VMEM),
        ],
        out_specs=[pl.BlockSpec(memory_space=pltpu.VMEM), pl.BlockSpec(memory_space=pltpu.VMEM)],
        out_shape=[
            jax.ShapeDtypeStruct((PROMPT, WIDTH), jnp.bfloat16),
            jax.ShapeDtypeStruct((EXPERTS * CAP, WIDTH), jnp.bfloat16),
        ],
        compiler_params=pltpu.CompilerParams(vmem_limit_bytes=32 << 20),
        name="attend",
    )(limit, rows, ids_t)


def norm_kernel(x_ref, gain_ref, out_ref):
    total = jnp.zeros((CAP, 1), jnp.float32)
    for i in range(EXPERTS):
        part = x_ref[i].astype(jnp.float32)
        total = total + jnp.sum(part * part, axis=1, keepdims=True)
    factor = lax.rsqrt(total * (1.0 / D) + 1e-05)
    for i in range(EXPERTS):
        cols = slice(i * WIDTH, (i + 1) * WIDTH)
        out_ref[:, cols] = (x_ref[i].astype(jnp.float32) * factor * gain_ref[:, cols]).astype(
            jnp.bfloat16
        )


def normalise(arrived, gain):
    return pl.pallas_call(
        norm_kernel,
        out_shape=jax.ShapeDtypeStruct((CAP, D), jnp.bfloat16),
        compiler_params=pltpu.CompilerParams(vmem_limit_bytes=32 << 20),
        name="normalise",
    )(arrived, gain)


K_PARTS = 6
K_PART = D // K_PARTS
COL_PARTS = 4
SIDES = EXPERTS // COL_PARTS
HALF = FF_DEV // 2
FF = 2 * FF_DEV
SPANS = ((0, FF_DEV), (FF_DEV, HALF), (FF_DEV + HALF, HALF))


def ffn_kernel(
    x0, x1, x2, x3, g0, g1, g2, u0, u1, u2, d0, d1, d2, o0, o1, o2, o3,
    xs, gate, up, down, outs, in_sem, out_sem,
):
    stages = []
    for k in range(K_PARTS):
        rows = pl.ds(k * K_PART, K_PART)
        pairs = [
            (x.at[:, rows], xs.at[pl.ds(j * CAP, CAP), rows])
            for j, x in enumerate((x0, x1, x2, x3))
        ]
        for sources, target in (((g0, g1, g2), gate), ((u0, u1, u2), up)):
            for source, (start, size) in zip(sources, SPANS):
                pairs.append((source.at[rows], target.at[rows, pl.ds(start, size)]))
        stages.append(pairs)
    for h in range(COL_PARTS):
        cols = pl.ds(h * SIDES * WIDTH, SIDES * WIDTH)
        stages.append(
            [
                (source.at[:, cols], down.at[pl.ds(start, size), cols])
                for source, (start, size) in zip((d0, d1, d2), SPANS)
            ]
        )
    stages = [
        [pltpu.make_async_copy(a, b, in_sem.at[i, j]) for j, (a, b) in enumerate(pairs)]
        for i, pairs in enumerate(stages)
    ]

    def begin(i):
        if i < len(stages):
            for copy in stages[i]:
                copy.start()

    def finish(i):
        for copy in stages[i]:
            copy.wait()
        begin(i + 2)

    begin(0)
    begin(1)
    gate_part = up_part = None
    for k in range(K_PARTS):
        finish(k)
        rows = slice(k * K_PART, (k + 1) * K_PART)
        x = xs[:, rows]
        g = jnp.dot(x, gate[rows, :], preferred_element_type=jnp.float32)
        u = jnp.dot(x, up[rows, :], preferred_element_type=jnp.float32)
        gate_part = g if gate_part is None else gate_part + g
        up_part = u if up_part is None else up_part + u
    hidden = (gate_part / (1.0 + jnp.exp(-gate_part)) * up_part).astype(jnp.bfloat16)
    out_copies = []
    for h in range(COL_PARTS):
        finish(K_PARTS + h)
        for i in range(h * SIDES, (h + 1) * SIDES):
            part = jnp.dot(
                hidden, down[:, i * WIDTH : (i + 1) * WIDTH], preferred_element_type=jnp.float32
            ).astype(jnp.bfloat16)
            for j in range(SIDE):
                outs[j, i] = part[j * CAP : (j + 1) * CAP]
        some = pl.ds(h * SIDES, SIDES)
        for j, o in enumerate((o0, o1, o2, o3)):
            copy = pltpu.make_async_copy(outs.at[j, some], o.at[some], out_sem.at[h, j])
            copy.start()
            out_copies.append(copy)
    for copy in out_copies:
        copy.wait()


def ffn(shards, gate, up, down):
    anywhere = pl.BlockSpec(memory_space=pl.ANY)
    return pl.pallas_call(
        ffn_kernel,
        in_specs=[anywhere] * 13,
        out_specs=[anywhere] * SIDE,
        out_shape=[jax.ShapeDtypeStruct((EXPERTS, CAP, WIDTH), jnp.bfloat16)] * SIDE,
        scratch_shapes=[
            pltpu.VMEM((SIDE * CAP, D), jnp.bfloat16),
            pltpu.VMEM((D, FF), jnp.bfloat16),
            pltpu.VMEM((D, FF), jnp.bfloat16),
            pltpu.VMEM((FF, D), jnp.bfloat16),
            pltpu.VMEM((SIDE, EXPERTS, CAP, WIDTH), jnp.bfloat16),
            pltpu.SemaphoreType.DMA((K_PARTS + COL_PARTS, 10)),
            pltpu.SemaphoreType.DMA((COL_PARTS, SIDE)),
        ],
        compiler_params=pltpu.CompilerParams(vmem_limit_bytes=58 << 20),
        cost_estimate=pl.CostEstimate(
            flops=6 * SIDE * CAP * D * FF,
            transcendentals=SIDE * CAP * FF,
            bytes_accessed=6 * D * FF + 4 * SIDE * CAP * D,
        ),
        name="ffn",
    )(*shards, *gate, *up, *down)


def shift(value, doubled, step):
    pairs = []
    for z in range(SIDE):
        for y in range(SIDE):
            for e in range(EXPERTS):
                along_y = (e % 2 == 0) == doubled
                to_z, to_y = (z, (y + step) % SIDE) if along_y else ((z + step) % SIDE, y)
                pairs.append(((z * SIDE + y) * EXPERTS + e, (to_z * SIDE + to_y) * EXPERTS + e))
    return lax.ppermute(value, ("z", "y", "expert"), pairs)


def trade(weight, dim):
    low = lax.slice_in_dim(weight, 0, HALF, axis=dim)
    high = lax.slice_in_dim(weight, HALF, FF_DEV, axis=dim)
    return weight, shift(low, True, 1), shift(high, True, -1)


def tie(*values):
    return lax.optimization_barrier(values)


def add(*parts):
    total = parts[0].astype(jnp.float32)
    for part in parts[1:]:
        total = total + part.astype(jnp.float32)
    return total.astype(jnp.bfloat16)


def experts(own, gate, up, down):
    across, own_low, own_high = tie(shift(own, True, 2), shift(own, False, 1), shift(own, False, -1))
    own_far, low, high = tie(shift(own_high, False, -1), shift(across, False, 1), shift(across, False, -1))
    far = shift(high, False, -1)
    sums = []
    for shards in ((own, own_low, own_high, own_far), (across, low, high, far)):
        here, to_low, to_high, to_far = ffn(shards, gate, up, down)
        passed = shift(to_far, False, -1)
        sums.append(
            add(here, shift(to_high, False, 1), shift(add(to_low, passed), False, -1))
        )
    return add(sums[0], shift(sums[1], True, 2))


def combine_kernel(att_ref, ret_ref, ids_ref, logits_ref, out_ref):
    names = lax.broadcasted_iota(jnp.int32, (PROMPT, HEAD), 1)
    ids = [ids_ref[:, c : c + 1] for c in range(2)]
    named = (ids[0] == names) | (ids[1] == names)
    first = lax.broadcasted_iota(jnp.int32, (PROMPT, PROMPT), 0)
    second = lax.broadcasted_iota(jnp.int32, (PROMPT, PROMPT), 1)
    before = jnp.where(second < first, 1.0, 0.0).astype(jnp.bfloat16)
    taken = jnp.where(named, 1.0, 0.0).astype(jnp.bfloat16)
    count = jnp.dot(before, taken, preferred_element_type=jnp.float32)
    logits = [logits_ref[:, c : c + 1] for c in range(2)]
    top = jnp.maximum(logits[0], logits[1])
    exps = [jnp.exp(v - top) for v in logits]
    total = exps[0] + exps[1]
    ret = ret_ref[...]
    column = lax.broadcasted_iota(jnp.int32, (PROMPT, EXPERTS * CAP), 1)
    mixed = None
    for c in range(2):
        slot = jnp.sum(jnp.where(ids[c] == names, count, 0.0), axis=1, keepdims=True)
        at = ids[c] * CAP + slot.astype(jnp.int32)
        chosen = jnp.where(column == at, 1.0, 0.0).astype(jnp.bfloat16)
        picked = jnp.dot(chosen, ret, preferred_element_type=jnp.float32)
        term = exps[c] / total * picked
        mixed = term if mixed is None else mixed + term
    out_ref[...] = (att_ref[...].astype(jnp.float32) + mixed).astype(jnp.bfloat16)


def combine(att, returned, ids, logits):
    return pl.pallas_call(
        combine_kernel,
        out_shape=jax.ShapeDtypeStruct((PROMPT, WIDTH), jnp.bfloat16),
        compiler_params=pltpu.CompilerParams(vmem_limit_bytes=32 << 20),
        name="combine",
    )(att, returned, ids, logits)


def fetch_rows(records, pair_blocks, gate, up_weight):
    z, y = lax.axis_index("z"), lax.axis_index("y")
    column = lax.all_gather(records, "z", axis=0, tiled=True)
    column, up_own, *gate = tie(column, up_weight, *gate)
    wanted = lax.dynamic_slice_in_dim(pair_blocks, z * SIDE, SIDE, 0).reshape(-1)
    owner = wanted // 2
    mine = (owner % SIDE == y).astype(jnp.int32)
    idx = (owner // SIDE) * 2 + wanted % 2
    picked = pick_blocks(idx, mine, column)
    rows = lax.psum_scatter(picked, "y", scatter_dimension=0, tiled=True)
    return rows, gate, up_own


def body(
    records,
    pair_blocks,
    lengths,
    norm_gain,
    gate_logits,
    expert_ids,
    gate_weight,
    up_weight,
    down_weight,
):
    dp_index = lax.axis_index("z") * SIDE + lax.axis_index("y")
    limit = lax.dynamic_slice_in_dim(lengths, dp_index, 1, 0)
    gate = trade(gate_weight[0], 1)
    rows, gate, up_own = fetch_rows(records, pair_blocks, gate, up_weight[0])
    rows, down_own, *up = tie(rows, down_weight[0], *trade(up_own, 1))
    rows = rows.reshape(PROMPT, QKV)
    down = trade(down_own, 0)
    att, outgoing = attend(limit, rows, expert_ids.T)
    arrived = lax.all_to_all(
        outgoing.reshape(EXPERTS, CAP, WIDTH), "expert", split_axis=0, concat_axis=0, tiled=True
    )
    arrived, *down = tie(arrived, *down)
    normed = normalise(arrived, norm_gain.reshape(1, D))
    summed = experts(normed, gate, up, down)
    returned = lax.all_to_all(summed, "expert", split_axis=0, concat_axis=0, tiled=True)
    return combine(att, returned.reshape(EXPERTS * CAP, WIDTH), expert_ids, gate_logits)


def solution(mesh):
    fine = Mesh(mesh.devices.reshape(SIDE, SIDE, EXPERTS), ("z", "y", "expert"))
    dp = ("z", "y")
    placed = (
        P(dp, None, "expert"),
        P(),
        P(),
        P(),
        P(dp, None),
        P(dp, None),
        P("expert", None, dp),
        P("expert", None, dp),
        P("expert", dp, None),
    )
    return jax.shard_map(
        body, mesh=fine, in_specs=placed, out_specs=P(dp, "expert"), check_vma=False
    )
```

```python
import math

import jax
import jax.numpy as jnp
from jax import lax
from jax.experimental import pallas as pl
from jax.experimental.pallas import tpu as pltpu
from jax.sharding import Mesh
from jax.sharding import PartitionSpec as P

HEAD = 128
GROUP = 6
BLOCK = 128
PROMPT = 256
EXPERTS = 8
CAP = 80
WIDTH = 768
D = 6144
FF_DEV = 512
N_DP = 16
SIDE = 4
QKV = 1024


def pick_kernel(sel_ref, own, low, high, far0, far1, here, up, down, up_far, down_far):
    sources = [own.at[0], own.at[1], low.at[0], low.at[1], high.at[0], high.at[1], far0.at[0], far1.at[0]]
    targets = [here.at[0], here.at[1], up.at[0], up.at[1], down.at[0], down.at[1], up_far.at[0], down_far.at[0]]
    for i, target in enumerate(targets):
        for k, source in enumerate(sources):

            @pl.when(sel_ref[i] == k)
            def _():
                target[...] = source[...]

        @pl.when(sel_ref[i] < 0)
        def _():
            target[...] = jnp.zeros_like(target)


def pick_blocks(sel, blocks):
    vmem = pl.BlockSpec(memory_space=pltpu.VMEM)
    return pl.pallas_call(
        pick_kernel,
        in_specs=[pl.BlockSpec(memory_space=pltpu.SMEM)] + [vmem] * 5,
        out_specs=[vmem] * 5,
        out_shape=[
            jax.ShapeDtypeStruct((n, BLOCK, QKV), jnp.bfloat16) for n in (2, 2, 2, 1, 1)
        ],
        compiler_params=pltpu.CompilerParams(vmem_limit_bytes=16 << 20),
        name="pick_blocks",
    )(sel, *blocks)


def attend_kernel(len_ref, here_ref, low_ref, high_ref, ids_ref, att_ref, out_ref, rows_ref):
    limit = len_ref[0]
    rows_ref[...] = here_ref[...] + low_ref[...] + high_ref[...]
    scale = 1.0 / math.sqrt(HEAD)
    for top in (0, BLOCK):
        span = top + BLOCK
        keys = rows_ref[0:span, GROUP * HEAD : (GROUP + 1) * HEAD]
        values = rows_ref[0:span, (GROUP + 1) * HEAD : (GROUP + 2) * HEAD]
        row = lax.broadcasted_iota(jnp.int32, (BLOCK, span), 0) + top
        col = lax.broadcasted_iota(jnp.int32, (BLOCK, span), 1)
        allowed = (col <= row) & (col < limit)
        for g in range(GROUP):
            query = rows_ref[top:span, g * HEAD : (g + 1) * HEAD]
            scores = lax.dot_general(
                query, keys, (((1,), (1,)), ((), ())), preferred_element_type=jnp.float32
            )
            scores = jnp.where(allowed, scores * scale, -jnp.inf)
            exponent = jnp.exp(scores - jnp.max(scores, axis=1, keepdims=True))
            probs = (exponent / jnp.sum(exponent, axis=1, keepdims=True)).astype(jnp.bfloat16)
            mixed = jnp.dot(probs, values, preferred_element_type=jnp.float32)
            att_ref[top:span, g * HEAD : (g + 1) * HEAD] = mixed.astype(jnp.bfloat16)
    names = lax.broadcasted_iota(jnp.int32, (EXPERTS, PROMPT), 0)
    named = (ids_ref[0:1, :] == names) | (ids_ref[1:2, :] == names)
    first = lax.broadcasted_iota(jnp.int32, (PROMPT, PROMPT), 0)
    second = lax.broadcasted_iota(jnp.int32, (PROMPT, PROMPT), 1)
    before = jnp.where(first < second, 1.0, 0.0).astype(jnp.bfloat16)
    taken = jnp.where(named, 1.0, 0.0)
    slot = jnp.dot(taken.astype(jnp.bfloat16), before, preferred_element_type=jnp.float32)
    slot = jnp.where(named, slot, -1.0).astype(jnp.int32)
    att = att_ref[...]
    place = lax.broadcasted_iota(jnp.int32, (CAP, PROMPT), 0)
    for e in range(EXPERTS):
        chosen = jnp.where(place == slot[e : e + 1, :], 1.0, 0.0).astype(jnp.bfloat16)
        sent = jnp.dot(chosen, att, preferred_element_type=jnp.float32)
        out_ref[e * CAP : (e + 1) * CAP, :] = sent.astype(jnp.bfloat16)


def attend(limit, parts, ids_t):
    vmem = pl.BlockSpec(memory_space=pltpu.VMEM)
    return pl.pallas_call(
        attend_kernel,
        in_specs=[pl.BlockSpec(memory_space=pltpu.SMEM)] + [vmem] * 4,
        out_specs=[vmem, vmem],
        out_shape=[
            jax.ShapeDtypeStruct((PROMPT, WIDTH), jnp.bfloat16),
            jax.ShapeDtypeStruct((EXPERTS * CAP, WIDTH), jnp.bfloat16),
        ],
        scratch_shapes=[pltpu.VMEM((PROMPT, QKV), jnp.bfloat16)],
        compiler_params=pltpu.CompilerParams(vmem_limit_bytes=16 << 20),
        name="attend",
    )(limit, *parts, ids_t)


def norm_kernel(x_ref, gain_ref, out_ref):
    total = jnp.zeros((CAP, 1), jnp.float32)
    for i in range(EXPERTS):
        part = x_ref[i].astype(jnp.float32)
        total = total + jnp.sum(part * part, axis=1, keepdims=True)
    factor = lax.rsqrt(total * (1.0 / D) + 1e-05)
    for i in range(EXPERTS):
        cols = slice(i * WIDTH, (i + 1) * WIDTH)
        out_ref[:, cols] = (x_ref[i].astype(jnp.float32) * factor * gain_ref[:, cols]).astype(
            jnp.bfloat16
        )


def normalise(arrived, gain):
    return pl.pallas_call(
        norm_kernel,
        out_shape=jax.ShapeDtypeStruct((CAP, D), jnp.bfloat16),
        compiler_params=pltpu.CompilerParams(vmem_limit_bytes=32 << 20),
        name="normalise",
    )(arrived, gain)


def ffn_kernel(x0, x1, x2, x3, gate_ref, up_ref, down_ref, o0, o1, o2, o3, xs):
    for j, x in enumerate((x0, x1, x2, x3)):
        xs[j * CAP : (j + 1) * CAP, :] = x[...]
    gate = jnp.dot(xs[...], gate_ref[0], preferred_element_type=jnp.float32)
    up = jnp.dot(xs[...], up_ref[0], preferred_element_type=jnp.float32)
    hidden = (gate / (1.0 + jnp.exp(-gate)) * up).astype(jnp.bfloat16)
    for i in range(EXPERTS):
        part = jnp.dot(
            hidden, down_ref[0, :, i * WIDTH : (i + 1) * WIDTH], preferred_element_type=jnp.float32
        ).astype(jnp.bfloat16)
        for j, o in enumerate((o0, o1, o2, o3)):
            o[i] = part[j * CAP : (j + 1) * CAP]


def ffn(shards, gate, up, down):
    vmem = pl.BlockSpec(memory_space=pltpu.VMEM)
    return pl.pallas_call(
        ffn_kernel,
        in_specs=[vmem] * 7,
        out_specs=[vmem] * SIDE,
        out_shape=[jax.ShapeDtypeStruct((EXPERTS, CAP, WIDTH), jnp.bfloat16)] * SIDE,
        scratch_shapes=[pltpu.VMEM((SIDE * CAP, D), jnp.bfloat16)],
        compiler_params=pltpu.CompilerParams(vmem_limit_bytes=12 << 20),
        cost_estimate=pl.CostEstimate(
            flops=6 * SIDE * CAP * D * FF_DEV,
            transcendentals=SIDE * CAP * FF_DEV,
            bytes_accessed=4 * SIDE * CAP * D,
        ),
        name="ffn",
    )(*shards, gate, up, down)


def shift(value, first, step):
    pairs = []
    for z in range(SIDE):
        for y in range(SIDE):
            for e in range(EXPERTS):
                along_y = (e % 2 == 0) == first
                to_z, to_y = (z, (y + step) % SIDE) if along_y else ((z + step) % SIDE, y)
                pairs.append(((z * SIDE + y) * EXPERTS + e, (to_z * SIDE + to_y) * EXPERTS + e))
    return lax.ppermute(value, ("z", "y", "expert"), pairs)


def tie(*values):
    return lax.optimization_barrier(values)


def add(*parts):
    total = parts[0].astype(jnp.float32)
    for part in parts[1:]:
        total = total + part.astype(jnp.float32)
    return total.astype(jnp.bfloat16)


def load_kernel(gate_hbm, up_hbm, down_hbm, gate, up, down, sems):
    copies = [
        pltpu.make_async_copy(a, b, sems.at[i])
        for i, (a, b) in enumerate(((gate_hbm, gate), (up_hbm, up), (down_hbm, down)))
    ]
    for copy in copies:
        copy.start()
    for copy in copies:
        copy.wait()


def load(*weights):
    return pl.pallas_call(
        load_kernel,
        in_specs=[pl.BlockSpec(memory_space=pl.ANY)] * 3,
        out_specs=[pl.BlockSpec(memory_space=pltpu.VMEM)] * 3,
        out_shape=[jax.ShapeDtypeStruct(w.shape, w.dtype) for w in weights],
        scratch_shapes=[pltpu.SemaphoreType.DMA((3,))],
        compiler_params=pltpu.CompilerParams(vmem_limit_bytes=4 << 20),
        name="load",
    )(*weights)


def experts(own, weights):
    low, high, own_low, own_high, *weights = tie(
        shift(own, True, 1),
        shift(own, True, -1),
        shift(own, False, 1),
        shift(own, False, -1),
        *load(*weights),
    )
    across, own_far, low_low, low_high, high_low, high_high = tie(
        shift(low, True, 1),
        shift(own_high, False, -1),
        shift(low, False, 1),
        shift(low, False, -1),
        shift(high, False, 1),
        shift(high, False, -1),
    )
    parts = {0: ffn((own, own_low, own_high, own_far), *weights)}
    low_far, high_far, across_low, across_high, *parts[0] = tie(
        shift(low_low, False, 1),
        shift(high_high, False, -1),
        shift(across, False, 1),
        shift(across, False, -1),
        *parts[0],
    )
    parts[-1] = ffn((low, low_low, low_high, low_far), *weights)
    across_far, *parts[-1] = tie(shift(across_low, False, 1), *parts[-1])
    parts[2] = ffn((across, across_low, across_high, across_far), *weights)
    parts[1] = ffn((high, high_low, high_high, high_far), *weights)
    sums = {}
    for a, way in ((0, -1), (-1, 1), (2, 1), (1, -1)):
        here, to_low, to_high, to_far = parts[a]
        ahead, behind = (to_high, to_low) if way == 1 else (to_low, to_high)
        passed = shift(to_far, False, way)
        sums[a] = add(here, shift(add(ahead, passed), False, way), shift(behind, False, -way))
    passed = shift(sums[2], True, 1)
    return add(sums[0], shift(add(sums[1], passed), True, 1), shift(sums[-1], True, -1))


def combine_kernel(att_ref, ret_ref, ids_ref, logits_ref, out_ref):
    names = lax.broadcasted_iota(jnp.int32, (PROMPT, HEAD), 1)
    ids = [ids_ref[:, c : c + 1] for c in range(2)]
    named = (ids[0] == names) | (ids[1] == names)
    first = lax.broadcasted_iota(jnp.int32, (PROMPT, PROMPT), 0)
    second = lax.broadcasted_iota(jnp.int32, (PROMPT, PROMPT), 1)
    before = jnp.where(second < first, 1.0, 0.0).astype(jnp.bfloat16)
    taken = jnp.where(named, 1.0, 0.0).astype(jnp.bfloat16)
    count = jnp.dot(before, taken, preferred_element_type=jnp.float32)
    logits = [logits_ref[:, c : c + 1] for c in range(2)]
    top = jnp.maximum(logits[0], logits[1])
    exps = [jnp.exp(v - top) for v in logits]
    total = exps[0] + exps[1]
    ret = ret_ref[...]
    column = lax.broadcasted_iota(jnp.int32, (PROMPT, EXPERTS * CAP), 1)
    mixed = None
    for c in range(2):
        slot = jnp.sum(jnp.where(ids[c] == names, count, 0.0), axis=1, keepdims=True)
        at = ids[c] * CAP + slot.astype(jnp.int32)
        chosen = jnp.where(column == at, 1.0, 0.0).astype(jnp.bfloat16)
        picked = jnp.dot(chosen, ret, preferred_element_type=jnp.float32)
        term = exps[c] / total * picked
        mixed = term if mixed is None else mixed + term
    out_ref[...] = (att_ref[...].astype(jnp.float32) + mixed).astype(jnp.bfloat16)


def combine(att, returned, ids, logits):
    return pl.pallas_call(
        combine_kernel,
        out_shape=jax.ShapeDtypeStruct((PROMPT, WIDTH), jnp.bfloat16),
        compiler_params=pltpu.CompilerParams(vmem_limit_bytes=32 << 20),
        name="combine",
    )(att, returned, ids, logits)


def fetch_rows(records, pair_blocks):
    z, y = lax.axis_index("z"), lax.axis_index("y")
    y_first = lax.axis_index("expert") % 2 == 0
    low, high = tie(shift(records, True, 1), shift(records, True, -1))
    far0, far1 = tie(shift(low[:1], True, 1), shift(high[1:], True, -1))
    first, second = jnp.where(y_first, y, z), jnp.where(y_first, z, y)
    ahead = jnp.array([0, 0, 1, 1, -1, -1, 2, 2], jnp.int32)
    slot = jnp.array([0, 1, 0, 1, 0, 1, 0, 1], jnp.int32)
    target = (second + ahead) % SIDE
    prompt = jnp.where(y_first, target * SIDE + first, first * SIDE + target)
    wanted = pair_blocks[prompt, slot]
    owner = wanted // 2
    own_z, own_y = owner // SIDE, owner % SIDE
    own_first, own_second = jnp.where(y_first, own_y, own_z), jnp.where(y_first, own_z, own_y)
    away = (own_first - first) % SIDE
    half = wanted % 2
    source = jnp.where(away == 0, half, jnp.where(away == 3, 2 + half, jnp.where(away == 1, 4 + half, 6 + half)))
    sel = jnp.where(own_second == second, source, -1)
    here, up, down, up_far, down_far = pick_blocks(sel, (records, low, high, far0, far1))
    up_got, down_got = tie(shift(up_far, False, 1), shift(down_far, False, -1))
    up = jnp.concatenate([up[:1] + up_got, up[1:]], axis=0)
    down = jnp.concatenate([down[:1], down[1:] + down_got], axis=0)
    return here, shift(up, False, 1), shift(down, False, -1)


def body(
    records,
    pair_blocks,
    lengths,
    norm_gain,
    gate_logits,
    expert_ids,
    gate_weight,
    up_weight,
    down_weight,
):
    dp_index = lax.axis_index("z") * SIDE + lax.axis_index("y")
    limit = lax.dynamic_slice_in_dim(lengths, dp_index, 1, 0)
    parts = [part.reshape(PROMPT, QKV) for part in fetch_rows(records, pair_blocks)]
    att, outgoing = attend(limit, parts, expert_ids.T)
    arrived = lax.all_to_all(
        outgoing.reshape(EXPERTS, CAP, WIDTH), "expert", split_axis=0, concat_axis=0, tiled=True
    )
    normed = normalise(arrived, norm_gain.reshape(1, D))
    summed = experts(normed, (gate_weight, up_weight, down_weight))
    returned = lax.all_to_all(summed, "expert", split_axis=0, concat_axis=0, tiled=True)
    return combine(att, returned.reshape(EXPERTS * CAP, WIDTH), expert_ids, gate_logits)


def solution(mesh):
    fine = Mesh(mesh.devices.reshape(SIDE, SIDE, EXPERTS), ("z", "y", "expert"))
    dp = ("z", "y")
    placed = (
        P(dp, None, "expert"),
        P(),
        P(),
        P(),
        P(dp, None),
        P(dp, None),
        P("expert", None, dp),
        P("expert", None, dp),
        P("expert", dp, None),
    )
    return jax.shard_map(
        body, mesh=fine, in_specs=placed, out_specs=P(dp, "expert"), check_vma=False
    )
```

```python
import math

import jax
import jax.numpy as jnp
from jax import lax
from jax.experimental import pallas as pl
from jax.experimental.pallas import tpu as pltpu
from jax.sharding import Mesh
from jax.sharding import PartitionSpec as P

HEAD = 128
GROUP = 6
BLOCK = 128
PROMPT = 256
EXPERTS = 8
CAP = 80
WIDTH = 768
D = 6144
FF_DEV = 512
N_DP = 16
SIDE = 4
QKV = 1024


def pick_kernel(sel_ref, own, low, high, far0, far1, here, up, down, up_far, down_far):
    sources = [own.at[0], own.at[1], low.at[0], low.at[1], high.at[0], high.at[1], far0.at[0], far1.at[0]]
    targets = [here.at[0], here.at[1], up.at[0], up.at[1], down.at[0], down.at[1], up_far.at[0], down_far.at[0]]
    for i, target in enumerate(targets):
        for k, source in enumerate(sources):

            @pl.when(sel_ref[i] == k)
            def _():
                target[...] = source[...]

        @pl.when(sel_ref[i] < 0)
        def _():
            target[...] = jnp.zeros_like(target)


def pick_blocks(sel, blocks):
    vmem = pl.BlockSpec(memory_space=pltpu.VMEM)
    return pl.pallas_call(
        pick_kernel,
        in_specs=[pl.BlockSpec(memory_space=pltpu.SMEM)] + [vmem] * 5,
        out_specs=[vmem] * 5,
        out_shape=[
            jax.ShapeDtypeStruct((n, BLOCK, QKV), jnp.bfloat16) for n in (2, 2, 2, 1, 1)
        ],
        compiler_params=pltpu.CompilerParams(vmem_limit_bytes=16 << 20),
        name="pick_blocks",
    )(sel, *blocks)


def attend_kernel(len_ref, here_ref, low_ref, high_ref, ids_ref, att_ref, out_ref, rows_ref):
    limit = len_ref[0]
    rows_ref[...] = here_ref[...] + low_ref[...] + high_ref[...]
    scale = 1.0 / math.sqrt(HEAD)
    for top in (0, BLOCK):
        span = top + BLOCK
        keys = rows_ref[0:span, GROUP * HEAD : (GROUP + 1) * HEAD]
        values = rows_ref[0:span, (GROUP + 1) * HEAD : (GROUP + 2) * HEAD]
        row = lax.broadcasted_iota(jnp.int32, (BLOCK, span), 0) + top
        col = lax.broadcasted_iota(jnp.int32, (BLOCK, span), 1)
        allowed = (col <= row) & (col < limit)
        for g in range(GROUP):
            query = rows_ref[top:span, g * HEAD : (g + 1) * HEAD]
            scores = lax.dot_general(
                query, keys, (((1,), (1,)), ((), ())), preferred_element_type=jnp.float32
            )
            scores = jnp.where(allowed, scores * scale, -jnp.inf)
            exponent = jnp.exp(scores - jnp.max(scores, axis=1, keepdims=True))
            probs = (exponent / jnp.sum(exponent, axis=1, keepdims=True)).astype(jnp.bfloat16)
            mixed = jnp.dot(probs, values, preferred_element_type=jnp.float32)
            att_ref[top:span, g * HEAD : (g + 1) * HEAD] = mixed.astype(jnp.bfloat16)
    names = lax.broadcasted_iota(jnp.int32, (EXPERTS, PROMPT), 0)
    named = (ids_ref[0:1, :] == names) | (ids_ref[1:2, :] == names)
    first = lax.broadcasted_iota(jnp.int32, (PROMPT, PROMPT), 0)
    second = lax.broadcasted_iota(jnp.int32, (PROMPT, PROMPT), 1)
    before = jnp.where(first < second, 1.0, 0.0).astype(jnp.bfloat16)
    taken = jnp.where(named, 1.0, 0.0)
    slot = jnp.dot(taken.astype(jnp.bfloat16), before, preferred_element_type=jnp.float32)
    slot = jnp.where(named, slot, -1.0).astype(jnp.int32)
    att = att_ref[...]
    place = lax.broadcasted_iota(jnp.int32, (CAP, PROMPT), 0)
    for e in range(EXPERTS):
        chosen = jnp.where(place == slot[e : e + 1, :], 1.0, 0.0).astype(jnp.bfloat16)
        sent = jnp.dot(chosen, att, preferred_element_type=jnp.float32)
        out_ref[e * CAP : (e + 1) * CAP, :] = sent.astype(jnp.bfloat16)


def attend(limit, parts, ids_t):
    vmem = pl.BlockSpec(memory_space=pltpu.VMEM)
    return pl.pallas_call(
        attend_kernel,
        in_specs=[pl.BlockSpec(memory_space=pltpu.SMEM)] + [vmem] * 4,
        out_specs=[vmem, vmem],
        out_shape=[
            jax.ShapeDtypeStruct((PROMPT, WIDTH), jnp.bfloat16),
            jax.ShapeDtypeStruct((EXPERTS * CAP, WIDTH), jnp.bfloat16),
        ],
        scratch_shapes=[pltpu.VMEM((PROMPT, QKV), jnp.bfloat16)],
        compiler_params=pltpu.CompilerParams(vmem_limit_bytes=16 << 20),
        name="attend",
    )(limit, *parts, ids_t)


def norm_kernel(x_ref, gain_ref, out_ref):
    total = jnp.zeros((CAP, 1), jnp.float32)
    for i in range(EXPERTS):
        part = x_ref[i].astype(jnp.float32)
        total = total + jnp.sum(part * part, axis=1, keepdims=True)
    factor = lax.rsqrt(total * (1.0 / D) + 1e-05)
    for i in range(EXPERTS):
        cols = slice(i * WIDTH, (i + 1) * WIDTH)
        out_ref[:, cols] = (x_ref[i].astype(jnp.float32) * factor * gain_ref[:, cols]).astype(
            jnp.bfloat16
        )


def normalise(arrived, gain):
    return pl.pallas_call(
        norm_kernel,
        out_shape=jax.ShapeDtypeStruct((CAP, D), jnp.bfloat16),
        compiler_params=pltpu.CompilerParams(vmem_limit_bytes=32 << 20),
        name="normalise",
    )(arrived, gain)


def ffn_kernel(x0, x1, x2, x3, gate_ref, up_ref, down_ref, o0, o1, o2, o3, xs):
    for j, x in enumerate((x0, x1, x2, x3)):
        xs[j * CAP : (j + 1) * CAP, :] = x[...]
    gate = jnp.dot(xs[...], gate_ref[0], preferred_element_type=jnp.float32)
    up = jnp.dot(xs[...], up_ref[0], preferred_element_type=jnp.float32)
    hidden = (gate / (1.0 + jnp.exp(-gate)) * up).astype(jnp.bfloat16)
    for i in range(EXPERTS):
        part = jnp.dot(
            hidden, down_ref[0, :, i * WIDTH : (i + 1) * WIDTH], preferred_element_type=jnp.float32
        ).astype(jnp.bfloat16)
        for j, o in enumerate((o0, o1, o2, o3)):
            o[i] = part[j * CAP : (j + 1) * CAP]


def ffn(shards, gate, up, down):
    vmem = pl.BlockSpec(memory_space=pltpu.VMEM)
    return pl.pallas_call(
        ffn_kernel,
        in_specs=[vmem] * 7,
        out_specs=[vmem] * SIDE,
        out_shape=[jax.ShapeDtypeStruct((EXPERTS, CAP, WIDTH), jnp.bfloat16)] * SIDE,
        scratch_shapes=[pltpu.VMEM((SIDE * CAP, D), jnp.bfloat16)],
        compiler_params=pltpu.CompilerParams(vmem_limit_bytes=12 << 20),
        cost_estimate=pl.CostEstimate(
            flops=6 * SIDE * CAP * D * FF_DEV,
            transcendentals=SIDE * CAP * FF_DEV,
            bytes_accessed=4 * SIDE * CAP * D,
        ),
        name="ffn",
    )(*shards, gate, up, down)


def shift(value, first, step):
    pairs = []
    for z in range(SIDE):
        for y in range(SIDE):
            for e in range(EXPERTS):
                along_y = (e % 2 == 0) == first
                to_z, to_y = (z, (y + step) % SIDE) if along_y else ((z + step) % SIDE, y)
                pairs.append(((z * SIDE + y) * EXPERTS + e, (to_z * SIDE + to_y) * EXPERTS + e))
    return lax.ppermute(value, ("z", "y", "expert"), pairs)


def tie(*values):
    return lax.optimization_barrier(values)


def add(*parts):
    total = parts[0].astype(jnp.float32)
    for part in parts[1:]:
        total = total + part.astype(jnp.float32)
    return total.astype(jnp.bfloat16)


def load_kernel(gate_hbm, up_hbm, down_hbm, gate, up, down, sems):
    copies = [
        pltpu.make_async_copy(a, b, sems.at[i])
        for i, (a, b) in enumerate(((gate_hbm, gate), (up_hbm, up), (down_hbm, down)))
    ]
    for copy in copies:
        copy.start()
    for copy in copies:
        copy.wait()


def load(*weights):
    return pl.pallas_call(
        load_kernel,
        in_specs=[pl.BlockSpec(memory_space=pl.ANY)] * 3,
        out_specs=[pl.BlockSpec(memory_space=pltpu.VMEM)] * 3,
        out_shape=[jax.ShapeDtypeStruct(w.shape, w.dtype) for w in weights],
        scratch_shapes=[pltpu.SemaphoreType.DMA((3,))],
        compiler_params=pltpu.CompilerParams(vmem_limit_bytes=4 << 20),
        name="load",
    )(*weights)


def experts(own, weights):
    low, high = shift(own, True, 1), shift(own, True, -1)
    own_low, own_high = shift(own, False, 1), shift(own, False, -1)
    low, high, *weights = tie(low, high, *load(*weights))
    across, low_high = shift(low, True, 1), shift(low, False, -1)
    own_low, own_high, low, high = tie(own_low, own_high, low, high)
    low_low, high_high = shift(low, False, 1), shift(high, False, -1)
    across, low_high, own_high, high = tie(across, low_high, own_high, high)
    high_low, own_far = shift(high, False, 1), shift(own_high, False, -1)
    low_low, high_high, across = tie(low_low, high_high, across)
    across_low, across_high = shift(across, False, 1), shift(across, False, -1)
    high_low, own_far, low_low, high_high = tie(high_low, own_far, low_low, high_high)
    low_far, high_far = shift(low_low, False, 1), shift(high_high, False, -1)
    own_parts = ffn((own, own_low, own_high, own_far), *weights)
    across_low, across_high, *own_parts = tie(across_low, across_high, *own_parts)
    across_far, own_passed = shift(across_low, False, 1), shift(own_parts[3], False, -1)
    low_far, high_far = tie(low_far, high_far)
    low_parts = ffn((low, low_low, low_high, low_far), *weights)
    low_passed = shift(low_parts[3], False, 1)
    high_parts = ffn((high, high_low, high_high, high_far), *weights)
    high_passed = shift(high_parts[3], False, -1)
    across_far, own_passed = tie(across_far, own_passed)
    across_parts = ffn((across, across_low, across_high, across_far), *weights)
    own_sum = add(
        own_parts[0],
        shift(add(own_parts[1], own_passed), False, -1),
        shift(own_parts[2], False, 1),
    )
    low_passed, high_passed, *across_parts = tie(low_passed, high_passed, *across_parts)
    across_passed = shift(across_parts[3], False, 1)
    across_sum = add(
        across_parts[0],
        shift(add(across_parts[2], across_passed), False, 1),
        shift(across_parts[1], False, -1),
    )
    low_sum = add(
        low_parts[0],
        shift(add(low_parts[2], low_passed), False, 1),
        shift(low_parts[1], False, -1),
    )
    high_sum = add(
        high_parts[0],
        shift(add(high_parts[1], high_passed), False, -1),
        shift(high_parts[2], False, 1),
    )
    passed = shift(across_sum, True, 1)
    return add(own_sum, shift(add(high_sum, passed), True, 1), shift(low_sum, True, -1))


def combine_kernel(att_ref, ret_ref, ids_ref, logits_ref, out_ref):
    names = lax.broadcasted_iota(jnp.int32, (PROMPT, HEAD), 1)
    ids = [ids_ref[:, c : c + 1] for c in range(2)]
    named = (ids[0] == names) | (ids[1] == names)
    first = lax.broadcasted_iota(jnp.int32, (PROMPT, PROMPT), 0)
    second = lax.broadcasted_iota(jnp.int32, (PROMPT, PROMPT), 1)
    before = jnp.where(second < first, 1.0, 0.0).astype(jnp.bfloat16)
    taken = jnp.where(named, 1.0, 0.0).astype(jnp.bfloat16)
    count = jnp.dot(before, taken, preferred_element_type=jnp.float32)
    logits = [logits_ref[:, c : c + 1] for c in range(2)]
    top = jnp.maximum(logits[0], logits[1])
    exps = [jnp.exp(v - top) for v in logits]
    total = exps[0] + exps[1]
    ret = ret_ref[...]
    column = lax.broadcasted_iota(jnp.int32, (PROMPT, EXPERTS * CAP), 1)
    mixed = None
    for c in range(2):
        slot = jnp.sum(jnp.where(ids[c] == names, count, 0.0), axis=1, keepdims=True)
        at = ids[c] * CAP + slot.astype(jnp.int32)
        chosen = jnp.where(column == at, 1.0, 0.0).astype(jnp.bfloat16)
        picked = jnp.dot(chosen, ret, preferred_element_type=jnp.float32)
        term = exps[c] / total * picked
        mixed = term if mixed is None else mixed + term
    out_ref[...] = (att_ref[...].astype(jnp.float32) + mixed).astype(jnp.bfloat16)


def combine(att, returned, ids, logits):
    return pl.pallas_call(
        combine_kernel,
        out_shape=jax.ShapeDtypeStruct((PROMPT, WIDTH), jnp.bfloat16),
        compiler_params=pltpu.CompilerParams(vmem_limit_bytes=32 << 20),
        name="combine",
    )(att, returned, ids, logits)


def fetch_rows(records, pair_blocks):
    z, y = lax.axis_index("z"), lax.axis_index("y")
    y_first = lax.axis_index("expert") % 2 == 0
    low, high = tie(shift(records, True, 1), shift(records, True, -1))
    far0, far1 = tie(shift(low[:1], True, 1), shift(high[1:], True, -1))
    first, second = jnp.where(y_first, y, z), jnp.where(y_first, z, y)
    ahead = jnp.array([0, 0, 1, 1, -1, -1, 2, 2], jnp.int32)
    slot = jnp.array([0, 1, 0, 1, 0, 1, 0, 1], jnp.int32)
    target = (second + ahead) % SIDE
    prompt = jnp.where(y_first, target * SIDE + first, first * SIDE + target)
    wanted = pair_blocks[prompt, slot]
    owner = wanted // 2
    own_z, own_y = owner // SIDE, owner % SIDE
    own_first, own_second = jnp.where(y_first, own_y, own_z), jnp.where(y_first, own_z, own_y)
    away = (own_first - first) % SIDE
    half = wanted % 2
    source = jnp.where(away == 0, half, jnp.where(away == 3, 2 + half, jnp.where(away == 1, 4 + half, 6 + half)))
    sel = jnp.where(own_second == second, source, -1)
    here, up, down, up_far, down_far = pick_blocks(sel, (records, low, high, far0, far1))
    up_got, down_got = tie(shift(up_far, False, 1), shift(down_far, False, -1))
    up = jnp.concatenate([up[:1] + up_got, up[1:]], axis=0)
    down = jnp.concatenate([down[:1], down[1:] + down_got], axis=0)
    return here, shift(up, False, 1), shift(down, False, -1)


def body(
    records,
    pair_blocks,
    lengths,
    norm_gain,
    gate_logits,
    expert_ids,
    gate_weight,
    up_weight,
    down_weight,
):
    dp_index = lax.axis_index("z") * SIDE + lax.axis_index("y")
    limit = lax.dynamic_slice_in_dim(lengths, dp_index, 1, 0)
    parts = [part.reshape(PROMPT, QKV) for part in fetch_rows(records, pair_blocks)]
    att, outgoing = attend(limit, parts, expert_ids.T)
    arrived = lax.all_to_all(
        outgoing.reshape(EXPERTS, CAP, WIDTH), "expert", split_axis=0, concat_axis=0, tiled=True
    )
    normed = normalise(arrived, norm_gain.reshape(1, D))
    summed = experts(normed, (gate_weight, up_weight, down_weight))
    returned = lax.all_to_all(summed, "expert", split_axis=0, concat_axis=0, tiled=True)
    return combine(att, returned.reshape(EXPERTS * CAP, WIDTH), expert_ids, gate_logits)


def solution(mesh):
    fine = Mesh(mesh.devices.reshape(SIDE, SIDE, EXPERTS), ("z", "y", "expert"))
    dp = ("z", "y")
    placed = (
        P(dp, None, "expert"),
        P(),
        P(),
        P(),
        P(dp, None),
        P(dp, None),
        P("expert", None, dp),
        P("expert", None, dp),
        P("expert", dp, None),
    )
    return jax.shard_map(
        body, mesh=fine, in_specs=placed, out_specs=P(dp, "expert"), check_vma=False
    )
```

```python
import math

import jax
import jax.numpy as jnp
from jax import lax
from jax.experimental import pallas as pl
from jax.experimental.pallas import tpu as pltpu
from jax.sharding import Mesh
from jax.sharding import PartitionSpec as P

HEAD = 128
GROUP = 6
BLOCK = 128
PROMPT = 256
EXPERTS = 8
CAP = 80
WIDTH = 768
D = 6144
FF_DEV = 512
N_DP = 16
SIDE = 4
QKV = 1024


def pick_kernel(sel_ref, own, low, high, far0, far1, here, up, down, up_far, down_far):
    sources = [own.at[0], own.at[1], low.at[0], low.at[1], high.at[0], high.at[1], far0.at[0], far1.at[0]]
    targets = [here.at[0], here.at[1], up.at[0], up.at[1], down.at[0], down.at[1], up_far.at[0], down_far.at[0]]
    for i, target in enumerate(targets):
        for k, source in enumerate(sources):

            @pl.when(sel_ref[i] == k)
            def _():
                target[...] = source[...]

        @pl.when(sel_ref[i] < 0)
        def _():
            target[...] = jnp.zeros_like(target)


def pick_blocks(sel, blocks):
    vmem = pl.BlockSpec(memory_space=pltpu.VMEM)
    return pl.pallas_call(
        pick_kernel,
        in_specs=[pl.BlockSpec(memory_space=pltpu.SMEM)] + [vmem] * 5,
        out_specs=[vmem] * 5,
        out_shape=[
            jax.ShapeDtypeStruct((n, BLOCK, QKV), jnp.bfloat16) for n in (2, 2, 2, 1, 1)
        ],
        compiler_params=pltpu.CompilerParams(vmem_limit_bytes=16 << 20),
        name="pick_blocks",
    )(sel, *blocks)


def attend_kernel(len_ref, here_ref, low_ref, high_ref, ids_ref, att_ref, out_ref, rows_ref):
    limit = len_ref[0]
    rows_ref[...] = here_ref[...] + low_ref[...] + high_ref[...]
    scale = 1.0 / math.sqrt(HEAD)
    for top in (0, BLOCK):
        span = top + BLOCK
        keys = rows_ref[0:span, GROUP * HEAD : (GROUP + 1) * HEAD]
        values = rows_ref[0:span, (GROUP + 1) * HEAD : (GROUP + 2) * HEAD]
        row = lax.broadcasted_iota(jnp.int32, (BLOCK, span), 0) + top
        col = lax.broadcasted_iota(jnp.int32, (BLOCK, span), 1)
        allowed = (col <= row) & (col < limit)
        for g in range(GROUP):
            query = rows_ref[top:span, g * HEAD : (g + 1) * HEAD]
            scores = lax.dot_general(
                query, keys, (((1,), (1,)), ((), ())), preferred_element_type=jnp.float32
            )
            scores = jnp.where(allowed, scores * scale, -jnp.inf)
            exponent = jnp.exp(scores - jnp.max(scores, axis=1, keepdims=True))
            probs = (exponent / jnp.sum(exponent, axis=1, keepdims=True)).astype(jnp.bfloat16)
            mixed = jnp.dot(probs, values, preferred_element_type=jnp.float32)
            att_ref[top:span, g * HEAD : (g + 1) * HEAD] = mixed.astype(jnp.bfloat16)
    names = lax.broadcasted_iota(jnp.int32, (EXPERTS, PROMPT), 0)
    named = (ids_ref[0:1, :] == names) | (ids_ref[1:2, :] == names)
    first = lax.broadcasted_iota(jnp.int32, (PROMPT, PROMPT), 0)
    second = lax.broadcasted_iota(jnp.int32, (PROMPT, PROMPT), 1)
    before = jnp.where(first < second, 1.0, 0.0).astype(jnp.bfloat16)
    taken = jnp.where(named, 1.0, 0.0)
    slot = jnp.dot(taken.astype(jnp.bfloat16), before, preferred_element_type=jnp.float32)
    slot = jnp.where(named, slot, -1.0).astype(jnp.int32)
    att = att_ref[...]
    place = lax.broadcasted_iota(jnp.int32, (CAP, PROMPT), 0)
    for e in range(EXPERTS):
        chosen = jnp.where(place == slot[e : e + 1, :], 1.0, 0.0).astype(jnp.bfloat16)
        sent = jnp.dot(chosen, att, preferred_element_type=jnp.float32)
        out_ref[e * CAP : (e + 1) * CAP, :] = sent.astype(jnp.bfloat16)


def attend(limit, parts, ids_t):
    vmem = pl.BlockSpec(memory_space=pltpu.VMEM)
    return pl.pallas_call(
        attend_kernel,
        in_specs=[pl.BlockSpec(memory_space=pltpu.SMEM)] + [vmem] * 4,
        out_specs=[vmem, vmem],
        out_shape=[
            jax.ShapeDtypeStruct((PROMPT, WIDTH), jnp.bfloat16),
            jax.ShapeDtypeStruct((EXPERTS * CAP, WIDTH), jnp.bfloat16),
        ],
        scratch_shapes=[pltpu.VMEM((PROMPT, QKV), jnp.bfloat16)],
        compiler_params=pltpu.CompilerParams(vmem_limit_bytes=16 << 20),
        name="attend",
    )(limit, *parts, ids_t)


def norm_kernel(x_ref, gain_ref, out_ref):
    total = jnp.zeros((CAP, 1), jnp.float32)
    for i in range(EXPERTS):
        part = x_ref[i].astype(jnp.float32)
        total = total + jnp.sum(part * part, axis=1, keepdims=True)
    factor = lax.rsqrt(total * (1.0 / D) + 1e-05)
    for i in range(EXPERTS):
        cols = slice(i * WIDTH, (i + 1) * WIDTH)
        out_ref[:, cols] = (x_ref[i].astype(jnp.float32) * factor * gain_ref[:, cols]).astype(
            jnp.bfloat16
        )


def normalise(arrived, gain):
    return pl.pallas_call(
        norm_kernel,
        out_shape=jax.ShapeDtypeStruct((CAP, D), jnp.bfloat16),
        compiler_params=pltpu.CompilerParams(vmem_limit_bytes=32 << 20),
        name="normalise",
    )(arrived, gain)


def ffn_kernel(x0, x1, x2, x3, gate_ref, up_ref, down_ref, o0, o1, o2, o3, xs):
    for j, x in enumerate((x0, x1, x2, x3)):
        xs[j * CAP : (j + 1) * CAP, :] = x[...]
    gate = jnp.dot(xs[...], gate_ref[0], preferred_element_type=jnp.float32)
    up = jnp.dot(xs[...], up_ref[0], preferred_element_type=jnp.float32)
    hidden = (gate / (1.0 + jnp.exp(-gate)) * up).astype(jnp.bfloat16)
    for i in range(EXPERTS):
        part = jnp.dot(
            hidden, down_ref[0, :, i * WIDTH : (i + 1) * WIDTH], preferred_element_type=jnp.float32
        ).astype(jnp.bfloat16)
        for j, o in enumerate((o0, o1, o2, o3)):
            o[i] = part[j * CAP : (j + 1) * CAP]


def ffn(shards, gate, up, down):
    vmem = pl.BlockSpec(memory_space=pltpu.VMEM)
    return pl.pallas_call(
        ffn_kernel,
        in_specs=[vmem] * 7,
        out_specs=[vmem] * SIDE,
        out_shape=[jax.ShapeDtypeStruct((EXPERTS, CAP, WIDTH), jnp.bfloat16)] * SIDE,
        scratch_shapes=[pltpu.VMEM((SIDE * CAP, D), jnp.bfloat16)],
        compiler_params=pltpu.CompilerParams(vmem_limit_bytes=12 << 20),
        cost_estimate=pl.CostEstimate(
            flops=6 * SIDE * CAP * D * FF_DEV,
            transcendentals=SIDE * CAP * FF_DEV,
            bytes_accessed=4 * SIDE * CAP * D,
        ),
        name="ffn",
    )(*shards, gate, up, down)


def shift(value, first, step):
    pairs = []
    for z in range(SIDE):
        for y in range(SIDE):
            for e in range(EXPERTS):
                along_y = (e % 2 == 0) == first
                to_z, to_y = (z, (y + step) % SIDE) if along_y else ((z + step) % SIDE, y)
                pairs.append(((z * SIDE + y) * EXPERTS + e, (to_z * SIDE + to_y) * EXPERTS + e))
    return lax.ppermute(value, ("z", "y", "expert"), pairs)


def tie(*values):
    return lax.optimization_barrier(values)


def add_kernel(*refs):
    *parts, out_ref = refs
    total = parts[0][...].astype(jnp.float32)
    for part in parts[1:]:
        total = total + part[...].astype(jnp.float32)
    out_ref[...] = total.astype(jnp.bfloat16)


def add(*parts):
    shape = parts[0].shape
    block = pl.BlockSpec(memory_space=pltpu.VMEM)
    return pl.pallas_call(
        add_kernel,
        in_specs=[block] * len(parts),
        out_specs=block,
        out_shape=jax.ShapeDtypeStruct(shape, jnp.bfloat16),
        compiler_params=pltpu.CompilerParams(vmem_limit_bytes=4 << 20),
        name="add",
    )(*parts)


def load_kernel(source, target, sem):
    copy = pltpu.make_async_copy(source, target, sem)
    copy.start()
    copy.wait()


def load(weight):
    return pl.pallas_call(
        load_kernel,
        in_specs=[pl.BlockSpec(memory_space=pltpu.HBM)],
        out_specs=pl.BlockSpec(memory_space=pltpu.VMEM),
        out_shape=jax.ShapeDtypeStruct(weight.shape, weight.dtype),
        scratch_shapes=[pltpu.SemaphoreType.DMA],
        compiler_params=pltpu.CompilerParams(vmem_limit_bytes=4 << 20),
        name="load",
    )(weight)


def experts(own, weights):
    low, high = shift(own, True, 1), shift(own, True, -1)
    own_low, own_high = shift(own, False, 1), shift(own, False, -1)
    low, high = tie(low, high)
    across, low_high = shift(low, True, 1), shift(low, False, -1)
    own_low, own_high, low, high, *weights = tie(
        own_low, own_high, low, high, *[load(weight) for weight in weights]
    )
    low_low, high_high = shift(low, False, 1), shift(high, False, -1)
    across, low_high, own_high, high = tie(across, low_high, own_high, high)
    high_low, own_far = shift(high, False, 1), shift(own_high, False, -1)
    low_low, high_high, across = tie(low_low, high_high, across)
    across_low, across_high = shift(across, False, 1), shift(across, False, -1)
    high_low, own_far, low_low, high_high = tie(high_low, own_far, low_low, high_high)
    low_far, high_far = shift(low_low, False, 1), shift(high_high, False, -1)
    own_parts = ffn((own, own_low, own_high, own_far), *weights)
    across_low, across_high, *own_parts = tie(across_low, across_high, *own_parts)
    across_far, own_passed = shift(across_low, False, 1), shift(own_parts[3], False, -1)
    own_behind = shift(own_parts[2], False, 1)
    low_far, high_far, across_far, own_passed = tie(low_far, high_far, across_far, own_passed)
    across_parts = ffn((across, across_low, across_high, across_far), *weights)
    own_ahead = shift(add(own_parts[1], own_passed), False, -1)
    own_behind, high, *across_parts = tie(own_behind, high, *across_parts)
    across_passed = shift(across_parts[3], False, 1)
    high_parts = ffn((high, high_low, high_high, high_far), *weights)
    own_ahead, low, *high_parts = tie(own_ahead, low, *high_parts)
    high_passed = shift(high_parts[3], False, -1)
    low_parts = ffn((low, low_low, low_high, low_far), *weights)
    low_passed = shift(low_parts[3], False, 1)
    own_sum = add(own_parts[0], own_ahead, own_behind)
    across_sum = add(
        across_parts[0],
        shift(add(across_parts[2], across_passed), False, 1),
        shift(across_parts[1], False, -1),
    )
    high_sum = add(
        high_parts[0],
        shift(add(high_parts[1], high_passed), False, -1),
        shift(high_parts[2], False, 1),
    )
    low_sum = add(
        low_parts[0],
        shift(add(low_parts[2], low_passed), False, 1),
        shift(low_parts[1], False, -1),
    )
    passed = shift(across_sum, True, 1)
    return add(own_sum, shift(add(high_sum, passed), True, 1), shift(low_sum, True, -1))


def combine_kernel(att_ref, ret_ref, ids_ref, logits_ref, out_ref):
    names = lax.broadcasted_iota(jnp.int32, (PROMPT, HEAD), 1)
    ids = [ids_ref[:, c : c + 1] for c in range(2)]
    named = (ids[0] == names) | (ids[1] == names)
    first = lax.broadcasted_iota(jnp.int32, (PROMPT, PROMPT), 0)
    second = lax.broadcasted_iota(jnp.int32, (PROMPT, PROMPT), 1)
    before = jnp.where(second < first, 1.0, 0.0).astype(jnp.bfloat16)
    taken = jnp.where(named, 1.0, 0.0).astype(jnp.bfloat16)
    count = jnp.dot(before, taken, preferred_element_type=jnp.float32)
    logits = [logits_ref[:, c : c + 1] for c in range(2)]
    top = jnp.maximum(logits[0], logits[1])
    exps = [jnp.exp(v - top) for v in logits]
    total = exps[0] + exps[1]
    ret = ret_ref[...]
    column = lax.broadcasted_iota(jnp.int32, (PROMPT, EXPERTS * CAP), 1)
    mixed = None
    for c in range(2):
        slot = jnp.sum(jnp.where(ids[c] == names, count, 0.0), axis=1, keepdims=True)
        at = ids[c] * CAP + slot.astype(jnp.int32)
        chosen = jnp.where(column == at, 1.0, 0.0).astype(jnp.bfloat16)
        picked = jnp.dot(chosen, ret, preferred_element_type=jnp.float32)
        term = exps[c] / total * picked
        mixed = term if mixed is None else mixed + term
    out_ref[...] = (att_ref[...].astype(jnp.float32) + mixed).astype(jnp.bfloat16)


def combine(att, returned, ids, logits):
    return pl.pallas_call(
        combine_kernel,
        out_shape=jax.ShapeDtypeStruct((PROMPT, WIDTH), jnp.bfloat16),
        compiler_params=pltpu.CompilerParams(vmem_limit_bytes=32 << 20),
        name="combine",
    )(att, returned, ids, logits)


def fetch_rows(records, pair_blocks):
    z, y = lax.axis_index("z"), lax.axis_index("y")
    y_first = lax.axis_index("expert") % 2 == 0
    low, high = tie(shift(records, True, 1), shift(records, True, -1))
    far0, far1 = tie(shift(low[:1], True, 1), shift(high[1:], True, -1))
    first, second = jnp.where(y_first, y, z), jnp.where(y_first, z, y)
    ahead = jnp.array([0, 0, 1, 1, -1, -1, 2, 2], jnp.int32)
    slot = jnp.array([0, 1, 0, 1, 0, 1, 0, 1], jnp.int32)
    target = (second + ahead) % SIDE
    prompt = jnp.where(y_first, target * SIDE + first, first * SIDE + target)
    wanted = pair_blocks[prompt, slot]
    owner = wanted // 2
    own_z, own_y = owner // SIDE, owner % SIDE
    own_first, own_second = jnp.where(y_first, own_y, own_z), jnp.where(y_first, own_z, own_y)
    away = (own_first - first) % SIDE
    half = wanted % 2
    source = jnp.where(away == 0, half, jnp.where(away == 3, 2 + half, jnp.where(away == 1, 4 + half, 6 + half)))
    sel = jnp.where(own_second == second, source, -1)
    here, up, down, up_far, down_far = pick_blocks(sel, (records, low, high, far0, far1))
    up_got, down_got = tie(shift(up_far, False, 1), shift(down_far, False, -1))
    up = jnp.concatenate([up[:1] + up_got, up[1:]], axis=0)
    down = jnp.concatenate([down[:1], down[1:] + down_got], axis=0)
    return here, shift(up, False, 1), shift(down, False, -1)


def body(
    records,
    pair_blocks,
    lengths,
    norm_gain,
    gate_logits,
    expert_ids,
    gate_weight,
    up_weight,
    down_weight,
):
    dp_index = lax.axis_index("z") * SIDE + lax.axis_index("y")
    limit = lax.dynamic_slice_in_dim(lengths, dp_index, 1, 0)
    parts = [part.reshape(PROMPT, QKV) for part in fetch_rows(records, pair_blocks)]
    att, outgoing = attend(limit, parts, expert_ids.T)
    arrived = lax.all_to_all(
        outgoing.reshape(EXPERTS, CAP, WIDTH), "expert", split_axis=0, concat_axis=0, tiled=True
    )
    normed = normalise(arrived, norm_gain.reshape(1, D))
    summed = experts(normed, (gate_weight, up_weight, down_weight))
    returned = lax.all_to_all(summed, "expert", split_axis=0, concat_axis=0, tiled=True)
    return combine(att, returned.reshape(EXPERTS * CAP, WIDTH), expert_ids, gate_logits)


def solution(mesh):
    fine = Mesh(mesh.devices.reshape(SIDE, SIDE, EXPERTS), ("z", "y", "expert"))
    dp = ("z", "y")
    placed = (
        P(dp, None, "expert"),
        P(),
        P(),
        P(),
        P(dp, None),
        P(dp, None),
        P("expert", None, dp),
        P("expert", None, dp),
        P("expert", dp, None),
    )
    return jax.shard_map(
        body, mesh=fine, in_specs=placed, out_specs=P(dp, "expert"), check_vma=False
    )
```

```python
import math

import jax
import jax.numpy as jnp
from jax import lax
from jax.experimental import pallas as pl
from jax.experimental.pallas import tpu as pltpu
from jax.sharding import Mesh
from jax.sharding import PartitionSpec as P

HEAD = 128
GROUP = 6
BLOCK = 128
PROMPT = 256
EXPERTS = 8
CAP = 80
WIDTH = 768
D = 6144
FF_DEV = 512
N_DP = 16
SIDE = 4
QKV = 1024


def pick_kernel(sel_ref, own, low, high, far0, far1, here, up, down, up_far, down_far):
    sources = [own.at[0], own.at[1], low.at[0], low.at[1], high.at[0], high.at[1], far0.at[0], far1.at[0]]
    targets = [here.at[0], here.at[1], up.at[0], up.at[1], down.at[0], down.at[1], up_far.at[0], down_far.at[0]]
    for i, target in enumerate(targets):
        for k, source in enumerate(sources):

            @pl.when(sel_ref[i] == k)
            def _():
                target[...] = source[...]

        @pl.when(sel_ref[i] < 0)
        def _():
            target[...] = jnp.zeros_like(target)


def pick_blocks(sel, blocks):
    vmem = pl.BlockSpec(memory_space=pltpu.VMEM)
    return pl.pallas_call(
        pick_kernel,
        in_specs=[pl.BlockSpec(memory_space=pltpu.SMEM)] + [vmem] * 5,
        out_specs=[vmem] * 5,
        out_shape=[
            jax.ShapeDtypeStruct((n, BLOCK, QKV), jnp.bfloat16) for n in (2, 2, 2, 1, 1)
        ],
        compiler_params=pltpu.CompilerParams(vmem_limit_bytes=16 << 20),
        name="pick_blocks",
    )(sel, *blocks)


def attend_kernel(len_ref, here_ref, low_ref, high_ref, ids_ref, att_ref, out_ref, rows_ref):
    limit = len_ref[0]
    rows_ref[...] = here_ref[...] + low_ref[...] + high_ref[...]
    scale = 1.0 / math.sqrt(HEAD)
    for top in (0, BLOCK):
        span = top + BLOCK
        keys = rows_ref[0:span, GROUP * HEAD : (GROUP + 1) * HEAD]
        values = rows_ref[0:span, (GROUP + 1) * HEAD : (GROUP + 2) * HEAD]
        row = lax.broadcasted_iota(jnp.int32, (BLOCK, span), 0) + top
        col = lax.broadcasted_iota(jnp.int32, (BLOCK, span), 1)
        allowed = (col <= row) & (col < limit)
        for g in range(GROUP):
            query = rows_ref[top:span, g * HEAD : (g + 1) * HEAD]
            scores = lax.dot_general(
                query, keys, (((1,), (1,)), ((), ())), preferred_element_type=jnp.float32
            )
            scores = jnp.where(allowed, scores * scale, -jnp.inf)
            exponent = jnp.exp(scores - jnp.max(scores, axis=1, keepdims=True))
            probs = (exponent / jnp.sum(exponent, axis=1, keepdims=True)).astype(jnp.bfloat16)
            mixed = jnp.dot(probs, values, preferred_element_type=jnp.float32)
            att_ref[top:span, g * HEAD : (g + 1) * HEAD] = mixed.astype(jnp.bfloat16)
    names = lax.broadcasted_iota(jnp.int32, (EXPERTS, PROMPT), 0)
    named = (ids_ref[0:1, :] == names) | (ids_ref[1:2, :] == names)
    first = lax.broadcasted_iota(jnp.int32, (PROMPT, PROMPT), 0)
    second = lax.broadcasted_iota(jnp.int32, (PROMPT, PROMPT), 1)
    before = jnp.where(first < second, 1.0, 0.0).astype(jnp.bfloat16)
    taken = jnp.where(named, 1.0, 0.0)
    slot = jnp.dot(taken.astype(jnp.bfloat16), before, preferred_element_type=jnp.float32)
    slot = jnp.where(named, slot, -1.0).astype(jnp.int32)
    att = att_ref[...]
    place = lax.broadcasted_iota(jnp.int32, (CAP, PROMPT), 0)
    for e in range(EXPERTS):
        chosen = jnp.where(place == slot[e : e + 1, :], 1.0, 0.0).astype(jnp.bfloat16)
        sent = jnp.dot(chosen, att, preferred_element_type=jnp.float32)
        out_ref[e * CAP : (e + 1) * CAP, :] = sent.astype(jnp.bfloat16)


def attend(limit, parts, ids_t):
    vmem = pl.BlockSpec(memory_space=pltpu.VMEM)
    return pl.pallas_call(
        attend_kernel,
        in_specs=[pl.BlockSpec(memory_space=pltpu.SMEM)] + [vmem] * 4,
        out_specs=[vmem, vmem],
        out_shape=[
            jax.ShapeDtypeStruct((PROMPT, WIDTH), jnp.bfloat16),
            jax.ShapeDtypeStruct((EXPERTS * CAP, WIDTH), jnp.bfloat16),
        ],
        scratch_shapes=[pltpu.VMEM((PROMPT, QKV), jnp.bfloat16)],
        compiler_params=pltpu.CompilerParams(vmem_limit_bytes=16 << 20),
        name="attend",
    )(limit, *parts, ids_t)


def norm_kernel(x_ref, gain_ref, out_ref):
    total = jnp.zeros((CAP, 1), jnp.float32)
    for i in range(EXPERTS):
        part = x_ref[i].astype(jnp.float32)
        total = total + jnp.sum(part * part, axis=1, keepdims=True)
    factor = lax.rsqrt(total * (1.0 / D) + 1e-05)
    for i in range(EXPERTS):
        cols = slice(i * WIDTH, (i + 1) * WIDTH)
        out_ref[:, cols] = (x_ref[i].astype(jnp.float32) * factor * gain_ref[:, cols]).astype(
            jnp.bfloat16
        )


def normalise(arrived, gain):
    return pl.pallas_call(
        norm_kernel,
        out_shape=jax.ShapeDtypeStruct((CAP, D), jnp.bfloat16),
        compiler_params=pltpu.CompilerParams(vmem_limit_bytes=32 << 20),
        name="normalise",
    )(arrived, gain)


def ffn_kernel(x0, x1, x2, x3, gate_ref, up_ref, down_ref, o0, o1, o2, o3, xs):
    for j, x in enumerate((x0, x1, x2, x3)):
        xs[j * CAP : (j + 1) * CAP, :] = x[...]
    gate = jnp.dot(xs[...], gate_ref[0], preferred_element_type=jnp.float32)
    up = jnp.dot(xs[...], up_ref[0], preferred_element_type=jnp.float32)
    hidden = (gate / (1.0 + jnp.exp(-gate)) * up).astype(jnp.bfloat16)
    for i in range(EXPERTS):
        part = jnp.dot(
            hidden, down_ref[0, :, i * WIDTH : (i + 1) * WIDTH], preferred_element_type=jnp.float32
        ).astype(jnp.bfloat16)
        for j, o in enumerate((o0, o1, o2, o3)):
            o[i] = part[j * CAP : (j + 1) * CAP]


def ffn(shards, gate, up, down):
    vmem = pl.BlockSpec(memory_space=pltpu.VMEM)
    return pl.pallas_call(
        ffn_kernel,
        in_specs=[vmem] * 7,
        out_specs=[vmem] * SIDE,
        out_shape=[jax.ShapeDtypeStruct((EXPERTS, CAP, WIDTH), jnp.bfloat16)] * SIDE,
        scratch_shapes=[pltpu.VMEM((SIDE * CAP, D), jnp.bfloat16)],
        compiler_params=pltpu.CompilerParams(vmem_limit_bytes=12 << 20),
        cost_estimate=pl.CostEstimate(
            flops=6 * SIDE * CAP * D * FF_DEV,
            transcendentals=SIDE * CAP * FF_DEV,
            bytes_accessed=4 * SIDE * CAP * D,
        ),
        name="ffn",
    )(*shards, gate, up, down)


def shift(value, first, step):
    pairs = []
    for z in range(SIDE):
        for y in range(SIDE):
            for e in range(EXPERTS):
                along_y = (e % 2 == 0) == first
                to_z, to_y = (z, (y + step) % SIDE) if along_y else ((z + step) % SIDE, y)
                pairs.append(((z * SIDE + y) * EXPERTS + e, (to_z * SIDE + to_y) * EXPERTS + e))
    return lax.ppermute(value, ("z", "y", "expert"), pairs)


def tie(*values):
    return lax.optimization_barrier(values)


def add_kernel(*refs):
    *parts, out_ref = refs
    total = parts[0][...].astype(jnp.float32)
    for part in parts[1:]:
        total = total + part[...].astype(jnp.float32)
    out_ref[...] = total.astype(jnp.bfloat16)


def add(*parts):
    shape = parts[0].shape
    block = pl.BlockSpec(memory_space=pltpu.VMEM)
    return pl.pallas_call(
        add_kernel,
        in_specs=[block] * len(parts),
        out_specs=block,
        out_shape=jax.ShapeDtypeStruct(shape, jnp.bfloat16),
        compiler_params=pltpu.CompilerParams(vmem_limit_bytes=4 << 20),
        name="add",
    )(*parts)


def load_kernel(source, target, sem):
    copy = pltpu.make_async_copy(source, target, sem)
    copy.start()
    copy.wait()


def load(weight):
    return pl.pallas_call(
        load_kernel,
        in_specs=[pl.BlockSpec(memory_space=pltpu.HBM)],
        out_specs=pl.BlockSpec(memory_space=pltpu.VMEM),
        out_shape=jax.ShapeDtypeStruct(weight.shape, weight.dtype),
        scratch_shapes=[pltpu.SemaphoreType.DMA],
        compiler_params=pltpu.CompilerParams(vmem_limit_bytes=4 << 20),
        name="load",
    )(weight)


def experts(own, weights):
    gate, up, down = weights
    low, high = shift(own, True, 1), shift(own, True, -1)
    own_low, own_high = shift(own, False, 1), shift(own, False, -1)
    low, high, gate = tie(low, high, load(gate))
    across, low_high = shift(low, True, 1), shift(low, False, -1)
    own_low, own_high, low, high, up = tie(own_low, own_high, low, high, load(up))
    low_low, high_high = shift(low, False, 1), shift(high, False, -1)
    across, low_high, own_high, high, down = tie(across, low_high, own_high, high, load(down))
    weights = gate, up, down
    high_low, own_far = shift(high, False, 1), shift(own_high, False, -1)
    low_low, high_high = tie(low_low, high_high)
    low_far, high_far = shift(low_low, False, 1), shift(high_high, False, -1)
    high_low, own_far, across = tie(high_low, own_far, across)
    across_low, across_high = shift(across, False, 1), shift(across, False, -1)
    own_parts = ffn((own, own_low, own_high, own_far), *weights)
    low_far, high_far, *own_parts = tie(low_far, high_far, *own_parts)
    own_passed, own_behind = shift(own_parts[3], False, -1), shift(own_parts[2], False, 1)
    low_parts = ffn((low, low_low, low_high, low_far), *weights)
    across_low, across_high, *low_parts = tie(across_low, across_high, *low_parts)
    across_far = shift(across_low, False, 1)
    low_passed = shift(low_parts[3], False, -1)
    high_parts = ffn((high, high_low, high_high, high_far), *weights)
    high_passed = shift(high_parts[3], False, 1)
    own_passed, own_behind, across_far = tie(own_passed, own_behind, across_far)
    own_ahead = shift(add(own_parts[1], own_passed), False, -1)
    across_parts = ffn((across, across_low, across_high, across_far), *weights)
    low_passed, high_passed, *across_parts = tie(low_passed, high_passed, *across_parts)
    across_passed, across_behind = (
        shift(across_parts[3], False, 1),
        shift(across_parts[1], False, -1),
    )
    low_behind, high_behind = shift(low_parts[2], False, 1), shift(high_parts[1], False, -1)
    across_passed, own_ahead = tie(across_passed, own_ahead)
    low_ahead = shift(add(low_parts[1], low_passed), False, -1)
    high_ahead = shift(add(high_parts[2], high_passed), False, 1)
    across_ahead = shift(add(across_parts[2], across_passed), False, 1)
    own_sum = add(own_parts[0], own_ahead, own_behind)
    low_sum = add(low_parts[0], low_ahead, low_behind)
    high_sum = add(high_parts[0], high_ahead, high_behind)
    across_sum = add(across_parts[0], across_ahead, across_behind)
    passed = shift(across_sum, True, -1)
    own_sum = add(own_sum, shift(high_sum, True, 1))
    return add(own_sum, shift(add(low_sum, passed), True, -1))


def combine_kernel(att_ref, ret_ref, ids_ref, logits_ref, out_ref):
    names = lax.broadcasted_iota(jnp.int32, (PROMPT, HEAD), 1)
    ids = [ids_ref[:, c : c + 1] for c in range(2)]
    named = (ids[0] == names) | (ids[1] == names)
    first = lax.broadcasted_iota(jnp.int32, (PROMPT, PROMPT), 0)
    second = lax.broadcasted_iota(jnp.int32, (PROMPT, PROMPT), 1)
    before = jnp.where(second < first, 1.0, 0.0).astype(jnp.bfloat16)
    taken = jnp.where(named, 1.0, 0.0).astype(jnp.bfloat16)
    count = jnp.dot(before, taken, preferred_element_type=jnp.float32)
    logits = [logits_ref[:, c : c + 1] for c in range(2)]
    top = jnp.maximum(logits[0], logits[1])
    exps = [jnp.exp(v - top) for v in logits]
    total = exps[0] + exps[1]
    ret = ret_ref[...]
    column = lax.broadcasted_iota(jnp.int32, (PROMPT, EXPERTS * CAP), 1)
    mixed = None
    for c in range(2):
        slot = jnp.sum(jnp.where(ids[c] == names, count, 0.0), axis=1, keepdims=True)
        at = ids[c] * CAP + slot.astype(jnp.int32)
        chosen = jnp.where(column == at, 1.0, 0.0).astype(jnp.bfloat16)
        picked = jnp.dot(chosen, ret, preferred_element_type=jnp.float32)
        term = exps[c] / total * picked
        mixed = term if mixed is None else mixed + term
    out_ref[...] = (att_ref[...].astype(jnp.float32) + mixed).astype(jnp.bfloat16)


def combine(att, returned, ids, logits):
    return pl.pallas_call(
        combine_kernel,
        out_shape=jax.ShapeDtypeStruct((PROMPT, WIDTH), jnp.bfloat16),
        compiler_params=pltpu.CompilerParams(vmem_limit_bytes=32 << 20),
        name="combine",
    )(att, returned, ids, logits)


def fetch_rows(records, pair_blocks):
    z, y = lax.axis_index("z"), lax.axis_index("y")
    y_first = lax.axis_index("expert") % 2 == 0
    low, high = tie(shift(records, True, 1), shift(records, True, -1))
    far0, far1 = tie(shift(low[:1], True, 1), shift(high[1:], True, -1))
    first, second = jnp.where(y_first, y, z), jnp.where(y_first, z, y)
    ahead = jnp.array([0, 0, 1, 1, -1, -1, 2, 2], jnp.int32)
    slot = jnp.array([0, 1, 0, 1, 0, 1, 0, 1], jnp.int32)
    target = (second + ahead) % SIDE
    prompt = jnp.where(y_first, target * SIDE + first, first * SIDE + target)
    wanted = pair_blocks[prompt, slot]
    owner = wanted // 2
    own_z, own_y = owner // SIDE, owner % SIDE
    own_first, own_second = jnp.where(y_first, own_y, own_z), jnp.where(y_first, own_z, own_y)
    away = (own_first - first) % SIDE
    half = wanted % 2
    source = jnp.where(away == 0, half, jnp.where(away == 3, 2 + half, jnp.where(away == 1, 4 + half, 6 + half)))
    sel = jnp.where(own_second == second, source, -1)
    here, up, down, up_far, down_far = pick_blocks(sel, (records, low, high, far0, far1))
    up_got, down_got = tie(shift(up_far, False, 1), shift(down_far, False, -1))
    up = jnp.concatenate([up[:1] + up_got, up[1:]], axis=0)
    down = jnp.concatenate([down[:1], down[1:] + down_got], axis=0)
    return here, shift(up, False, 1), shift(down, False, -1)


def body(
    records,
    pair_blocks,
    lengths,
    norm_gain,
    gate_logits,
    expert_ids,
    gate_weight,
    up_weight,
    down_weight,
):
    dp_index = lax.axis_index("z") * SIDE + lax.axis_index("y")
    limit = lax.dynamic_slice_in_dim(lengths, dp_index, 1, 0)
    parts = [part.reshape(PROMPT, QKV) for part in fetch_rows(records, pair_blocks)]
    att, outgoing = attend(limit, parts, expert_ids.T)
    arrived = lax.all_to_all(
        outgoing.reshape(EXPERTS, CAP, WIDTH), "expert", split_axis=0, concat_axis=0, tiled=True
    )
    normed = normalise(arrived, norm_gain.reshape(1, D))
    summed = experts(normed, (gate_weight, up_weight, down_weight))
    returned = lax.all_to_all(summed, "expert", split_axis=0, concat_axis=0, tiled=True)
    return combine(att, returned.reshape(EXPERTS * CAP, WIDTH), expert_ids, gate_logits)


def solution(mesh):
    fine = Mesh(mesh.devices.reshape(SIDE, SIDE, EXPERTS), ("z", "y", "expert"))
    dp = ("z", "y")
    placed = (
        P(dp, None, "expert"),
        P(),
        P(),
        P(),
        P(dp, None),
        P(dp, None),
        P("expert", None, dp),
        P("expert", None, dp),
        P("expert", dp, None),
    )
    return jax.shard_map(
        body, mesh=fine, in_specs=placed, out_specs=P(dp, "expert"), check_vma=False
    )
```

```python
import math

import jax
import jax.numpy as jnp
from jax import lax
from jax.experimental import pallas as pl
from jax.experimental.pallas import tpu as pltpu
from jax.sharding import Mesh
from jax.sharding import PartitionSpec as P

HEAD = 128
GROUP = 6
BLOCK = 128
PROMPT = 256
EXPERTS = 8
CAP = 80
WIDTH = 768
D = 6144
FF_DEV = 512
N_DP = 16
SIDE = 4
QKV = 1024


def pick_kernel(sel_ref, own, low, high, far0, far1, here, up, down, up_far, down_far):
    sources = [own.at[0], own.at[1], low.at[0], low.at[1], high.at[0], high.at[1], far0.at[0], far1.at[0]]
    targets = [here.at[0], here.at[1], up.at[0], up.at[1], down.at[0], down.at[1], up_far.at[0], down_far.at[0]]
    for i, target in enumerate(targets):
        for k, source in enumerate(sources):

            @pl.when(sel_ref[i] == k)
            def _():
                target[...] = source[...]

        @pl.when(sel_ref[i] < 0)
        def _():
            target[...] = jnp.zeros_like(target)


def pick_blocks(sel, blocks):
    vmem = pl.BlockSpec(memory_space=pltpu.VMEM)
    return pl.pallas_call(
        pick_kernel,
        in_specs=[pl.BlockSpec(memory_space=pltpu.SMEM)] + [vmem] * 5,
        out_specs=[vmem] * 5,
        out_shape=[
            jax.ShapeDtypeStruct((n, BLOCK, QKV), jnp.bfloat16) for n in (2, 2, 2, 1, 1)
        ],
        compiler_params=pltpu.CompilerParams(vmem_limit_bytes=16 << 20),
        name="pick_blocks",
    )(sel, *blocks)


def attend_kernel(len_ref, here_ref, low_ref, high_ref, ids_ref, att_ref, out_ref, rows_ref):
    limit = len_ref[0]
    rows_ref[...] = here_ref[...] + low_ref[...] + high_ref[...]
    scale = 1.0 / math.sqrt(HEAD)
    for top in (0, BLOCK):
        span = top + BLOCK
        keys = rows_ref[0:span, GROUP * HEAD : (GROUP + 1) * HEAD]
        values = rows_ref[0:span, (GROUP + 1) * HEAD : (GROUP + 2) * HEAD]
        row = lax.broadcasted_iota(jnp.int32, (BLOCK, span), 0) + top
        col = lax.broadcasted_iota(jnp.int32, (BLOCK, span), 1)
        allowed = (col <= row) & (col < limit)
        for g in range(GROUP):
            query = rows_ref[top:span, g * HEAD : (g + 1) * HEAD]
            scores = lax.dot_general(
                query, keys, (((1,), (1,)), ((), ())), preferred_element_type=jnp.float32
            )
            scores = jnp.where(allowed, scores * scale, -jnp.inf)
            exponent = jnp.exp(scores - jnp.max(scores, axis=1, keepdims=True))
            probs = (exponent / jnp.sum(exponent, axis=1, keepdims=True)).astype(jnp.bfloat16)
            mixed = jnp.dot(probs, values, preferred_element_type=jnp.float32)
            att_ref[top:span, g * HEAD : (g + 1) * HEAD] = mixed.astype(jnp.bfloat16)
    names = lax.broadcasted_iota(jnp.int32, (EXPERTS, PROMPT), 0)
    named = (ids_ref[0:1, :] == names) | (ids_ref[1:2, :] == names)
    first = lax.broadcasted_iota(jnp.int32, (PROMPT, PROMPT), 0)
    second = lax.broadcasted_iota(jnp.int32, (PROMPT, PROMPT), 1)
    before = jnp.where(first < second, 1.0, 0.0).astype(jnp.bfloat16)
    taken = jnp.where(named, 1.0, 0.0)
    slot = jnp.dot(taken.astype(jnp.bfloat16), before, preferred_element_type=jnp.float32)
    slot = jnp.where(named, slot, -1.0).astype(jnp.int32)
    att = att_ref[...]
    place = lax.broadcasted_iota(jnp.int32, (CAP, PROMPT), 0)
    for e in range(EXPERTS):
        chosen = jnp.where(place == slot[e : e + 1, :], 1.0, 0.0).astype(jnp.bfloat16)
        sent = jnp.dot(chosen, att, preferred_element_type=jnp.float32)
        out_ref[e * CAP : (e + 1) * CAP, :] = sent.astype(jnp.bfloat16)


def attend(limit, parts, ids_t):
    vmem = pl.BlockSpec(memory_space=pltpu.VMEM)
    return pl.pallas_call(
        attend_kernel,
        in_specs=[pl.BlockSpec(memory_space=pltpu.SMEM)] + [vmem] * 4,
        out_specs=[vmem, vmem],
        out_shape=[
            jax.ShapeDtypeStruct((PROMPT, WIDTH), jnp.bfloat16),
            jax.ShapeDtypeStruct((EXPERTS * CAP, WIDTH), jnp.bfloat16),
        ],
        scratch_shapes=[pltpu.VMEM((PROMPT, QKV), jnp.bfloat16)],
        compiler_params=pltpu.CompilerParams(vmem_limit_bytes=16 << 20),
        name="attend",
    )(limit, *parts, ids_t)


def norm_kernel(x_ref, gain_ref, out_ref):
    total = jnp.zeros((CAP, 1), jnp.float32)
    for i in range(EXPERTS):
        part = x_ref[i].astype(jnp.float32)
        total = total + jnp.sum(part * part, axis=1, keepdims=True)
    factor = lax.rsqrt(total * (1.0 / D) + 1e-05)
    for i in range(EXPERTS):
        cols = slice(i * WIDTH, (i + 1) * WIDTH)
        out_ref[:, cols] = (x_ref[i].astype(jnp.float32) * factor * gain_ref[:, cols]).astype(
            jnp.bfloat16
        )


def normalise(arrived, gain):
    return pl.pallas_call(
        norm_kernel,
        out_shape=jax.ShapeDtypeStruct((CAP, D), jnp.bfloat16),
        compiler_params=pltpu.CompilerParams(vmem_limit_bytes=32 << 20),
        name="normalise",
    )(arrived, gain)


def ffn_kernel(x0, x1, x2, x3, gate_ref, up_ref, down_ref, o0, o1, o2, o3, xs):
    for j, x in enumerate((x0, x1, x2, x3)):
        xs[j * CAP : (j + 1) * CAP, :] = x[...]
    gate = jnp.dot(xs[...], gate_ref[0], preferred_element_type=jnp.float32)
    up = jnp.dot(xs[...], up_ref[0], preferred_element_type=jnp.float32)
    hidden = (gate / (1.0 + jnp.exp(-gate)) * up).astype(jnp.bfloat16)
    for i in range(EXPERTS):
        part = jnp.dot(
            hidden, down_ref[0, :, i * WIDTH : (i + 1) * WIDTH], preferred_element_type=jnp.float32
        ).astype(jnp.bfloat16)
        for j, o in enumerate((o0, o1, o2, o3)):
            o[i] = part[j * CAP : (j + 1) * CAP]


def ffn(shards, gate, up, down):
    vmem = pl.BlockSpec(memory_space=pltpu.VMEM)
    return pl.pallas_call(
        ffn_kernel,
        in_specs=[vmem] * 7,
        out_specs=[vmem] * SIDE,
        out_shape=[jax.ShapeDtypeStruct((EXPERTS, CAP, WIDTH), jnp.bfloat16)] * SIDE,
        scratch_shapes=[pltpu.VMEM((SIDE * CAP, D), jnp.bfloat16)],
        compiler_params=pltpu.CompilerParams(vmem_limit_bytes=12 << 20),
        cost_estimate=pl.CostEstimate(
            flops=6 * SIDE * CAP * D * FF_DEV,
            transcendentals=SIDE * CAP * FF_DEV,
            bytes_accessed=4 * SIDE * CAP * D,
        ),
        name="ffn",
    )(*shards, gate, up, down)


def shift(value, first, step):
    pairs = []
    for z in range(SIDE):
        for y in range(SIDE):
            for e in range(EXPERTS):
                along_y = (e % 2 == 0) == first
                to_z, to_y = (z, (y + step) % SIDE) if along_y else ((z + step) % SIDE, y)
                pairs.append(((z * SIDE + y) * EXPERTS + e, (to_z * SIDE + to_y) * EXPERTS + e))
    return lax.ppermute(value, ("z", "y", "expert"), pairs)


def tie(*values):
    return lax.optimization_barrier(values)


def add_kernel(*refs):
    *parts, out_ref = refs
    total = parts[0][...].astype(jnp.float32)
    for part in parts[1:]:
        total = total + part[...].astype(jnp.float32)
    out_ref[...] = total.astype(jnp.bfloat16)


def add(*parts):
    shape = parts[0].shape
    block = pl.BlockSpec(memory_space=pltpu.VMEM)
    return pl.pallas_call(
        add_kernel,
        in_specs=[block] * len(parts),
        out_specs=block,
        out_shape=jax.ShapeDtypeStruct(shape, jnp.bfloat16),
        compiler_params=pltpu.CompilerParams(vmem_limit_bytes=4 << 20),
        name="add",
    )(*parts)


def load_kernel(source, target, sem):
    copy = pltpu.make_async_copy(source, target, sem)
    copy.start()
    copy.wait()


def load(weight):
    return pl.pallas_call(
        load_kernel,
        in_specs=[pl.BlockSpec(memory_space=pltpu.HBM)],
        out_specs=pl.BlockSpec(memory_space=pltpu.VMEM),
        out_shape=jax.ShapeDtypeStruct(weight.shape, weight.dtype),
        scratch_shapes=[pltpu.SemaphoreType.DMA],
        compiler_params=pltpu.CompilerParams(vmem_limit_bytes=4 << 20),
        name="load",
    )(weight)


def experts(own, weights):
    gate, up, down = weights
    low, high = shift(own, True, 1), shift(own, True, -1)
    own_low, own_high = shift(own, False, 1), shift(own, False, -1)
    low, high, gate = tie(low, high, load(gate))
    across, low_high = shift(low, True, 1), shift(low, False, -1)
    own_low, own_high, low, high, up = tie(own_low, own_high, low, high, load(up))
    low_low, high_high = shift(low, False, 1), shift(high, False, -1)
    across, low_high, own_high, high, down = tie(across, low_high, own_high, high, load(down))
    weights = gate, up, down
    high_low, own_far = shift(high, False, 1), shift(own_high, False, -1)
    low_low, high_high = tie(low_low, high_high)
    low_far, high_far = shift(low_low, False, 1), shift(high_high, False, -1)
    high_low, own_far, across = tie(high_low, own_far, across)
    across_low, across_high = shift(across, False, 1), shift(across, False, -1)
    own_parts = ffn((own, own_low, own_high, own_far), *weights)
    low_far, high_far, *own_parts = tie(low_far, high_far, *own_parts)
    own_passed, own_behind = shift(own_parts[3], False, -1), shift(own_parts[2], False, 1)
    high_parts = ffn((high, high_low, high_high, high_far), *weights)
    across_low, across_high, *high_parts = tie(across_low, across_high, *high_parts)
    across_far = shift(across_high, False, -1)
    high_passed = shift(high_parts[3], False, 1)
    low_parts = ffn((low, low_low, low_high, low_far), *weights)
    low_passed, low_behind = shift(low_parts[3], False, -1), shift(low_parts[2], False, 1)
    own_passed, own_behind, across_far, high_passed = tie(
        own_passed, own_behind, across_far, high_passed
    )
    own_ahead = shift(add(own_parts[1], own_passed), False, -1)
    high_ahead = shift(add(high_parts[2], high_passed), False, 1)
    across_parts = ffn((across, across_low, across_high, across_far), *weights)
    low_passed, low_behind, own_ahead, high_ahead, *across_parts = tie(
        low_passed, low_behind, own_ahead, high_ahead, *across_parts
    )
    across_passed = shift(across_parts[3], False, 1)
    low_ahead = shift(add(low_parts[1], low_passed), False, -1)
    across_passed, low_ahead, *across_parts = tie(across_passed, low_ahead, *across_parts)
    across_ahead = shift(add(across_parts[2], across_passed), False, 1)
    across_behind = shift(across_parts[1], False, -1)
    across_sum = add(across_parts[0], across_ahead, across_behind)
    across_sum, to_low = tie(across_sum, high_parts[1])
    high_behind = shift(to_low, False, -1)
    own_sum = add(own_parts[0], own_ahead, own_behind)
    low_sum = add(low_parts[0], low_ahead, low_behind)
    high_sum = add(high_parts[0], high_ahead, high_behind)
    passed = shift(across_sum, True, 1)
    own_sum = add(own_sum, shift(low_sum, True, -1))
    return add(own_sum, shift(add(high_sum, passed), True, 1))


def combine_kernel(att_ref, ret_ref, ids_ref, logits_ref, out_ref):
    names = lax.broadcasted_iota(jnp.int32, (PROMPT, HEAD), 1)
    ids = [ids_ref[:, c : c + 1] for c in range(2)]
    named = (ids[0] == names) | (ids[1] == names)
    first = lax.broadcasted_iota(jnp.int32, (PROMPT, PROMPT), 0)
    second = lax.broadcasted_iota(jnp.int32, (PROMPT, PROMPT), 1)
    before = jnp.where(second < first, 1.0, 0.0).astype(jnp.bfloat16)
    taken = jnp.where(named, 1.0, 0.0).astype(jnp.bfloat16)
    count = jnp.dot(before, taken, preferred_element_type=jnp.float32)
    logits = [logits_ref[:, c : c + 1] for c in range(2)]
    top = jnp.maximum(logits[0], logits[1])
    exps = [jnp.exp(v - top) for v in logits]
    total = exps[0] + exps[1]
    ret = ret_ref[...]
    column = lax.broadcasted_iota(jnp.int32, (PROMPT, EXPERTS * CAP), 1)
    mixed = None
    for c in range(2):
        slot = jnp.sum(jnp.where(ids[c] == names, count, 0.0), axis=1, keepdims=True)
        at = ids[c] * CAP + slot.astype(jnp.int32)
        chosen = jnp.where(column == at, 1.0, 0.0).astype(jnp.bfloat16)
        picked = jnp.dot(chosen, ret, preferred_element_type=jnp.float32)
        term = exps[c] / total * picked
        mixed = term if mixed is None else mixed + term
    out_ref[...] = (att_ref[...].astype(jnp.float32) + mixed).astype(jnp.bfloat16)


def combine(att, returned, ids, logits):
    return pl.pallas_call(
        combine_kernel,
        out_shape=jax.ShapeDtypeStruct((PROMPT, WIDTH), jnp.bfloat16),
        compiler_params=pltpu.CompilerParams(vmem_limit_bytes=32 << 20),
        name="combine",
    )(att, returned, ids, logits)


def fetch_rows(records, pair_blocks):
    z, y = lax.axis_index("z"), lax.axis_index("y")
    y_first = lax.axis_index("expert") % 2 == 0
    low, high = tie(shift(records, True, 1), shift(records, True, -1))
    far0, far1 = tie(shift(low[:1], True, 1), shift(high[1:], True, -1))
    first, second = jnp.where(y_first, y, z), jnp.where(y_first, z, y)
    ahead = jnp.array([0, 0, 1, 1, -1, -1, 2, 2], jnp.int32)
    slot = jnp.array([0, 1, 0, 1, 0, 1, 0, 1], jnp.int32)
    target = (second + ahead) % SIDE
    prompt = jnp.where(y_first, target * SIDE + first, first * SIDE + target)
    wanted = pair_blocks[prompt, slot]
    owner = wanted // 2
    own_z, own_y = owner // SIDE, owner % SIDE
    own_first, own_second = jnp.where(y_first, own_y, own_z), jnp.where(y_first, own_z, own_y)
    away = (own_first - first) % SIDE
    half = wanted % 2
    source = jnp.where(away == 0, half, jnp.where(away == 3, 2 + half, jnp.where(away == 1, 4 + half, 6 + half)))
    sel = jnp.where(own_second == second, source, -1)
    here, up, down, up_far, down_far = pick_blocks(sel, (records, low, high, far0, far1))
    up_got, down_got = tie(shift(up_far, False, 1), shift(down_far, False, -1))
    up = jnp.concatenate([up[:1] + up_got, up[1:]], axis=0)
    down = jnp.concatenate([down[:1], down[1:] + down_got], axis=0)
    return here, shift(up, False, 1), shift(down, False, -1)


def body(
    records,
    pair_blocks,
    lengths,
    norm_gain,
    gate_logits,
    expert_ids,
    gate_weight,
    up_weight,
    down_weight,
):
    dp_index = lax.axis_index("z") * SIDE + lax.axis_index("y")
    limit = lax.dynamic_slice_in_dim(lengths, dp_index, 1, 0)
    parts = [part.reshape(PROMPT, QKV) for part in fetch_rows(records, pair_blocks)]
    att, outgoing = attend(limit, parts, expert_ids.T)
    arrived = lax.all_to_all(
        outgoing.reshape(EXPERTS, CAP, WIDTH), "expert", split_axis=0, concat_axis=0, tiled=True
    )
    normed = normalise(arrived, norm_gain.reshape(1, D))
    summed = experts(normed, (gate_weight, up_weight, down_weight))
    returned = lax.all_to_all(summed, "expert", split_axis=0, concat_axis=0, tiled=True)
    return combine(att, returned.reshape(EXPERTS * CAP, WIDTH), expert_ids, gate_logits)


def solution(mesh):
    fine = Mesh(mesh.devices.reshape(SIDE, SIDE, EXPERTS), ("z", "y", "expert"))
    dp = ("z", "y")
    placed = (
        P(dp, None, "expert"),
        P(),
        P(),
        P(),
        P(dp, None),
        P(dp, None),
        P("expert", None, dp),
        P("expert", None, dp),
        P("expert", dp, None),
    )
    return jax.shard_map(
        body, mesh=fine, in_specs=placed, out_specs=P(dp, "expert"), check_vma=False
    )
```

```python
import math

import jax
import jax.numpy as jnp
from jax import lax
from jax.experimental import pallas as pl
from jax.experimental.pallas import tpu as pltpu
from jax.sharding import Mesh
from jax.sharding import PartitionSpec as P

HEAD = 128
GROUP = 6
BLOCK = 128
PROMPT = 256
EXPERTS = 8
CAP = 80
WIDTH = 768
D = 6144
FF_DEV = 512
N_DP = 16
SIDE = 4
QKV = 1024


def pick_kernel(sel_ref, own, low, high, far0, far1, here, up, down, up_far, down_far):
    sources = [own.at[0], own.at[1], low.at[0], low.at[1], high.at[0], high.at[1], far0.at[0], far1.at[0]]
    targets = [here.at[0], here.at[1], up.at[0], up.at[1], down.at[0], down.at[1], up_far.at[0], down_far.at[0]]
    for i, target in enumerate(targets):
        for k, source in enumerate(sources):

            @pl.when(sel_ref[i] == k)
            def _():
                target[...] = source[...]

        @pl.when(sel_ref[i] < 0)
        def _():
            target[...] = jnp.zeros_like(target)


def pick_blocks(sel, blocks):
    vmem = pl.BlockSpec(memory_space=pltpu.VMEM)
    return pl.pallas_call(
        pick_kernel,
        in_specs=[pl.BlockSpec(memory_space=pltpu.SMEM)] + [vmem] * 5,
        out_specs=[vmem] * 5,
        out_shape=[
            jax.ShapeDtypeStruct((n, BLOCK, QKV), jnp.bfloat16) for n in (2, 2, 2, 1, 1)
        ],
        compiler_params=pltpu.CompilerParams(vmem_limit_bytes=16 << 20),
        name="pick_blocks",
    )(sel, *blocks)


def attend_kernel(len_ref, here_ref, low_ref, high_ref, ids_ref, att_ref, out_ref, rows_ref):
    limit = len_ref[0]
    rows_ref[...] = here_ref[...] + low_ref[...] + high_ref[...]
    scale = 1.0 / math.sqrt(HEAD)
    for top in (0, BLOCK):
        span = top + BLOCK
        keys = rows_ref[0:span, GROUP * HEAD : (GROUP + 1) * HEAD]
        values = rows_ref[0:span, (GROUP + 1) * HEAD : (GROUP + 2) * HEAD]
        row = lax.broadcasted_iota(jnp.int32, (BLOCK, span), 0) + top
        col = lax.broadcasted_iota(jnp.int32, (BLOCK, span), 1)
        allowed = (col <= row) & (col < limit)
        for g in range(GROUP):
            query = rows_ref[top:span, g * HEAD : (g + 1) * HEAD]
            scores = lax.dot_general(
                query, keys, (((1,), (1,)), ((), ())), preferred_element_type=jnp.float32
            )
            scores = jnp.where(allowed, scores * scale, -jnp.inf)
            exponent = jnp.exp(scores - jnp.max(scores, axis=1, keepdims=True))
            probs = (exponent / jnp.sum(exponent, axis=1, keepdims=True)).astype(jnp.bfloat16)
            mixed = jnp.dot(probs, values, preferred_element_type=jnp.float32)
            att_ref[top:span, g * HEAD : (g + 1) * HEAD] = mixed.astype(jnp.bfloat16)
    names = lax.broadcasted_iota(jnp.int32, (EXPERTS, PROMPT), 0)
    named = (ids_ref[0:1, :] == names) | (ids_ref[1:2, :] == names)
    first = lax.broadcasted_iota(jnp.int32, (PROMPT, PROMPT), 0)
    second = lax.broadcasted_iota(jnp.int32, (PROMPT, PROMPT), 1)
    before = jnp.where(first < second, 1.0, 0.0).astype(jnp.bfloat16)
    taken = jnp.where(named, 1.0, 0.0)
    slot = jnp.dot(taken.astype(jnp.bfloat16), before, preferred_element_type=jnp.float32)
    slot = jnp.where(named, slot, -1.0).astype(jnp.int32)
    att = att_ref[...]
    place = lax.broadcasted_iota(jnp.int32, (CAP, PROMPT), 0)
    for e in range(EXPERTS):
        chosen = jnp.where(place == slot[e : e + 1, :], 1.0, 0.0).astype(jnp.bfloat16)
        sent = jnp.dot(chosen, att, preferred_element_type=jnp.float32)
        out_ref[e * CAP : (e + 1) * CAP, :] = sent.astype(jnp.bfloat16)


def attend(limit, parts, ids_t):
    vmem = pl.BlockSpec(memory_space=pltpu.VMEM)
    return pl.pallas_call(
        attend_kernel,
        in_specs=[pl.BlockSpec(memory_space=pltpu.SMEM)] + [vmem] * 4,
        out_specs=[vmem, vmem],
        out_shape=[
            jax.ShapeDtypeStruct((PROMPT, WIDTH), jnp.bfloat16),
            jax.ShapeDtypeStruct((EXPERTS * CAP, WIDTH), jnp.bfloat16),
        ],
        scratch_shapes=[pltpu.VMEM((PROMPT, QKV), jnp.bfloat16)],
        compiler_params=pltpu.CompilerParams(vmem_limit_bytes=16 << 20),
        name="attend",
    )(limit, *parts, ids_t)


def norm_kernel(x_ref, gain_ref, out_ref):
    total = jnp.zeros((CAP, 1), jnp.float32)
    for i in range(EXPERTS):
        part = x_ref[i].astype(jnp.float32)
        total = total + jnp.sum(part * part, axis=1, keepdims=True)
    factor = lax.rsqrt(total * (1.0 / D) + 1e-05)
    for i in range(EXPERTS):
        cols = slice(i * WIDTH, (i + 1) * WIDTH)
        out_ref[:, cols] = (x_ref[i].astype(jnp.float32) * factor * gain_ref[:, cols]).astype(
            jnp.bfloat16
        )


def normalise(arrived, gain):
    return pl.pallas_call(
        norm_kernel,
        out_shape=jax.ShapeDtypeStruct((CAP, D), jnp.bfloat16),
        compiler_params=pltpu.CompilerParams(vmem_limit_bytes=32 << 20),
        name="normalise",
    )(arrived, gain)


HALF = EXPERTS // 2


def ffn_kernel(x0, x1, x2, x3, gate_ref, up_ref, down_ref, *rest):
    *outs, xs = rest
    for j, x in enumerate((x0, x1, x2, x3)):
        xs[j * CAP : (j + 1) * CAP, :] = x[...]
    gate = jnp.dot(xs[...], gate_ref[0], preferred_element_type=jnp.float32)
    up = jnp.dot(xs[...], up_ref[0], preferred_element_type=jnp.float32)
    hidden = (gate / (1.0 + jnp.exp(-gate)) * up).astype(jnp.bfloat16)
    for i in range(EXPERTS):
        part = jnp.dot(
            hidden, down_ref[0, :, i * WIDTH : (i + 1) * WIDTH], preferred_element_type=jnp.float32
        ).astype(jnp.bfloat16)
        for j in range(SIDE):
            rows = part[j * CAP : (j + 1) * CAP]
            if j == SIDE - 1 and len(outs) > SIDE:
                outs[j + i // HALF][i % HALF] = rows
            else:
                outs[j][i] = rows


def ffn(shards, gate, up, down, halves=False):
    vmem = pl.BlockSpec(memory_space=pltpu.VMEM)
    leads = [EXPERTS] * (SIDE - 1) + ([HALF] * 2 if halves else [EXPERTS])
    return pl.pallas_call(
        ffn_kernel,
        in_specs=[vmem] * 7,
        out_specs=[vmem] * len(leads),
        out_shape=[jax.ShapeDtypeStruct((n, CAP, WIDTH), jnp.bfloat16) for n in leads],
        scratch_shapes=[pltpu.VMEM((SIDE * CAP, D), jnp.bfloat16)],
        compiler_params=pltpu.CompilerParams(vmem_limit_bytes=12 << 20),
        cost_estimate=pl.CostEstimate(
            flops=6 * SIDE * CAP * D * FF_DEV,
            transcendentals=SIDE * CAP * FF_DEV,
            bytes_accessed=4 * SIDE * CAP * D,
        ),
        name="ffn",
    )(*shards, gate, up, down)


def shift(value, first, step):
    pairs = []
    for z in range(SIDE):
        for y in range(SIDE):
            for e in range(EXPERTS):
                along_y = (e % 2 == 0) == first
                to_z, to_y = (z, (y + step) % SIDE) if along_y else ((z + step) % SIDE, y)
                pairs.append(((z * SIDE + y) * EXPERTS + e, (to_z * SIDE + to_y) * EXPERTS + e))
    return lax.ppermute(value, ("z", "y", "expert"), pairs)


def tie(*values):
    return lax.optimization_barrier(values)


def add(*parts, half=None):
    lead = EXPERTS if half is None else HALF

    def kernel(*refs):
        *part_refs, out_ref = refs
        total = None
        for ref in part_refs:
            if ref.shape[0] > lead:
                part = ref[half * HALF : (half + 1) * HALF]
            else:
                part = ref[...]
            part = part.astype(jnp.float32)
            total = part if total is None else total + part
        out_ref[...] = total.astype(jnp.bfloat16)

    block = pl.BlockSpec(memory_space=pltpu.VMEM)
    return pl.pallas_call(
        kernel,
        in_specs=[block] * len(parts),
        out_specs=block,
        out_shape=jax.ShapeDtypeStruct((lead, CAP, WIDTH), jnp.bfloat16),
        compiler_params=pltpu.CompilerParams(vmem_limit_bytes=4 << 20),
        name="add",
    )(*parts)


def join_kernel(whole_ref, first_ref, second_ref, out_ref):
    for h, ref in enumerate((first_ref, second_ref)):
        some = slice(h * HALF, (h + 1) * HALF)
        total = whole_ref[some].astype(jnp.float32) + ref[...].astype(jnp.float32)
        out_ref[some] = total.astype(jnp.bfloat16)


def join(whole, first, second):
    block = pl.BlockSpec(memory_space=pltpu.VMEM)
    return pl.pallas_call(
        join_kernel,
        in_specs=[block] * 3,
        out_specs=block,
        out_shape=jax.ShapeDtypeStruct(whole.shape, whole.dtype),
        compiler_params=pltpu.CompilerParams(vmem_limit_bytes=4 << 20),
        name="join",
    )(whole, first, second)


def load_kernel(source, target, sem):
    copy = pltpu.make_async_copy(source, target, sem)
    copy.start()
    copy.wait()


def load(weight):
    return pl.pallas_call(
        load_kernel,
        in_specs=[pl.BlockSpec(memory_space=pltpu.HBM)],
        out_specs=pl.BlockSpec(memory_space=pltpu.VMEM),
        out_shape=jax.ShapeDtypeStruct(weight.shape, weight.dtype),
        scratch_shapes=[pltpu.SemaphoreType.DMA],
        compiler_params=pltpu.CompilerParams(vmem_limit_bytes=4 << 20),
        name="load",
    )(weight)


def experts(own, weights):
    gate, up, down = weights
    low, high = shift(own, True, 1), shift(own, True, -1)
    own_low, own_high = shift(own, False, 1), shift(own, False, -1)
    low, high, gate = tie(low, high, load(gate))
    across, low_high = shift(low, True, 1), shift(low, False, -1)
    own_low, own_high, low, high, up = tie(own_low, own_high, low, high, load(up))
    low_low, high_high = shift(low, False, 1), shift(high, False, -1)
    across, low_high, own_high, high, down = tie(across, low_high, own_high, high, load(down))
    weights = gate, up, down
    high_low, own_far = shift(high, False, 1), shift(own_high, False, -1)
    low_low, high_high = tie(low_low, high_high)
    low_far, high_far = shift(low_low, False, 1), shift(high_high, False, -1)
    high_low, own_far, across = tie(high_low, own_far, across)
    across_low, across_high = shift(across, False, 1), shift(across, False, -1)
    own_parts = ffn((own, own_low, own_high, own_far), *weights)
    low_far, high_far, *own_parts = tie(low_far, high_far, *own_parts)
    own_passed, own_behind = shift(own_parts[3], False, -1), shift(own_parts[2], False, 1)
    high_parts = ffn((high, high_low, high_high, high_far), *weights)
    across_low, across_high, *high_parts = tie(across_low, across_high, *high_parts)
    across_far = shift(across_high, False, -1)
    high_passed = shift(high_parts[3], False, 1)
    low_parts = ffn((low, low_low, low_high, low_far), *weights)
    low_passed, low_behind = shift(low_parts[3], False, -1), shift(low_parts[2], False, 1)
    own_passed, own_behind, across_far, high_passed = tie(
        own_passed, own_behind, across_far, high_passed
    )
    own_ahead = shift(add(own_parts[1], own_passed), False, -1)
    high_ahead = shift(add(high_parts[2], high_passed), False, 1)
    here, to_low, to_high, *to_far = ffn(
        (across, across_low, across_high, across_far), *weights, halves=True
    )
    low_passed, low_behind, *to_far = tie(low_passed, low_behind, *to_far)
    passed = [shift(part, False, 1) for part in to_far]
    low_ahead = shift(add(low_parts[1], low_passed), False, -1)
    passed[0], own_ahead, high_ahead = tie(passed[0], own_ahead, high_ahead)
    ahead = [shift(add(to_high, passed[h], half=h), False, 1) for h in range(2)]
    behind = shift(to_low, False, -1)
    ahead[0], low_ahead, behind, to_low = tie(ahead[0], low_ahead, behind, high_parts[1])
    high_behind = shift(to_low, False, -1)
    own_sum = add(own_parts[0], own_ahead, own_behind)
    low_sum = add(low_parts[0], low_ahead, low_behind)
    own_sum = add(own_sum, shift(low_sum, True, -1))
    passed = [shift(add(here, behind, ahead[h], half=h), True, 1) for h in range(2)]
    last = [
        shift(add(high_parts[0], high_ahead, high_behind, passed[h], half=h), True, 1)
        for h in range(2)
    ]
    return join(own_sum, *last)


def combine_kernel(att_ref, ret_ref, ids_ref, logits_ref, out_ref):
    names = lax.broadcasted_iota(jnp.int32, (PROMPT, HEAD), 1)
    ids = [ids_ref[:, c : c + 1] for c in range(2)]
    named = (ids[0] == names) | (ids[1] == names)
    first = lax.broadcasted_iota(jnp.int32, (PROMPT, PROMPT), 0)
    second = lax.broadcasted_iota(jnp.int32, (PROMPT, PROMPT), 1)
    before = jnp.where(second < first, 1.0, 0.0).astype(jnp.bfloat16)
    taken = jnp.where(named, 1.0, 0.0).astype(jnp.bfloat16)
    count = jnp.dot(before, taken, preferred_element_type=jnp.float32)
    logits = [logits_ref[:, c : c + 1] for c in range(2)]
    top = jnp.maximum(logits[0], logits[1])
    exps = [jnp.exp(v - top) for v in logits]
    total = exps[0] + exps[1]
    ret = ret_ref[...]
    column = lax.broadcasted_iota(jnp.int32, (PROMPT, EXPERTS * CAP), 1)
    mixed = None
    for c in range(2):
        slot = jnp.sum(jnp.where(ids[c] == names, count, 0.0), axis=1, keepdims=True)
        at = ids[c] * CAP + slot.astype(jnp.int32)
        chosen = jnp.where(column == at, 1.0, 0.0).astype(jnp.bfloat16)
        picked = jnp.dot(chosen, ret, preferred_element_type=jnp.float32)
        term = exps[c] / total * picked
        mixed = term if mixed is None else mixed + term
    out_ref[...] = (att_ref[...].astype(jnp.float32) + mixed).astype(jnp.bfloat16)


def combine(att, returned, ids, logits):
    return pl.pallas_call(
        combine_kernel,
        out_shape=jax.ShapeDtypeStruct((PROMPT, WIDTH), jnp.bfloat16),
        compiler_params=pltpu.CompilerParams(vmem_limit_bytes=32 << 20),
        name="combine",
    )(att, returned, ids, logits)


def fetch_rows(records, pair_blocks):
    z, y = lax.axis_index("z"), lax.axis_index("y")
    y_first = lax.axis_index("expert") % 2 == 0
    low, high = tie(shift(records, True, 1), shift(records, True, -1))
    far0, far1 = tie(shift(low[:1], True, 1), shift(high[1:], True, -1))
    first, second = jnp.where(y_first, y, z), jnp.where(y_first, z, y)
    ahead = jnp.array([0, 0, 1, 1, -1, -1, 2, 2], jnp.int32)
    slot = jnp.array([0, 1, 0, 1, 0, 1, 0, 1], jnp.int32)
    target = (second + ahead) % SIDE
    prompt = jnp.where(y_first, target * SIDE + first, first * SIDE + target)
    wanted = pair_blocks[prompt, slot]
    owner = wanted // 2
    own_z, own_y = owner // SIDE, owner % SIDE
    own_first, own_second = jnp.where(y_first, own_y, own_z), jnp.where(y_first, own_z, own_y)
    away = (own_first - first) % SIDE
    half = wanted % 2
    source = jnp.where(away == 0, half, jnp.where(away == 3, 2 + half, jnp.where(away == 1, 4 + half, 6 + half)))
    sel = jnp.where(own_second == second, source, -1)
    here, up, down, up_far, down_far = pick_blocks(sel, (records, low, high, far0, far1))
    up_got, down_got = tie(shift(up_far, False, 1), shift(down_far, False, -1))
    up = jnp.concatenate([up[:1] + up_got, up[1:]], axis=0)
    down = jnp.concatenate([down[:1], down[1:] + down_got], axis=0)
    return here, shift(up, False, 1), shift(down, False, -1)


def body(
    records,
    pair_blocks,
    lengths,
    norm_gain,
    gate_logits,
    expert_ids,
    gate_weight,
    up_weight,
    down_weight,
):
    dp_index = lax.axis_index("z") * SIDE + lax.axis_index("y")
    limit = lax.dynamic_slice_in_dim(lengths, dp_index, 1, 0)
    parts = [part.reshape(PROMPT, QKV) for part in fetch_rows(records, pair_blocks)]
    att, outgoing = attend(limit, parts, expert_ids.T)
    arrived = lax.all_to_all(
        outgoing.reshape(EXPERTS, CAP, WIDTH), "expert", split_axis=0, concat_axis=0, tiled=True
    )
    normed = normalise(arrived, norm_gain.reshape(1, D))
    summed = experts(normed, (gate_weight, up_weight, down_weight))
    returned = lax.all_to_all(summed, "expert", split_axis=0, concat_axis=0, tiled=True)
    return combine(att, returned.reshape(EXPERTS * CAP, WIDTH), expert_ids, gate_logits)


def solution(mesh):
    fine = Mesh(mesh.devices.reshape(SIDE, SIDE, EXPERTS), ("z", "y", "expert"))
    dp = ("z", "y")
    placed = (
        P(dp, None, "expert"),
        P(),
        P(),
        P(),
        P(dp, None),
        P(dp, None),
        P("expert", None, dp),
        P("expert", None, dp),
        P("expert", dp, None),
    )
    return jax.shard_map(
        body, mesh=fine, in_specs=placed, out_specs=P(dp, "expert"), check_vma=False
    )
```

```python
import math

import jax
import jax.numpy as jnp
from jax import lax
from jax.experimental import pallas as pl
from jax.experimental.pallas import tpu as pltpu
from jax.sharding import Mesh
from jax.sharding import PartitionSpec as P

HEAD = 128
GROUP = 6
BLOCK = 128
PROMPT = 256
EXPERTS = 8
CAP = 80
WIDTH = 768
D = 6144
FF_DEV = 512
N_DP = 16
SIDE = 4
QKV = 1024


def pick_kernel(sel_ref, own, low, high, far0, far1, here, up, down, up_far, down_far):
    sources = [own.at[0], own.at[1], low.at[0], low.at[1], high.at[0], high.at[1], far0.at[0], far1.at[0]]
    targets = [here.at[0], here.at[1], up.at[0], up.at[1], down.at[0], down.at[1], up_far.at[0], down_far.at[0]]
    for i, target in enumerate(targets):
        for k, source in enumerate(sources):

            @pl.when(sel_ref[i] == k)
            def _():
                target[...] = source[...]

        @pl.when(sel_ref[i] < 0)
        def _():
            target[...] = jnp.zeros_like(target)


def pick_blocks(sel, blocks):
    vmem = pl.BlockSpec(memory_space=pltpu.VMEM)
    return pl.pallas_call(
        pick_kernel,
        in_specs=[pl.BlockSpec(memory_space=pltpu.SMEM)] + [vmem] * 5,
        out_specs=[vmem] * 5,
        out_shape=[
            jax.ShapeDtypeStruct((n, BLOCK, QKV), jnp.bfloat16) for n in (2, 2, 2, 1, 1)
        ],
        compiler_params=pltpu.CompilerParams(vmem_limit_bytes=16 << 20),
        name="pick_blocks",
    )(sel, *blocks)


def attend_kernel(len_ref, here_ref, low_ref, high_ref, ids_ref, att_ref, out_ref, rows_ref):
    limit = len_ref[0]
    rows_ref[...] = here_ref[...] + low_ref[...] + high_ref[...]
    scale = 1.0 / math.sqrt(HEAD)
    for top in (0, BLOCK):
        span = top + BLOCK
        keys = rows_ref[0:span, GROUP * HEAD : (GROUP + 1) * HEAD]
        values = rows_ref[0:span, (GROUP + 1) * HEAD : (GROUP + 2) * HEAD]
        row = lax.broadcasted_iota(jnp.int32, (BLOCK, span), 0) + top
        col = lax.broadcasted_iota(jnp.int32, (BLOCK, span), 1)
        allowed = (col <= row) & (col < limit)
        for g in range(GROUP):
            query = rows_ref[top:span, g * HEAD : (g + 1) * HEAD]
            scores = lax.dot_general(
                query, keys, (((1,), (1,)), ((), ())), preferred_element_type=jnp.float32
            )
            scores = jnp.where(allowed, scores * scale, -jnp.inf)
            exponent = jnp.exp(scores - jnp.max(scores, axis=1, keepdims=True))
            probs = (exponent / jnp.sum(exponent, axis=1, keepdims=True)).astype(jnp.bfloat16)
            mixed = jnp.dot(probs, values, preferred_element_type=jnp.float32)
            att_ref[top:span, g * HEAD : (g + 1) * HEAD] = mixed.astype(jnp.bfloat16)
    names = lax.broadcasted_iota(jnp.int32, (EXPERTS, PROMPT), 0)
    named = (ids_ref[0:1, :] == names) | (ids_ref[1:2, :] == names)
    first = lax.broadcasted_iota(jnp.int32, (PROMPT, PROMPT), 0)
    second = lax.broadcasted_iota(jnp.int32, (PROMPT, PROMPT), 1)
    before = jnp.where(first < second, 1.0, 0.0).astype(jnp.bfloat16)
    taken = jnp.where(named, 1.0, 0.0)
    slot = jnp.dot(taken.astype(jnp.bfloat16), before, preferred_element_type=jnp.float32)
    slot = jnp.where(named, slot, -1.0).astype(jnp.int32)
    att = att_ref[...]
    place = lax.broadcasted_iota(jnp.int32, (CAP, PROMPT), 0)
    for e in range(EXPERTS):
        chosen = jnp.where(place == slot[e : e + 1, :], 1.0, 0.0).astype(jnp.bfloat16)
        sent = jnp.dot(chosen, att, preferred_element_type=jnp.float32)
        out_ref[e * CAP : (e + 1) * CAP, :] = sent.astype(jnp.bfloat16)


def attend(limit, parts, ids_t):
    vmem = pl.BlockSpec(memory_space=pltpu.VMEM)
    return pl.pallas_call(
        attend_kernel,
        in_specs=[pl.BlockSpec(memory_space=pltpu.SMEM)] + [vmem] * 4,
        out_specs=[vmem, vmem],
        out_shape=[
            jax.ShapeDtypeStruct((PROMPT, WIDTH), jnp.bfloat16),
            jax.ShapeDtypeStruct((EXPERTS * CAP, WIDTH), jnp.bfloat16),
        ],
        scratch_shapes=[pltpu.VMEM((PROMPT, QKV), jnp.bfloat16)],
        compiler_params=pltpu.CompilerParams(vmem_limit_bytes=16 << 20),
        name="attend",
    )(limit, *parts, ids_t)


def norm_kernel(x_ref, gain_ref, out_ref):
    total = jnp.zeros((CAP, 1), jnp.float32)
    for i in range(EXPERTS):
        part = x_ref[i].astype(jnp.float32)
        total = total + jnp.sum(part * part, axis=1, keepdims=True)
    factor = lax.rsqrt(total * (1.0 / D) + 1e-05)
    for i in range(EXPERTS):
        cols = slice(i * WIDTH, (i + 1) * WIDTH)
        out_ref[:, cols] = (x_ref[i].astype(jnp.float32) * factor * gain_ref[:, cols]).astype(
            jnp.bfloat16
        )


def normalise(arrived, gain):
    return pl.pallas_call(
        norm_kernel,
        out_shape=jax.ShapeDtypeStruct((CAP, D), jnp.bfloat16),
        compiler_params=pltpu.CompilerParams(vmem_limit_bytes=32 << 20),
        name="normalise",
    )(arrived, gain)


HALF = EXPERTS // 2


def ffn_kernel(x0, x1, x2, x3, gate_ref, up_ref, down_ref, *rest):
    *outs, xs = rest
    for j, x in enumerate((x0, x1, x2, x3)):
        xs[j * CAP : (j + 1) * CAP, :] = x[...]
    gate = jnp.dot(xs[...], gate_ref[0], preferred_element_type=jnp.float32)
    up = jnp.dot(xs[...], up_ref[0], preferred_element_type=jnp.float32)
    hidden = (gate / (1.0 + jnp.exp(-gate)) * up).astype(jnp.bfloat16)
    for i in range(EXPERTS):
        part = jnp.dot(
            hidden, down_ref[0, :, i * WIDTH : (i + 1) * WIDTH], preferred_element_type=jnp.float32
        ).astype(jnp.bfloat16)
        for j in range(SIDE):
            rows = part[j * CAP : (j + 1) * CAP]
            if j == SIDE - 1 and len(outs) > SIDE:
                outs[j + i // HALF][i % HALF] = rows
            else:
                outs[j][i] = rows


def ffn(shards, gate, up, down, halves=False):
    vmem = pl.BlockSpec(memory_space=pltpu.VMEM)
    leads = [EXPERTS] * (SIDE - 1) + ([HALF] * 2 if halves else [EXPERTS])
    return pl.pallas_call(
        ffn_kernel,
        in_specs=[vmem] * 7,
        out_specs=[vmem] * len(leads),
        out_shape=[jax.ShapeDtypeStruct((n, CAP, WIDTH), jnp.bfloat16) for n in leads],
        scratch_shapes=[pltpu.VMEM((SIDE * CAP, D), jnp.bfloat16)],
        compiler_params=pltpu.CompilerParams(vmem_limit_bytes=12 << 20),
        cost_estimate=pl.CostEstimate(
            flops=6 * SIDE * CAP * D * FF_DEV,
            transcendentals=SIDE * CAP * FF_DEV,
            bytes_accessed=4 * SIDE * CAP * D,
        ),
        name="ffn",
    )(*shards, gate, up, down)


def shift(value, first, step):
    pairs = []
    for z in range(SIDE):
        for y in range(SIDE):
            for e in range(EXPERTS):
                along_y = (e % 2 == 0) == first
                to_z, to_y = (z, (y + step) % SIDE) if along_y else ((z + step) % SIDE, y)
                pairs.append(((z * SIDE + y) * EXPERTS + e, (to_z * SIDE + to_y) * EXPERTS + e))
    return lax.ppermute(value, ("z", "y", "expert"), pairs)


def tie(*values):
    return lax.optimization_barrier(values)


def add(*parts, half=None):
    lead = EXPERTS if half is None else HALF

    def kernel(*refs):
        *part_refs, out_ref = refs
        total = None
        for ref in part_refs:
            if ref.shape[0] > lead:
                part = ref[half * HALF : (half + 1) * HALF]
            else:
                part = ref[...]
            part = part.astype(jnp.float32)
            total = part if total is None else total + part
        out_ref[...] = total.astype(jnp.bfloat16)

    block = pl.BlockSpec(memory_space=pltpu.VMEM)
    return pl.pallas_call(
        kernel,
        in_specs=[block] * len(parts),
        out_specs=block,
        out_shape=jax.ShapeDtypeStruct((lead, CAP, WIDTH), jnp.bfloat16),
        compiler_params=pltpu.CompilerParams(vmem_limit_bytes=4 << 20),
        name="add",
    )(*parts)


def join_kernel(whole_ref, first_ref, second_ref, out_ref):
    for h, ref in enumerate((first_ref, second_ref)):
        some = slice(h * HALF, (h + 1) * HALF)
        total = whole_ref[some].astype(jnp.float32) + ref[...].astype(jnp.float32)
        out_ref[some] = total.astype(jnp.bfloat16)


def join(whole, first, second):
    block = pl.BlockSpec(memory_space=pltpu.VMEM)
    return pl.pallas_call(
        join_kernel,
        in_specs=[block] * 3,
        out_specs=block,
        out_shape=jax.ShapeDtypeStruct(whole.shape, whole.dtype),
        compiler_params=pltpu.CompilerParams(vmem_limit_bytes=4 << 20),
        name="join",
    )(whole, first, second)


def load_kernel(source, target, sem):
    copy = pltpu.make_async_copy(source, target, sem)
    copy.start()
    copy.wait()


def load(weight):
    return pl.pallas_call(
        load_kernel,
        in_specs=[pl.BlockSpec(memory_space=pltpu.HBM)],
        out_specs=pl.BlockSpec(memory_space=pltpu.VMEM),
        out_shape=jax.ShapeDtypeStruct(weight.shape, weight.dtype),
        scratch_shapes=[pltpu.SemaphoreType.DMA],
        compiler_params=pltpu.CompilerParams(vmem_limit_bytes=4 << 20),
        name="load",
    )(weight)


def experts(own, weights):
    low, high = shift(own, True, 1), shift(own, True, -1)
    own_low, own_high = shift(own, False, 1), shift(own, False, -1)
    low, high, *weights = tie(low, high, *[load(weight) for weight in weights])
    across, low_high = shift(low, True, 1), shift(low, False, -1)
    own_low, own_high, low, high = tie(own_low, own_high, low, high)
    low_low, high_high = shift(low, False, 1), shift(high, False, -1)
    across, low_high, own_high, high = tie(across, low_high, own_high, high)
    high_low, own_far = shift(high, False, 1), shift(own_high, False, -1)
    low_low, high_high, across = tie(low_low, high_high, across)
    across_low, across_high = shift(across, False, 1), shift(across, False, -1)
    high_low, own_far, low_low, high_high = tie(high_low, own_far, low_low, high_high)
    low_far, high_far = shift(low_low, False, 1), shift(high_high, False, -1)
    own_parts = ffn((own, own_low, own_high, own_far), *weights)
    across_low, across_high, *own_parts = tie(across_low, across_high, *own_parts)
    across_far = shift(across_high, False, -1)
    own_passed, own_behind = shift(own_parts[3], False, -1), shift(own_parts[2], False, 1)
    high_parts = ffn((high, high_low, high_high, high_far), *weights)
    across_far, low_far, *high_parts = tie(across_far, low_far, *high_parts)
    high_passed = shift(high_parts[3], False, 1)
    here, to_low, to_high, *to_far = ffn(
        (across, across_low, across_high, across_far), *weights, halves=True
    )
    own_passed, own_behind, low, *to_far = tie(own_passed, own_behind, low, *to_far)
    passed = [shift(part, False, 1) for part in to_far]
    own_ahead = shift(add(own_parts[1], own_passed), False, -1)
    low_parts = ffn((low, low_low, low_high, low_far), *weights)
    low_passed, low_behind = shift(low_parts[3], False, -1), shift(low_parts[2], False, 1)
    passed[0], high_passed, own_ahead, to_low = tie(passed[0], high_passed, own_ahead, to_low)
    ahead = [shift(add(to_high, passed[h], half=h), False, 1) for h in range(2)]
    behind = shift(to_low, False, -1)
    high_ahead = shift(add(high_parts[2], high_passed), False, 1)
    ahead[0], behind, low_passed, high_ahead = tie(ahead[0], behind, low_passed, high_ahead)
    low_ahead = shift(add(low_parts[1], low_passed), False, -1)
    high_behind = shift(high_parts[1], False, -1)
    passed = [shift(add(here, behind, ahead[h], half=h), True, 1) for h in range(2)]
    last = [
        shift(add(high_parts[0], high_ahead, high_behind, passed[h], half=h), True, 1)
        for h in range(2)
    ]
    own_sum = add(own_parts[0], own_ahead, own_behind)
    low_sum = add(low_parts[0], low_ahead, low_behind)
    own_sum = add(own_sum, shift(low_sum, True, -1))
    return join(own_sum, *last)


def combine_kernel(att_ref, ret_ref, ids_ref, logits_ref, out_ref):
    names = lax.broadcasted_iota(jnp.int32, (PROMPT, HEAD), 1)
    ids = [ids_ref[:, c : c + 1] for c in range(2)]
    named = (ids[0] == names) | (ids[1] == names)
    first = lax.broadcasted_iota(jnp.int32, (PROMPT, PROMPT), 0)
    second = lax.broadcasted_iota(jnp.int32, (PROMPT, PROMPT), 1)
    before = jnp.where(second < first, 1.0, 0.0).astype(jnp.bfloat16)
    taken = jnp.where(named, 1.0, 0.0).astype(jnp.bfloat16)
    count = jnp.dot(before, taken, preferred_element_type=jnp.float32)
    logits = [logits_ref[:, c : c + 1] for c in range(2)]
    top = jnp.maximum(logits[0], logits[1])
    exps = [jnp.exp(v - top) for v in logits]
    total = exps[0] + exps[1]
    ret = ret_ref[...]
    column = lax.broadcasted_iota(jnp.int32, (PROMPT, EXPERTS * CAP), 1)
    mixed = None
    for c in range(2):
        slot = jnp.sum(jnp.where(ids[c] == names, count, 0.0), axis=1, keepdims=True)
        at = ids[c] * CAP + slot.astype(jnp.int32)
        chosen = jnp.where(column == at, 1.0, 0.0).astype(jnp.bfloat16)
        picked = jnp.dot(chosen, ret, preferred_element_type=jnp.float32)
        term = exps[c] / total * picked
        mixed = term if mixed is None else mixed + term
    out_ref[...] = (att_ref[...].astype(jnp.float32) + mixed).astype(jnp.bfloat16)


def combine(att, returned, ids, logits):
    return pl.pallas_call(
        combine_kernel,
        out_shape=jax.ShapeDtypeStruct((PROMPT, WIDTH), jnp.bfloat16),
        compiler_params=pltpu.CompilerParams(vmem_limit_bytes=32 << 20),
        name="combine",
    )(att, returned, ids, logits)


def fetch_rows(records, pair_blocks):
    z, y = lax.axis_index("z"), lax.axis_index("y")
    y_first = lax.axis_index("expert") % 2 == 0
    low, high = tie(shift(records, True, 1), shift(records, True, -1))
    far0, far1 = tie(shift(low[:1], True, 1), shift(high[1:], True, -1))
    first, second = jnp.where(y_first, y, z), jnp.where(y_first, z, y)
    ahead = jnp.array([0, 0, 1, 1, -1, -1, 2, 2], jnp.int32)
    slot = jnp.array([0, 1, 0, 1, 0, 1, 0, 1], jnp.int32)
    target = (second + ahead) % SIDE
    prompt = jnp.where(y_first, target * SIDE + first, first * SIDE + target)
    wanted = pair_blocks[prompt, slot]
    owner = wanted // 2
    own_z, own_y = owner // SIDE, owner % SIDE
    own_first, own_second = jnp.where(y_first, own_y, own_z), jnp.where(y_first, own_z, own_y)
    away = (own_first - first) % SIDE
    half = wanted % 2
    source = jnp.where(away == 0, half, jnp.where(away == 3, 2 + half, jnp.where(away == 1, 4 + half, 6 + half)))
    sel = jnp.where(own_second == second, source, -1)
    here, up, down, up_far, down_far = pick_blocks(sel, (records, low, high, far0, far1))
    up_got, down_got = tie(shift(up_far, False, 1), shift(down_far, False, -1))
    up = jnp.concatenate([up[:1] + up_got, up[1:]], axis=0)
    down = jnp.concatenate([down[:1], down[1:] + down_got], axis=0)
    return here, shift(up, False, 1), shift(down, False, -1)


def body(
    records,
    pair_blocks,
    lengths,
    norm_gain,
    gate_logits,
    expert_ids,
    gate_weight,
    up_weight,
    down_weight,
):
    dp_index = lax.axis_index("z") * SIDE + lax.axis_index("y")
    limit = lax.dynamic_slice_in_dim(lengths, dp_index, 1, 0)
    parts = [part.reshape(PROMPT, QKV) for part in fetch_rows(records, pair_blocks)]
    att, outgoing = attend(limit, parts, expert_ids.T)
    arrived = lax.all_to_all(
        outgoing.reshape(EXPERTS, CAP, WIDTH), "expert", split_axis=0, concat_axis=0, tiled=True
    )
    normed = normalise(arrived, norm_gain.reshape(1, D))
    summed = experts(normed, (gate_weight, up_weight, down_weight))
    returned = lax.all_to_all(summed, "expert", split_axis=0, concat_axis=0, tiled=True)
    return combine(att, returned.reshape(EXPERTS * CAP, WIDTH), expert_ids, gate_logits)


def solution(mesh):
    fine = Mesh(mesh.devices.reshape(SIDE, SIDE, EXPERTS), ("z", "y", "expert"))
    dp = ("z", "y")
    placed = (
        P(dp, None, "expert"),
        P(),
        P(),
        P(),
        P(dp, None),
        P(dp, None),
        P("expert", None, dp),
        P("expert", None, dp),
        P("expert", dp, None),
    )
    return jax.shard_map(
        body, mesh=fine, in_specs=placed, out_specs=P(dp, "expert"), check_vma=False
    )
```

```python
import math

import jax
import jax.numpy as jnp
from jax import lax
from jax.experimental import pallas as pl
from jax.experimental.pallas import tpu as pltpu
from jax.sharding import Mesh
from jax.sharding import PartitionSpec as P

HEAD = 128
GROUP = 6
BLOCK = 128
PROMPT = 256
EXPERTS = 8
CAP = 80
WIDTH = 768
D = 6144
FF_DEV = 512
N_DP = 16
SIDE = 4
QKV = 1024


def pick_kernel(sel_ref, own, low, high, far0, far1, here, up, down, up_far, down_far):
    sources = [own.at[0], own.at[1], low.at[0], low.at[1], high.at[0], high.at[1], far0.at[0], far1.at[0]]
    targets = [here.at[0], here.at[1], up.at[0], up.at[1], down.at[0], down.at[1], up_far.at[0], down_far.at[0]]
    for i, target in enumerate(targets):
        for k, source in enumerate(sources):

            @pl.when(sel_ref[i] == k)
            def _():
                target[...] = source[...]

        @pl.when(sel_ref[i] < 0)
        def _():
            target[...] = jnp.zeros_like(target)


def pick_blocks(sel, blocks):
    vmem = pl.BlockSpec(memory_space=pltpu.VMEM)
    return pl.pallas_call(
        pick_kernel,
        in_specs=[pl.BlockSpec(memory_space=pltpu.SMEM)] + [vmem] * 5,
        out_specs=[vmem] * 5,
        out_shape=[
            jax.ShapeDtypeStruct((n, BLOCK, QKV), jnp.bfloat16) for n in (2, 2, 2, 1, 1)
        ],
        compiler_params=pltpu.CompilerParams(vmem_limit_bytes=16 << 20),
        name="pick_blocks",
    )(sel, *blocks)


def attend_kernel(len_ref, here_ref, low_ref, high_ref, ids_ref, att_ref, out_ref, rows_ref):
    limit = len_ref[0]
    rows_ref[...] = here_ref[...] + low_ref[...] + high_ref[...]
    scale = 1.0 / math.sqrt(HEAD)
    for top in (0, BLOCK):
        span = top + BLOCK
        keys = rows_ref[0:span, GROUP * HEAD : (GROUP + 1) * HEAD]
        values = rows_ref[0:span, (GROUP + 1) * HEAD : (GROUP + 2) * HEAD]
        row = lax.broadcasted_iota(jnp.int32, (BLOCK, span), 0) + top
        col = lax.broadcasted_iota(jnp.int32, (BLOCK, span), 1)
        allowed = (col <= row) & (col < limit)
        for g in range(GROUP):
            query = rows_ref[top:span, g * HEAD : (g + 1) * HEAD]
            scores = lax.dot_general(
                query, keys, (((1,), (1,)), ((), ())), preferred_element_type=jnp.float32
            )
            scores = jnp.where(allowed, scores * scale, -jnp.inf)
            exponent = jnp.exp(scores - jnp.max(scores, axis=1, keepdims=True))
            probs = (exponent / jnp.sum(exponent, axis=1, keepdims=True)).astype(jnp.bfloat16)
            mixed = jnp.dot(probs, values, preferred_element_type=jnp.float32)
            att_ref[top:span, g * HEAD : (g + 1) * HEAD] = mixed.astype(jnp.bfloat16)
    names = lax.broadcasted_iota(jnp.int32, (EXPERTS, PROMPT), 0)
    named = (ids_ref[0:1, :] == names) | (ids_ref[1:2, :] == names)
    first = lax.broadcasted_iota(jnp.int32, (PROMPT, PROMPT), 0)
    second = lax.broadcasted_iota(jnp.int32, (PROMPT, PROMPT), 1)
    before = jnp.where(first < second, 1.0, 0.0).astype(jnp.bfloat16)
    taken = jnp.where(named, 1.0, 0.0)
    slot = jnp.dot(taken.astype(jnp.bfloat16), before, preferred_element_type=jnp.float32)
    slot = jnp.where(named, slot, -1.0).astype(jnp.int32)
    att = att_ref[...]
    place = lax.broadcasted_iota(jnp.int32, (CAP, PROMPT), 0)
    for e in range(EXPERTS):
        chosen = jnp.where(place == slot[e : e + 1, :], 1.0, 0.0).astype(jnp.bfloat16)
        sent = jnp.dot(chosen, att, preferred_element_type=jnp.float32)
        out_ref[e * CAP : (e + 1) * CAP, :] = sent.astype(jnp.bfloat16)


def attend(limit, parts, ids_t):
    vmem = pl.BlockSpec(memory_space=pltpu.VMEM)
    return pl.pallas_call(
        attend_kernel,
        in_specs=[pl.BlockSpec(memory_space=pltpu.SMEM)] + [vmem] * 4,
        out_specs=[vmem, vmem],
        out_shape=[
            jax.ShapeDtypeStruct((PROMPT, WIDTH), jnp.bfloat16),
            jax.ShapeDtypeStruct((EXPERTS * CAP, WIDTH), jnp.bfloat16),
        ],
        scratch_shapes=[pltpu.VMEM((PROMPT, QKV), jnp.bfloat16)],
        compiler_params=pltpu.CompilerParams(vmem_limit_bytes=16 << 20),
        name="attend",
    )(limit, *parts, ids_t)


def norm_kernel(x_ref, gain_ref, out_ref):
    total = jnp.zeros((CAP, 1), jnp.float32)
    for i in range(EXPERTS):
        part = x_ref[i].astype(jnp.float32)
        total = total + jnp.sum(part * part, axis=1, keepdims=True)
    factor = lax.rsqrt(total * (1.0 / D) + 1e-05)
    for i in range(EXPERTS):
        cols = slice(i * WIDTH, (i + 1) * WIDTH)
        out_ref[:, cols] = (x_ref[i].astype(jnp.float32) * factor * gain_ref[:, cols]).astype(
            jnp.bfloat16
        )


def normalise(arrived, gain):
    return pl.pallas_call(
        norm_kernel,
        out_shape=jax.ShapeDtypeStruct((CAP, D), jnp.bfloat16),
        compiler_params=pltpu.CompilerParams(vmem_limit_bytes=32 << 20),
        name="normalise",
    )(arrived, gain)


def ffn_kernel(x0, x1, x2, x3, gate_ref, up_ref, down_ref, o0, o1, o2, o3, xs):
    for j, x in enumerate((x0, x1, x2, x3)):
        xs[j * CAP : (j + 1) * CAP, :] = x[...]
    gate = jnp.dot(xs[...], gate_ref[0], preferred_element_type=jnp.float32)
    up = jnp.dot(xs[...], up_ref[0], preferred_element_type=jnp.float32)
    hidden = (gate / (1.0 + jnp.exp(-gate)) * up).astype(jnp.bfloat16)
    for i in range(EXPERTS):
        part = jnp.dot(
            hidden, down_ref[0, :, i * WIDTH : (i + 1) * WIDTH], preferred_element_type=jnp.float32
        ).astype(jnp.bfloat16)
        for j, o in enumerate((o0, o1, o2, o3)):
            o[i] = part[j * CAP : (j + 1) * CAP]


def ffn(shards, gate, up, down):
    vmem = pl.BlockSpec(memory_space=pltpu.VMEM)
    return pl.pallas_call(
        ffn_kernel,
        in_specs=[vmem] * 7,
        out_specs=[vmem] * SIDE,
        out_shape=[jax.ShapeDtypeStruct((EXPERTS, CAP, WIDTH), jnp.bfloat16)] * SIDE,
        scratch_shapes=[pltpu.VMEM((SIDE * CAP, D), jnp.bfloat16)],
        compiler_params=pltpu.CompilerParams(vmem_limit_bytes=12 << 20),
        cost_estimate=pl.CostEstimate(
            flops=6 * SIDE * CAP * D * FF_DEV,
            transcendentals=SIDE * CAP * FF_DEV,
            bytes_accessed=4 * SIDE * CAP * D,
        ),
        name="ffn",
    )(*shards, gate, up, down)


def shift(value, first, step):
    pairs = []
    for z in range(SIDE):
        for y in range(SIDE):
            for e in range(EXPERTS):
                along_y = (e % 2 == 0) == first
                to_z, to_y = (z, (y + step) % SIDE) if along_y else ((z + step) % SIDE, y)
                pairs.append(((z * SIDE + y) * EXPERTS + e, (to_z * SIDE + to_y) * EXPERTS + e))
    return lax.ppermute(value, ("z", "y", "expert"), pairs)


def tie(*values):
    return lax.optimization_barrier(values)


def add_kernel(*refs):
    *parts, out_ref = refs
    total = parts[0][...].astype(jnp.float32)
    for part in parts[1:]:
        total = total + part[...].astype(jnp.float32)
    out_ref[...] = total.astype(jnp.bfloat16)


def add(*parts):
    shape = parts[0].shape
    block = pl.BlockSpec(memory_space=pltpu.VMEM)
    return pl.pallas_call(
        add_kernel,
        in_specs=[block] * len(parts),
        out_specs=block,
        out_shape=jax.ShapeDtypeStruct(shape, jnp.bfloat16),
        compiler_params=pltpu.CompilerParams(vmem_limit_bytes=4 << 20),
        name="add",
    )(*parts)


def load_kernel(source, target, sem):
    copy = pltpu.make_async_copy(source, target, sem)
    copy.start()
    copy.wait()


def load(weight):
    return pl.pallas_call(
        load_kernel,
        in_specs=[pl.BlockSpec(memory_space=pltpu.HBM)],
        out_specs=pl.BlockSpec(memory_space=pltpu.VMEM),
        out_shape=jax.ShapeDtypeStruct(weight.shape, weight.dtype),
        scratch_shapes=[pltpu.SemaphoreType.DMA],
        compiler_params=pltpu.CompilerParams(vmem_limit_bytes=4 << 20),
        name="load",
    )(weight)


def experts(own, weights):
    gate, up, down = weights
    low, high = shift(own, True, 1), shift(own, True, -1)
    own_low, own_high = shift(own, False, 1), shift(own, False, -1)
    low, high, gate = tie(low, high, load(gate))
    across, low_high = shift(low, True, 1), shift(low, False, -1)
    own_low, own_high, low, high, up = tie(own_low, own_high, low, high, load(up))
    low_low, high_high = shift(low, False, 1), shift(high, False, -1)
    across, low_high, own_high, high, down = tie(across, low_high, own_high, high, load(down))
    weights = gate, up, down
    high_low, own_far = shift(high, False, 1), shift(own_high, False, -1)
    low_low, high_high = tie(low_low, high_high)
    low_far, high_far = shift(low_low, False, 1), shift(high_high, False, -1)
    high_low, own_far, across = tie(high_low, own_far, across)
    across_low, across_high = shift(across, False, 1), shift(across, False, -1)
    own_parts = ffn((own, own_low, own_high, own_far), *weights)
    low_far, high_far, *own_parts = tie(low_far, high_far, *own_parts)
    own_passed, own_behind = shift(own_parts[3], False, -1), shift(own_parts[2], False, 1)
    low_parts = ffn((low, low_low, low_high, low_far), *weights)
    across_low, across_high, *low_parts = tie(across_low, across_high, *low_parts)
    across_far = shift(across_low, False, 1)
    low_passed = shift(low_parts[3], False, -1)
    high_parts = ffn((high, high_low, high_high, high_far), *weights)
    high_passed = shift(high_parts[3], False, 1)
    own_passed, own_behind, across_far = tie(own_passed, own_behind, across_far)
    own_ahead = shift(add(own_parts[1], own_passed), False, -1)
    across_parts = ffn((across, across_low, across_high, across_far), *weights)
    high_behind = shift(high_parts[1], False, -1)
    low_passed, high_passed, high_behind, *across_parts = tie(
        low_passed, high_passed, high_behind, *across_parts
    )
    across_passed, across_behind = (
        shift(across_parts[3], False, 1),
        shift(across_parts[1], False, -1),
    )
    low_behind = shift(low_parts[2], False, 1)
    across_passed, own_ahead = tie(across_passed, own_ahead)
    low_ahead = shift(add(low_parts[1], low_passed), False, -1)
    high_ahead = shift(add(high_parts[2], high_passed), False, 1)
    across_ahead = shift(add(across_parts[2], across_passed), False, 1)
    across_sum = add(across_parts[0], across_ahead, across_behind)
    across_sum, low_ahead = tie(across_sum, low_ahead)
    own_sum = add(own_parts[0], own_ahead, own_behind)
    low_sum = add(low_parts[0], low_ahead, low_behind)
    high_sum = add(high_parts[0], high_ahead, high_behind)
    passed = shift(across_sum, True, -1)
    own_sum = add(own_sum, shift(high_sum, True, 1))
    return add(own_sum, shift(add(low_sum, passed), True, -1))


def combine_kernel(att_ref, ret_ref, ids_ref, logits_ref, out_ref):
    names = lax.broadcasted_iota(jnp.int32, (PROMPT, HEAD), 1)
    ids = [ids_ref[:, c : c + 1] for c in range(2)]
    named = (ids[0] == names) | (ids[1] == names)
    first = lax.broadcasted_iota(jnp.int32, (PROMPT, PROMPT), 0)
    second = lax.broadcasted_iota(jnp.int32, (PROMPT, PROMPT), 1)
    before = jnp.where(second < first, 1.0, 0.0).astype(jnp.bfloat16)
    taken = jnp.where(named, 1.0, 0.0).astype(jnp.bfloat16)
    count = jnp.dot(before, taken, preferred_element_type=jnp.float32)
    logits = [logits_ref[:, c : c + 1] for c in range(2)]
    top = jnp.maximum(logits[0], logits[1])
    exps = [jnp.exp(v - top) for v in logits]
    total = exps[0] + exps[1]
    ret = ret_ref[...]
    column = lax.broadcasted_iota(jnp.int32, (PROMPT, EXPERTS * CAP), 1)
    mixed = None
    for c in range(2):
        slot = jnp.sum(jnp.where(ids[c] == names, count, 0.0), axis=1, keepdims=True)
        at = ids[c] * CAP + slot.astype(jnp.int32)
        chosen = jnp.where(column == at, 1.0, 0.0).astype(jnp.bfloat16)
        picked = jnp.dot(chosen, ret, preferred_element_type=jnp.float32)
        term = exps[c] / total * picked
        mixed = term if mixed is None else mixed + term
    out_ref[...] = (att_ref[...].astype(jnp.float32) + mixed).astype(jnp.bfloat16)


def combine(att, returned, ids, logits):
    return pl.pallas_call(
        combine_kernel,
        out_shape=jax.ShapeDtypeStruct((PROMPT, WIDTH), jnp.bfloat16),
        compiler_params=pltpu.CompilerParams(vmem_limit_bytes=32 << 20),
        name="combine",
    )(att, returned, ids, logits)


def fetch_rows(records, pair_blocks):
    z, y = lax.axis_index("z"), lax.axis_index("y")
    y_first = lax.axis_index("expert") % 2 == 0
    low, high = tie(shift(records, True, 1), shift(records, True, -1))
    far0, far1 = tie(shift(low[:1], True, 1), shift(high[1:], True, -1))
    first, second = jnp.where(y_first, y, z), jnp.where(y_first, z, y)
    ahead = jnp.array([0, 0, 1, 1, -1, -1, 2, 2], jnp.int32)
    slot = jnp.array([0, 1, 0, 1, 0, 1, 0, 1], jnp.int32)
    target = (second + ahead) % SIDE
    prompt = jnp.where(y_first, target * SIDE + first, first * SIDE + target)
    wanted = pair_blocks[prompt, slot]
    owner = wanted // 2
    own_z, own_y = owner // SIDE, owner % SIDE
    own_first, own_second = jnp.where(y_first, own_y, own_z), jnp.where(y_first, own_z, own_y)
    away = (own_first - first) % SIDE
    half = wanted % 2
    source = jnp.where(away == 0, half, jnp.where(away == 3, 2 + half, jnp.where(away == 1, 4 + half, 6 + half)))
    sel = jnp.where(own_second == second, source, -1)
    here, up, down, up_far, down_far = pick_blocks(sel, (records, low, high, far0, far1))
    up_got, down_got = tie(shift(up_far, False, 1), shift(down_far, False, -1))
    up = jnp.concatenate([up[:1] + up_got, up[1:]], axis=0)
    down = jnp.concatenate([down[:1], down[1:] + down_got], axis=0)
    return here, shift(up, False, 1), shift(down, False, -1)


def body(
    records,
    pair_blocks,
    lengths,
    norm_gain,
    gate_logits,
    expert_ids,
    gate_weight,
    up_weight,
    down_weight,
):
    dp_index = lax.axis_index("z") * SIDE + lax.axis_index("y")
    limit = lax.dynamic_slice_in_dim(lengths, dp_index, 1, 0)
    parts = [part.reshape(PROMPT, QKV) for part in fetch_rows(records, pair_blocks)]
    att, outgoing = attend(limit, parts, expert_ids.T)
    arrived = lax.all_to_all(
        outgoing.reshape(EXPERTS, CAP, WIDTH), "expert", split_axis=0, concat_axis=0, tiled=True
    )
    normed = normalise(arrived, norm_gain.reshape(1, D))
    summed = experts(normed, (gate_weight, up_weight, down_weight))
    returned = lax.all_to_all(summed, "expert", split_axis=0, concat_axis=0, tiled=True)
    return combine(att, returned.reshape(EXPERTS * CAP, WIDTH), expert_ids, gate_logits)


def solution(mesh):
    fine = Mesh(mesh.devices.reshape(SIDE, SIDE, EXPERTS), ("z", "y", "expert"))
    dp = ("z", "y")
    placed = (
        P(dp, None, "expert"),
        P(),
        P(),
        P(),
        P(dp, None),
        P(dp, None),
        P("expert", None, dp),
        P("expert", None, dp),
        P("expert", dp, None),
    )
    return jax.shard_map(
        body, mesh=fine, in_specs=placed, out_specs=P(dp, "expert"), check_vma=False
    )
```

```python
import math

import jax
import jax.numpy as jnp
from jax import lax
from jax.experimental import pallas as pl
from jax.experimental.pallas import tpu as pltpu
from jax.sharding import Mesh
from jax.sharding import PartitionSpec as P

HEAD = 128
GROUP = 6
BLOCK = 128
PROMPT = 256
EXPERTS = 8
CAP = 80
WIDTH = 768
D = 6144
FF_DEV = 512
N_DP = 16
SIDE = 4
QKV = 1024


def pick_kernel(sel_ref, own, low, high, far0, far1, here, up, down, up_far, down_far):
    sources = [own.at[0], own.at[1], low.at[0], low.at[1], high.at[0], high.at[1], far0.at[0], far1.at[0]]
    targets = [here.at[0], here.at[1], up.at[0], up.at[1], down.at[0], down.at[1], up_far.at[0], down_far.at[0]]
    for i, target in enumerate(targets):
        for k, source in enumerate(sources):

            @pl.when(sel_ref[i] == k)
            def _():
                target[...] = source[...]

        @pl.when(sel_ref[i] < 0)
        def _():
            target[...] = jnp.zeros_like(target)


def pick_blocks(sel, blocks):
    vmem = pl.BlockSpec(memory_space=pltpu.VMEM)
    return pl.pallas_call(
        pick_kernel,
        in_specs=[pl.BlockSpec(memory_space=pltpu.SMEM)] + [vmem] * 5,
        out_specs=[vmem] * 5,
        out_shape=[
            jax.ShapeDtypeStruct((n, BLOCK, QKV), jnp.bfloat16) for n in (2, 2, 2, 1, 1)
        ],
        compiler_params=pltpu.CompilerParams(vmem_limit_bytes=16 << 20),
        name="pick_blocks",
    )(sel, *blocks)


def attend_kernel(len_ref, here_ref, low_ref, high_ref, ids_ref, att_ref, out_ref, rows_ref):
    limit = len_ref[0]
    rows_ref[...] = here_ref[...] + low_ref[...] + high_ref[...]
    scale = 1.0 / math.sqrt(HEAD)
    for top in (0, BLOCK):
        span = top + BLOCK
        keys = rows_ref[0:span, GROUP * HEAD : (GROUP + 1) * HEAD]
        values = rows_ref[0:span, (GROUP + 1) * HEAD : (GROUP + 2) * HEAD]
        row = lax.broadcasted_iota(jnp.int32, (BLOCK, span), 0) + top
        col = lax.broadcasted_iota(jnp.int32, (BLOCK, span), 1)
        allowed = (col <= row) & (col < limit)
        for g in range(GROUP):
            query = rows_ref[top:span, g * HEAD : (g + 1) * HEAD]
            scores = lax.dot_general(
                query, keys, (((1,), (1,)), ((), ())), preferred_element_type=jnp.float32
            )
            scores = jnp.where(allowed, scores * scale, -jnp.inf)
            exponent = jnp.exp(scores - jnp.max(scores, axis=1, keepdims=True))
            probs = (exponent / jnp.sum(exponent, axis=1, keepdims=True)).astype(jnp.bfloat16)
            mixed = jnp.dot(probs, values, preferred_element_type=jnp.float32)
            att_ref[top:span, g * HEAD : (g + 1) * HEAD] = mixed.astype(jnp.bfloat16)
    names = lax.broadcasted_iota(jnp.int32, (EXPERTS, PROMPT), 0)
    named = (ids_ref[0:1, :] == names) | (ids_ref[1:2, :] == names)
    first = lax.broadcasted_iota(jnp.int32, (PROMPT, PROMPT), 0)
    second = lax.broadcasted_iota(jnp.int32, (PROMPT, PROMPT), 1)
    before = jnp.where(first < second, 1.0, 0.0).astype(jnp.bfloat16)
    taken = jnp.where(named, 1.0, 0.0)
    slot = jnp.dot(taken.astype(jnp.bfloat16), before, preferred_element_type=jnp.float32)
    slot = jnp.where(named, slot, -1.0).astype(jnp.int32)
    att = att_ref[...]
    place = lax.broadcasted_iota(jnp.int32, (CAP, PROMPT), 0)
    for e in range(EXPERTS):
        chosen = jnp.where(place == slot[e : e + 1, :], 1.0, 0.0).astype(jnp.bfloat16)
        sent = jnp.dot(chosen, att, preferred_element_type=jnp.float32)
        out_ref[e * CAP : (e + 1) * CAP, :] = sent.astype(jnp.bfloat16)


def attend(limit, parts, ids_t):
    vmem = pl.BlockSpec(memory_space=pltpu.VMEM)
    return pl.pallas_call(
        attend_kernel,
        in_specs=[pl.BlockSpec(memory_space=pltpu.SMEM)] + [vmem] * 4,
        out_specs=[vmem, vmem],
        out_shape=[
            jax.ShapeDtypeStruct((PROMPT, WIDTH), jnp.bfloat16),
            jax.ShapeDtypeStruct((EXPERTS * CAP, WIDTH), jnp.bfloat16),
        ],
        scratch_shapes=[pltpu.VMEM((PROMPT, QKV), jnp.bfloat16)],
        compiler_params=pltpu.CompilerParams(vmem_limit_bytes=16 << 20),
        name="attend",
    )(limit, *parts, ids_t)


def norm_kernel(x_ref, gain_ref, out_ref):
    total = jnp.zeros((CAP, 1), jnp.float32)
    for i in range(EXPERTS):
        part = x_ref[i].astype(jnp.float32)
        total = total + jnp.sum(part * part, axis=1, keepdims=True)
    factor = lax.rsqrt(total * (1.0 / D) + 1e-05)
    for i in range(EXPERTS):
        cols = slice(i * WIDTH, (i + 1) * WIDTH)
        out_ref[:, cols] = (x_ref[i].astype(jnp.float32) * factor * gain_ref[:, cols]).astype(
            jnp.bfloat16
        )


def normalise(arrived, gain):
    return pl.pallas_call(
        norm_kernel,
        out_shape=jax.ShapeDtypeStruct((CAP, D), jnp.bfloat16),
        compiler_params=pltpu.CompilerParams(vmem_limit_bytes=32 << 20),
        name="normalise",
    )(arrived, gain)


def ffn_kernel(x0, x1, x2, x3, gate_ref, up_ref, down_ref, o0, o1, o2, o3, xs):
    for j, x in enumerate((x0, x1, x2, x3)):
        xs[j * CAP : (j + 1) * CAP, :] = x[...]
    gate = jnp.dot(xs[...], gate_ref[0], preferred_element_type=jnp.float32)
    up = jnp.dot(xs[...], up_ref[0], preferred_element_type=jnp.float32)
    hidden = (gate / (1.0 + jnp.exp(-gate)) * up).astype(jnp.bfloat16)
    for i in range(EXPERTS):
        part = jnp.dot(
            hidden, down_ref[0, :, i * WIDTH : (i + 1) * WIDTH], preferred_element_type=jnp.float32
        ).astype(jnp.bfloat16)
        for j, o in enumerate((o0, o1, o2, o3)):
            o[i] = part[j * CAP : (j + 1) * CAP]


def ffn(shards, gate, up, down):
    vmem = pl.BlockSpec(memory_space=pltpu.VMEM)
    return pl.pallas_call(
        ffn_kernel,
        in_specs=[vmem] * 7,
        out_specs=[vmem] * SIDE,
        out_shape=[jax.ShapeDtypeStruct((EXPERTS, CAP, WIDTH), jnp.bfloat16)] * SIDE,
        scratch_shapes=[pltpu.VMEM((SIDE * CAP, D), jnp.bfloat16)],
        compiler_params=pltpu.CompilerParams(vmem_limit_bytes=12 << 20),
        cost_estimate=pl.CostEstimate(
            flops=6 * SIDE * CAP * D * FF_DEV,
            transcendentals=SIDE * CAP * FF_DEV,
            bytes_accessed=4 * SIDE * CAP * D,
        ),
        name="ffn",
    )(*shards, gate, up, down)


def shift(value, first, step):
    pairs = []
    for z in range(SIDE):
        for y in range(SIDE):
            for e in range(EXPERTS):
                along_y = (e % 2 == 0) == first
                to_z, to_y = (z, (y + step) % SIDE) if along_y else ((z + step) % SIDE, y)
                pairs.append(((z * SIDE + y) * EXPERTS + e, (to_z * SIDE + to_y) * EXPERTS + e))
    return lax.ppermute(value, ("z", "y", "expert"), pairs)


def tie(*values):
    return lax.optimization_barrier(values)


def add_kernel(*refs):
    *parts, out_ref = refs
    total = parts[0][...].astype(jnp.float32)
    for part in parts[1:]:
        total = total + part[...].astype(jnp.float32)
    out_ref[...] = total.astype(jnp.bfloat16)


def add(*parts):
    shape = parts[0].shape
    block = pl.BlockSpec(memory_space=pltpu.VMEM)
    return pl.pallas_call(
        add_kernel,
        in_specs=[block] * len(parts),
        out_specs=block,
        out_shape=jax.ShapeDtypeStruct(shape, jnp.bfloat16),
        compiler_params=pltpu.CompilerParams(vmem_limit_bytes=4 << 20),
        name="add",
    )(*parts)


def load_kernel(source, target, sem):
    copy = pltpu.make_async_copy(source, target, sem)
    copy.start()
    copy.wait()


def load(weight):
    return pl.pallas_call(
        load_kernel,
        in_specs=[pl.BlockSpec(memory_space=pltpu.HBM)],
        out_specs=pl.BlockSpec(memory_space=pltpu.VMEM),
        out_shape=jax.ShapeDtypeStruct(weight.shape, weight.dtype),
        scratch_shapes=[pltpu.SemaphoreType.DMA],
        compiler_params=pltpu.CompilerParams(vmem_limit_bytes=4 << 20),
        name="load",
    )(weight)


def experts(own, weights):
    gate, up, down = weights
    low, high = shift(own, True, 1), shift(own, True, -1)
    own_low, own_high = shift(own, False, 1), shift(own, False, -1)
    low, high, gate = tie(low, high, load(gate))
    across, low_high = shift(low, True, 1), shift(low, False, -1)
    own_low, own_high, low, high, up = tie(own_low, own_high, low, high, load(up))
    low_low, high_high = shift(low, False, 1), shift(high, False, -1)
    across, low_high, own_high, high, down = tie(across, low_high, own_high, high, load(down))
    weights = gate, up, down
    high_low, own_far = shift(high, False, 1), shift(own_high, False, -1)
    low_low, high_high = tie(low_low, high_high)
    low_far, high_far = shift(low_low, False, 1), shift(high_high, False, -1)
    high_low, own_far, across = tie(high_low, own_far, across)
    across_low, across_high = shift(across, False, 1), shift(across, False, -1)
    own_parts = ffn((own, own_low, own_high, own_far), *weights)
    low_far, high_far, *own_parts = tie(low_far, high_far, *own_parts)
    own_passed, own_behind = shift(own_parts[3], False, -1), shift(own_parts[2], False, 1)
    low_parts = ffn((low, low_low, low_high, low_far), *weights)
    across_low, across_high, *low_parts = tie(across_low, across_high, *low_parts)
    across_far = shift(across_low, False, 1)
    low_passed = shift(low_parts[3], False, -1)
    high_parts = ffn((high, high_low, high_high, high_far), *weights)
    high_passed = shift(high_parts[3], False, 1)
    own_passed, own_behind, across_far = tie(own_passed, own_behind, across_far)
    own_ahead = shift(add(own_parts[1], own_passed), False, -1)
    across_parts = ffn((across, across_low, across_high, across_far), *weights)
    high_behind = shift(high_parts[1], False, -1)
    low_passed, high_passed, high_behind, *across_parts = tie(
        low_passed, high_passed, high_behind, *across_parts
    )
    across_passed, across_behind = (
        shift(across_parts[3], False, 1),
        shift(across_parts[1], False, -1),
    )
    across_passed, own_ahead = tie(across_passed, own_ahead)
    low_ahead = shift(add(low_parts[1], low_passed), False, -1)
    high_ahead = shift(add(high_parts[2], high_passed), False, 1)
    across_ahead = shift(add(across_parts[2], across_passed), False, 1)
    across_sum = add(across_parts[0], across_ahead, across_behind)
    across_sum, to_high = tie(across_sum, low_parts[2])
    low_behind = shift(to_high, False, 1)
    own_sum = add(own_parts[0], own_ahead, own_behind)
    low_sum = add(low_parts[0], low_ahead, low_behind)
    high_sum = add(high_parts[0], high_ahead, high_behind)
    passed = shift(across_sum, True, -1)
    own_sum = add(own_sum, shift(high_sum, True, 1))
    return add(own_sum, shift(add(low_sum, passed), True, -1))


def combine_kernel(att_ref, ret_ref, ids_ref, logits_ref, out_ref):
    names = lax.broadcasted_iota(jnp.int32, (PROMPT, HEAD), 1)
    ids = [ids_ref[:, c : c + 1] for c in range(2)]
    named = (ids[0] == names) | (ids[1] == names)
    first = lax.broadcasted_iota(jnp.int32, (PROMPT, PROMPT), 0)
    second = lax.broadcasted_iota(jnp.int32, (PROMPT, PROMPT), 1)
    before = jnp.where(second < first, 1.0, 0.0).astype(jnp.bfloat16)
    taken = jnp.where(named, 1.0, 0.0).astype(jnp.bfloat16)
    count = jnp.dot(before, taken, preferred_element_type=jnp.float32)
    logits = [logits_ref[:, c : c + 1] for c in range(2)]
    top = jnp.maximum(logits[0], logits[1])
    exps = [jnp.exp(v - top) for v in logits]
    total = exps[0] + exps[1]
    ret = ret_ref[...]
    column = lax.broadcasted_iota(jnp.int32, (PROMPT, EXPERTS * CAP), 1)
    mixed = None
    for c in range(2):
        slot = jnp.sum(jnp.where(ids[c] == names, count, 0.0), axis=1, keepdims=True)
        at = ids[c] * CAP + slot.astype(jnp.int32)
        chosen = jnp.where(column == at, 1.0, 0.0).astype(jnp.bfloat16)
        picked = jnp.dot(chosen, ret, preferred_element_type=jnp.float32)
        term = exps[c] / total * picked
        mixed = term if mixed is None else mixed + term
    out_ref[...] = (att_ref[...].astype(jnp.float32) + mixed).astype(jnp.bfloat16)


def combine(att, returned, ids, logits):
    return pl.pallas_call(
        combine_kernel,
        out_shape=jax.ShapeDtypeStruct((PROMPT, WIDTH), jnp.bfloat16),
        compiler_params=pltpu.CompilerParams(vmem_limit_bytes=32 << 20),
        name="combine",
    )(att, returned, ids, logits)


def fetch_rows(records, pair_blocks):
    z, y = lax.axis_index("z"), lax.axis_index("y")
    y_first = lax.axis_index("expert") % 2 == 0
    low, high = tie(shift(records, True, 1), shift(records, True, -1))
    far0, far1 = tie(shift(low[:1], True, 1), shift(high[1:], True, -1))
    first, second = jnp.where(y_first, y, z), jnp.where(y_first, z, y)
    ahead = jnp.array([0, 0, 1, 1, -1, -1, 2, 2], jnp.int32)
    slot = jnp.array([0, 1, 0, 1, 0, 1, 0, 1], jnp.int32)
    target = (second + ahead) % SIDE
    prompt = jnp.where(y_first, target * SIDE + first, first * SIDE + target)
    wanted = pair_blocks[prompt, slot]
    owner = wanted // 2
    own_z, own_y = owner // SIDE, owner % SIDE
    own_first, own_second = jnp.where(y_first, own_y, own_z), jnp.where(y_first, own_z, own_y)
    away = (own_first - first) % SIDE
    half = wanted % 2
    source = jnp.where(away == 0, half, jnp.where(away == 3, 2 + half, jnp.where(away == 1, 4 + half, 6 + half)))
    sel = jnp.where(own_second == second, source, -1)
    here, up, down, up_far, down_far = pick_blocks(sel, (records, low, high, far0, far1))
    up_got, down_got = tie(shift(up_far, False, 1), shift(down_far, False, -1))
    up = jnp.concatenate([up[:1] + up_got, up[1:]], axis=0)
    down = jnp.concatenate([down[:1], down[1:] + down_got], axis=0)
    return here, shift(up, False, 1), shift(down, False, -1)


def body(
    records,
    pair_blocks,
    lengths,
    norm_gain,
    gate_logits,
    expert_ids,
    gate_weight,
    up_weight,
    down_weight,
):
    dp_index = lax.axis_index("z") * SIDE + lax.axis_index("y")
    limit = lax.dynamic_slice_in_dim(lengths, dp_index, 1, 0)
    parts = [part.reshape(PROMPT, QKV) for part in fetch_rows(records, pair_blocks)]
    att, outgoing = attend(limit, parts, expert_ids.T)
    arrived = lax.all_to_all(
        outgoing.reshape(EXPERTS, CAP, WIDTH), "expert", split_axis=0, concat_axis=0, tiled=True
    )
    normed = normalise(arrived, norm_gain.reshape(1, D))
    summed = experts(normed, (gate_weight, up_weight, down_weight))
    returned = lax.all_to_all(summed, "expert", split_axis=0, concat_axis=0, tiled=True)
    return combine(att, returned.reshape(EXPERTS * CAP, WIDTH), expert_ids, gate_logits)


def solution(mesh):
    fine = Mesh(mesh.devices.reshape(SIDE, SIDE, EXPERTS), ("z", "y", "expert"))
    dp = ("z", "y")
    placed = (
        P(dp, None, "expert"),
        P(),
        P(),
        P(),
        P(dp, None),
        P(dp, None),
        P("expert", None, dp),
        P("expert", None, dp),
        P("expert", dp, None),
    )
    return jax.shard_map(
        body, mesh=fine, in_specs=placed, out_specs=P(dp, "expert"), check_vma=False
    )
```

```python
import math

import jax
import jax.numpy as jnp
from jax import lax
from jax.experimental import pallas as pl
from jax.experimental.pallas import tpu as pltpu
from jax.sharding import Mesh
from jax.sharding import PartitionSpec as P

HEAD = 128
GROUP = 6
BLOCK = 128
PROMPT = 256
EXPERTS = 8
CAP = 80
WIDTH = 768
D = 6144
FF_DEV = 512
N_DP = 16
SIDE = 4
QKV = 1024


def pick_kernel(sel_ref, own, low, high, far0, far1, here, up, down, up_far, down_far):
    sources = [own.at[0], own.at[1], low.at[0], low.at[1], high.at[0], high.at[1], far0.at[0], far1.at[0]]
    targets = [here.at[0], here.at[1], up.at[0], up.at[1], down.at[0], down.at[1], up_far.at[0], down_far.at[0]]
    for i, target in enumerate(targets):
        for k, source in enumerate(sources):

            @pl.when(sel_ref[i] == k)
            def _():
                target[...] = source[...]

        @pl.when(sel_ref[i] < 0)
        def _():
            target[...] = jnp.zeros_like(target)


def pick_blocks(sel, blocks):
    vmem = pl.BlockSpec(memory_space=pltpu.VMEM)
    return pl.pallas_call(
        pick_kernel,
        in_specs=[pl.BlockSpec(memory_space=pltpu.SMEM)] + [vmem] * 5,
        out_specs=[vmem] * 5,
        out_shape=[
            jax.ShapeDtypeStruct((n, BLOCK, QKV), jnp.bfloat16) for n in (2, 2, 2, 1, 1)
        ],
        compiler_params=pltpu.CompilerParams(vmem_limit_bytes=16 << 20),
        name="pick_blocks",
    )(sel, *blocks)


def attend_kernel(len_ref, here_ref, low_ref, high_ref, ids_ref, att_ref, out_ref, rows_ref):
    limit = len_ref[0]
    rows_ref[...] = here_ref[...] + low_ref[...] + high_ref[...]
    scale = 1.0 / math.sqrt(HEAD)
    for top in (0, BLOCK):
        span = top + BLOCK
        keys = rows_ref[0:span, GROUP * HEAD : (GROUP + 1) * HEAD]
        values = rows_ref[0:span, (GROUP + 1) * HEAD : (GROUP + 2) * HEAD]
        row = lax.broadcasted_iota(jnp.int32, (BLOCK, span), 0) + top
        col = lax.broadcasted_iota(jnp.int32, (BLOCK, span), 1)
        allowed = (col <= row) & (col < limit)
        for g in range(GROUP):
            query = rows_ref[top:span, g * HEAD : (g + 1) * HEAD]
            scores = lax.dot_general(
                query, keys, (((1,), (1,)), ((), ())), preferred_element_type=jnp.float32
            )
            scores = jnp.where(allowed, scores * scale, -jnp.inf)
            exponent = jnp.exp(scores - jnp.max(scores, axis=1, keepdims=True))
            probs = (exponent / jnp.sum(exponent, axis=1, keepdims=True)).astype(jnp.bfloat16)
            mixed = jnp.dot(probs, values, preferred_element_type=jnp.float32)
            att_ref[top:span, g * HEAD : (g + 1) * HEAD] = mixed.astype(jnp.bfloat16)
    names = lax.broadcasted_iota(jnp.int32, (EXPERTS, PROMPT), 0)
    named = (ids_ref[0:1, :] == names) | (ids_ref[1:2, :] == names)
    first = lax.broadcasted_iota(jnp.int32, (PROMPT, PROMPT), 0)
    second = lax.broadcasted_iota(jnp.int32, (PROMPT, PROMPT), 1)
    before = jnp.where(first < second, 1.0, 0.0).astype(jnp.bfloat16)
    taken = jnp.where(named, 1.0, 0.0)
    slot = jnp.dot(taken.astype(jnp.bfloat16), before, preferred_element_type=jnp.float32)
    slot = jnp.where(named, slot, -1.0).astype(jnp.int32)
    att = att_ref[...]
    place = lax.broadcasted_iota(jnp.int32, (CAP, PROMPT), 0)
    for e in range(EXPERTS):
        chosen = jnp.where(place == slot[e : e + 1, :], 1.0, 0.0).astype(jnp.bfloat16)
        sent = jnp.dot(chosen, att, preferred_element_type=jnp.float32)
        out_ref[e * CAP : (e + 1) * CAP, :] = sent.astype(jnp.bfloat16)


def attend(limit, parts, ids_t):
    vmem = pl.BlockSpec(memory_space=pltpu.VMEM)
    return pl.pallas_call(
        attend_kernel,
        in_specs=[pl.BlockSpec(memory_space=pltpu.SMEM)] + [vmem] * 4,
        out_specs=[vmem, vmem],
        out_shape=[
            jax.ShapeDtypeStruct((PROMPT, WIDTH), jnp.bfloat16),
            jax.ShapeDtypeStruct((EXPERTS * CAP, WIDTH), jnp.bfloat16),
        ],
        scratch_shapes=[pltpu.VMEM((PROMPT, QKV), jnp.bfloat16)],
        compiler_params=pltpu.CompilerParams(vmem_limit_bytes=16 << 20),
        name="attend",
    )(limit, *parts, ids_t)


def norm_kernel(x_ref, gain_ref, out_ref):
    total = jnp.zeros((CAP, 1), jnp.float32)
    for i in range(EXPERTS):
        part = x_ref[i].astype(jnp.float32)
        total = total + jnp.sum(part * part, axis=1, keepdims=True)
    factor = lax.rsqrt(total * (1.0 / D) + 1e-05)
    for i in range(EXPERTS):
        cols = slice(i * WIDTH, (i + 1) * WIDTH)
        out_ref[:, cols] = (x_ref[i].astype(jnp.float32) * factor * gain_ref[:, cols]).astype(
            jnp.bfloat16
        )


def normalise(arrived, gain):
    return pl.pallas_call(
        norm_kernel,
        out_shape=jax.ShapeDtypeStruct((CAP, D), jnp.bfloat16),
        compiler_params=pltpu.CompilerParams(vmem_limit_bytes=32 << 20),
        name="normalise",
    )(arrived, gain)


def ffn_kernel(x0, x1, x2, x3, gate_ref, up_ref, down_ref, o0, o1, o2, o3, xs):
    for j, x in enumerate((x0, x1, x2, x3)):
        xs[j * CAP : (j + 1) * CAP, :] = x[...]
    gate = jnp.dot(xs[...], gate_ref[0], preferred_element_type=jnp.float32)
    up = jnp.dot(xs[...], up_ref[0], preferred_element_type=jnp.float32)
    hidden = (gate / (1.0 + jnp.exp(-gate)) * up).astype(jnp.bfloat16)
    for i in range(EXPERTS):
        part = jnp.dot(
            hidden, down_ref[0, :, i * WIDTH : (i + 1) * WIDTH], preferred_element_type=jnp.float32
        ).astype(jnp.bfloat16)
        for j, o in enumerate((o0, o1, o2, o3)):
            o[i] = part[j * CAP : (j + 1) * CAP]


def ffn(shards, gate, up, down):
    vmem = pl.BlockSpec(memory_space=pltpu.VMEM)
    return pl.pallas_call(
        ffn_kernel,
        in_specs=[vmem] * 7,
        out_specs=[vmem] * SIDE,
        out_shape=[jax.ShapeDtypeStruct((EXPERTS, CAP, WIDTH), jnp.bfloat16)] * SIDE,
        scratch_shapes=[pltpu.VMEM((SIDE * CAP, D), jnp.bfloat16)],
        compiler_params=pltpu.CompilerParams(vmem_limit_bytes=12 << 20),
        cost_estimate=pl.CostEstimate(
            flops=6 * SIDE * CAP * D * FF_DEV,
            transcendentals=SIDE * CAP * FF_DEV,
            bytes_accessed=4 * SIDE * CAP * D,
        ),
        name="ffn",
    )(*shards, gate, up, down)


def shift(value, first, step):
    pairs = []
    for z in range(SIDE):
        for y in range(SIDE):
            for e in range(EXPERTS):
                along_y = (e % 2 == 0) == first
                to_z, to_y = (z, (y + step) % SIDE) if along_y else ((z + step) % SIDE, y)
                pairs.append(((z * SIDE + y) * EXPERTS + e, (to_z * SIDE + to_y) * EXPERTS + e))
    return lax.ppermute(value, ("z", "y", "expert"), pairs)


def tie(*values):
    return lax.optimization_barrier(values)


def add_kernel(*refs):
    *parts, out_ref = refs
    total = parts[0][...].astype(jnp.float32)
    for part in parts[1:]:
        total = total + part[...].astype(jnp.float32)
    out_ref[...] = total.astype(jnp.bfloat16)


def add(*parts):
    shape = parts[0].shape
    block = pl.BlockSpec(memory_space=pltpu.VMEM)
    return pl.pallas_call(
        add_kernel,
        in_specs=[block] * len(parts),
        out_specs=block,
        out_shape=jax.ShapeDtypeStruct(shape, jnp.bfloat16),
        compiler_params=pltpu.CompilerParams(vmem_limit_bytes=4 << 20),
        name="add",
    )(*parts)


def load_kernel(source, target, sem):
    copy = pltpu.make_async_copy(source, target, sem)
    copy.start()
    copy.wait()


def load(weight):
    return pl.pallas_call(
        load_kernel,
        in_specs=[pl.BlockSpec(memory_space=pltpu.HBM)],
        out_specs=pl.BlockSpec(memory_space=pltpu.VMEM),
        out_shape=jax.ShapeDtypeStruct(weight.shape, weight.dtype),
        scratch_shapes=[pltpu.SemaphoreType.DMA],
        compiler_params=pltpu.CompilerParams(vmem_limit_bytes=4 << 20),
        name="load",
    )(weight)


def experts(own, weights):
    gate, up, down = weights
    low, high = shift(own, True, 1), shift(own, True, -1)
    own_low, own_high = shift(own, False, 1), shift(own, False, -1)
    low, high, gate = tie(low, high, load(gate))
    across, low_high = shift(low, True, 1), shift(low, False, -1)
    own_low, own_high, low, high, up = tie(own_low, own_high, low, high, load(up))
    low_low, high_high = shift(low, False, 1), shift(high, False, -1)
    across, low_high, own_high, high, down = tie(across, low_high, own_high, high, load(down))
    weights = gate, up, down
    high_low, own_far = shift(high, False, 1), shift(own_high, False, -1)
    low_low, high_high = tie(low_low, high_high)
    low_far, high_far = shift(low_low, False, 1), shift(high_high, False, -1)
    high_low, own_far, across = tie(high_low, own_far, across)
    across_low, across_high = shift(across, False, 1), shift(across, False, -1)
    own_parts = ffn((own, own_low, own_high, own_far), *weights)
    low_far, high_far, *own_parts = tie(low_far, high_far, *own_parts)
    own_passed, own_behind = shift(own_parts[3], False, -1), shift(own_parts[2], False, 1)
    low_parts = ffn((low, low_low, low_high, low_far), *weights)
    across_low, across_high, *low_parts = tie(across_low, across_high, *low_parts)
    across_far = shift(across_low, False, 1)
    low_passed = shift(low_parts[3], False, -1)
    high_parts = ffn((high, high_low, high_high, high_far), *weights)
    high_passed = shift(high_parts[3], False, 1)
    own_passed, own_behind, across_far = tie(own_passed, own_behind, across_far)
    own_ahead = shift(add(own_parts[1], own_passed), False, -1)
    across_parts = ffn((across, across_low, across_high, across_far), *weights)
    low_passed, high_passed, *across_parts = tie(low_passed, high_passed, *across_parts)
    across_passed, across_behind = (
        shift(across_parts[3], False, 1),
        shift(across_parts[1], False, -1),
    )
    low_behind, high_behind = shift(low_parts[2], False, 1), shift(high_parts[1], False, -1)
    across_passed, own_ahead = tie(across_passed, own_ahead)
    low_ahead = shift(add(low_parts[1], low_passed), False, -1)
    high_ahead = shift(add(high_parts[2], high_passed), False, 1)
    across_ahead = shift(add(across_parts[2], across_passed), False, 1)
    own_sum = add(own_parts[0], own_ahead, own_behind)
    low_sum = add(low_parts[0], low_ahead, low_behind)
    high_sum = add(high_parts[0], high_ahead, high_behind)
    across_sum = add(across_parts[0], across_ahead, across_behind)
    passed = shift(across_sum, True, -1)
    own_sum = add(own_sum, shift(high_sum, True, 1))
    return add(own_sum, shift(add(low_sum, passed), True, -1))


def combine_kernel(att_ref, ret_ref, ids_ref, logits_ref, out_ref):
    names = lax.broadcasted_iota(jnp.int32, (PROMPT, HEAD), 1)
    ids = [ids_ref[:, c : c + 1] for c in range(2)]
    named = (ids[0] == names) | (ids[1] == names)
    first = lax.broadcasted_iota(jnp.int32, (PROMPT, PROMPT), 0)
    second = lax.broadcasted_iota(jnp.int32, (PROMPT, PROMPT), 1)
    before = jnp.where(second < first, 1.0, 0.0).astype(jnp.bfloat16)
    taken = jnp.where(named, 1.0, 0.0).astype(jnp.bfloat16)
    count = jnp.dot(before, taken, preferred_element_type=jnp.float32)
    logits = [logits_ref[:, c : c + 1] for c in range(2)]
    top = jnp.maximum(logits[0], logits[1])
    exps = [jnp.exp(v - top) for v in logits]
    total = exps[0] + exps[1]
    ret = ret_ref[...]
    column = lax.broadcasted_iota(jnp.int32, (PROMPT, EXPERTS * CAP), 1)
    mixed = None
    for c in range(2):
        slot = jnp.sum(jnp.where(ids[c] == names, count, 0.0), axis=1, keepdims=True)
        at = ids[c] * CAP + slot.astype(jnp.int32)
        chosen = jnp.where(column == at, 1.0, 0.0).astype(jnp.bfloat16)
        picked = jnp.dot(chosen, ret, preferred_element_type=jnp.float32)
        term = exps[c] / total * picked
        mixed = term if mixed is None else mixed + term
    out_ref[...] = (att_ref[...].astype(jnp.float32) + mixed).astype(jnp.bfloat16)


def combine(att, returned, ids, logits):
    return pl.pallas_call(
        combine_kernel,
        out_shape=jax.ShapeDtypeStruct((PROMPT, WIDTH), jnp.bfloat16),
        compiler_params=pltpu.CompilerParams(vmem_limit_bytes=32 << 20),
        name="combine",
    )(att, returned, ids, logits)


def merge_kernel(up_ref, up_got, down_ref, down_got, up_out, down_out):
    up_out[0] = up_ref[0] + up_got[0]
    up_out[1] = up_ref[1]
    down_out[0] = down_ref[0]
    down_out[1] = down_ref[1] + down_got[0]


def merge(up, up_got, down, down_got):
    vmem = pl.BlockSpec(memory_space=pltpu.VMEM)
    return pl.pallas_call(
        merge_kernel,
        in_specs=[vmem] * 4,
        out_specs=[vmem] * 2,
        out_shape=[jax.ShapeDtypeStruct(up.shape, up.dtype)] * 2,
        compiler_params=pltpu.CompilerParams(vmem_limit_bytes=4 << 20),
        name="merge",
    )(up, up_got, down, down_got)


def fetch_rows(records, pair_blocks):
    z, y = lax.axis_index("z"), lax.axis_index("y")
    y_first = lax.axis_index("expert") % 2 == 0
    low, high = tie(shift(records, True, 1), shift(records, True, -1))
    far0, far1 = tie(shift(low[:1], True, 1), shift(high[1:], True, -1))
    first, second = jnp.where(y_first, y, z), jnp.where(y_first, z, y)
    ahead = jnp.array([0, 0, 1, 1, -1, -1, 2, 2], jnp.int32)
    slot = jnp.array([0, 1, 0, 1, 0, 1, 0, 1], jnp.int32)
    target = (second + ahead) % SIDE
    prompt = jnp.where(y_first, target * SIDE + first, first * SIDE + target)
    wanted = pair_blocks[prompt, slot]
    owner = wanted // 2
    own_z, own_y = owner // SIDE, owner % SIDE
    own_first, own_second = jnp.where(y_first, own_y, own_z), jnp.where(y_first, own_z, own_y)
    away = (own_first - first) % SIDE
    half = wanted % 2
    source = jnp.where(away == 0, half, jnp.where(away == 3, 2 + half, jnp.where(away == 1, 4 + half, 6 + half)))
    sel = jnp.where(own_second == second, source, -1)
    here, up, down, up_far, down_far = pick_blocks(sel, (records, low, high, far0, far1))
    up_got, down_got = tie(shift(up_far, False, 1), shift(down_far, False, -1))
    up, down = merge(up, up_got, down, down_got)
    return here, shift(up, False, 1), shift(down, False, -1)


def body(
    records,
    pair_blocks,
    lengths,
    norm_gain,
    gate_logits,
    expert_ids,
    gate_weight,
    up_weight,
    down_weight,
):
    dp_index = lax.axis_index("z") * SIDE + lax.axis_index("y")
    limit = lax.dynamic_slice_in_dim(lengths, dp_index, 1, 0)
    parts = [part.reshape(PROMPT, QKV) for part in fetch_rows(records, pair_blocks)]
    att, outgoing = attend(limit, parts, expert_ids.T)
    arrived = lax.all_to_all(
        outgoing.reshape(EXPERTS, CAP, WIDTH), "expert", split_axis=0, concat_axis=0, tiled=True
    )
    normed = normalise(arrived, norm_gain.reshape(1, D))
    summed = experts(normed, (gate_weight, up_weight, down_weight))
    returned = lax.all_to_all(summed, "expert", split_axis=0, concat_axis=0, tiled=True)
    return combine(att, returned.reshape(EXPERTS * CAP, WIDTH), expert_ids, gate_logits)


def solution(mesh):
    fine = Mesh(mesh.devices.reshape(SIDE, SIDE, EXPERTS), ("z", "y", "expert"))
    dp = ("z", "y")
    placed = (
        P(dp, None, "expert"),
        P(),
        P(),
        P(),
        P(dp, None),
        P(dp, None),
        P("expert", None, dp),
        P("expert", None, dp),
        P("expert", dp, None),
    )
    return jax.shard_map(
        body, mesh=fine, in_specs=placed, out_specs=P(dp, "expert"), check_vma=False
    )
```
